128 devices in a mesh: dom: 32 (over y, x, core), rep: 4 (over z).
Axes of the slice: x: 4, y: 4, z: 4, core: 2. Of those that a mesh axis runs over, the one named last changes fastest.
Arguments:
- features: bfloat16 [131072, 512], P('dom', 'rep'), may hold values from -6 to 6
- tile_values: bfloat16 [1024, 8, 128, 128], P('dom'), may hold values from -0.1875 to 0.1875
- tile_columns: int32 [1024, 8], P('dom'), may hold values from 0 to 63
- boundary_rows: int32 [32, 128], P('dom'), may hold values from 0 to 4095
- train_rows: int32 [32, 4096], P('dom'), may hold values from 0 to 4095
- shuffle: int32 [32, 4096], P('dom'), may hold values from 0 to 4095, each once within a row
- labels: int32 [131072], P(('dom', 'rep')), may hold values from 0 to 152
- first_weight: bfloat16 [4, 512, 1024], replicated, may hold values from -0.125 to 0.125
- mid_weight: bfloat16 [1024, 1024], replicated, may hold values from -0.1875 to 0.1875
- out_weight: bfloat16 [1024, 153], replicated, may hold values from -0.1875 to 0.1875
Outputs:
- first_grad: float32 [4, 512, 1024], P('rep', 'dom')
- mid_grad: float32 [1024, 1024], P(('dom', 'rep'))
- out_grad: float32 [1024, 153], P(('dom', 'rep'))
The draws below stay inside these ranges and needn't reach their ends.
Inputs may be any that keep to these rules, and one draw needn't show every extreme that they name: `tile_columns`: an entry below 32 names a block of the partition's own rows, an entry c of 32 or more names block c - 32 of the gathered boundary rows. `train_rows`: indices may repeat. `shuffle`: each row is a permutation of 0 to 4095.
All inputs are finite; a program needn't handle non-finite values.
Results may differ from the reference program's by a relative error of at most 0.02.
Values may be sent and summed in bfloat16 or wider, within the bound.
No kernel may reach another device: no remote copies, remote signals or barrier semaphores. Data moves between devices by JAX's collectives and lax.ppermute only.
A program may use at most 128 MiB of HBM per device.

```python
import math
import jax
import jax.numpy as jnp
from jax import lax

F = 512
HID = 1024
C = 153
TILE = 128
K = 8
B = 128
HOPS = 3
R = 4096
TRAIN_DEV = 4096
SLAB = 128
NB = 32
NCB = 64
NODES = 131072
TRAIN = 131072
GROUP = 128
N_DOM = 32
N_REP = 4


def place_ends(entries, rng, least, top_value):
    spot = [jax.random.randint(jax.random.fold_in(rng, axis), (), 0, length) for axis, length in enumerate(entries.shape)]
    longest = entries.shape.index(max(entries.shape))
    beside = spot[:longest] + [(spot[longest] + 1) % entries.shape[longest]] + spot[longest + 1:]
    return entries.at[tuple(spot)].set(least).at[tuple(beside)].set(top_value)


def steps_of(stream_key, dims, cuts, least, top_value):
    def one(axis_at, blocks):
        heights = jax.random.uniform(jax.random.fold_in(jax.random.fold_in(stream_key, 6), axis_at), (blocks,), jnp.float32, least / len(cuts), top_value / len(cuts))
        return jnp.repeat(jnp.exp(heights), dims[axis_at] // blocks).reshape((-1,) + (1,) * (len(dims) - axis_at - 1))

    factor_of = one(*cuts[0])
    for cut in cuts[1:]:
        factor_of = factor_of * one(*cut)
    return factor_of


def centred(own_key, shape, deviation, limit, cuts=(), held_as=jnp.bfloat16):
    drawn = deviation * jax.random.normal(own_key, shape, jnp.float32)
    if cuts:
        drawn = drawn * steps_of(own_key, shape, cuts, -0.22, 0.18)
    return jnp.clip(drawn, -limit, limit).astype(held_as)


def setup_inputs(seed: int = 0) -> dict:
    streams_of = jax.random.split(jax.random.key(seed), 11)
    return {
        "features": centred(streams_of[0], (NODES, F), 1.0, 6.0, ((0, 32), (1, 4))),
        "tile_values": centred(streams_of[1], (N_DOM * NB, K, TILE, TILE), (K * TILE) ** -0.5, 0.1875, ((0, 32),)),
        "tile_columns": place_ends(jax.random.randint(streams_of[2], (N_DOM * NB, K), 0, NCB), jax.random.fold_in(streams_of[2], 1), 0, NCB - 1).astype(jnp.int32),
        "boundary_rows": place_ends(jax.random.randint(streams_of[3], (N_DOM, B), 0, R), jax.random.fold_in(streams_of[3], 1), 0, R - 1).astype(jnp.int32),
        "train_rows": place_ends(jax.random.randint(streams_of[4], (N_DOM, TRAIN_DEV), 0, R), jax.random.fold_in(streams_of[4], 1), 0, R - 1).astype(jnp.int32),
        "shuffle": jax.vmap(lambda own: jax.random.permutation(own, TRAIN_DEV))(jax.random.split(streams_of[5], N_DOM)).reshape((N_DOM, TRAIN_DEV)).astype(jnp.int32),
        "labels": place_ends(jax.random.randint(streams_of[6], (TRAIN,), 0, C), jax.random.fold_in(streams_of[6], 1), 0, C - 1).astype(jnp.int32),
        "first_weight": centred(streams_of[7], (N_REP, (HOPS + 1) * SLAB, HID), ((HOPS + 1) * F) ** -0.5, 0.125),
        "mid_weight": centred(streams_of[8], (HID, HID), HID ** -0.5, 0.1875),
        "out_weight": centred(streams_of[9], (HID, C), HID ** -0.5, 0.1875),
    }


root_two_pi = 0.7978845608028654
cubic_term = 0.044715

def gelu_pair(values):
    inner_arg = root_two_pi * (values + cubic_term * values * values * values)
    tanh_part = jnp.tanh(inner_arg)
    output = 0.5 * values * (1.0 + tanh_part)
    slope_out = 0.5 * (1.0 + tanh_part) + 0.5 * values * (1.0 - tanh_part * tanh_part) * root_two_pi * (1.0 + 3.0 * cubic_term * values * values)
    return (output, slope_out)

def outer_rows(left_side, right_side):
    return lax.dot_general(left_side, right_side, (((0,), (0,)), ((), ())), preferred_element_type=jnp.float32)

def inner_cols(left_side, right_side):
    return lax.dot_general(left_side, right_side, (((1,), (1,)), ((), ())), preferred_element_type=jnp.float32)

def reference(features, tile_values, tile_columns, boundary_rows, train_rows, shuffle, labels, first_weight, mid_weight, out_weight):
    tiles = tile_values.reshape(N_DOM, NB, K, TILE, TILE)
    columns = tile_columns.reshape(N_DOM, NB, K)
    offsets = (jnp.arange(N_DOM, dtype=jnp.int32) * R)[:, None]
    halo_index = (boundary_rows + offsets).reshape(-1)
    hop_list = [features]
    for hop_index in range(HOPS):
        current = hop_list[-1]
        halo_rows = current[halo_index]
        own_parts = current.reshape(N_DOM, R, F)

        def one_part(pieces):
            own_rows, part_tiles, part_columns = pieces
            joined = jnp.concatenate([own_rows, halo_rows], axis=0)
            blocks = joined.reshape(NCB, TILE, F)
            picked = blocks[part_columns]
            summed = jnp.einsum('bkij,bkjf->bif', part_tiles.astype(jnp.float32), picked.astype(jnp.float32))
            return summed.reshape(R, F).astype(jnp.bfloat16)
        hop_list.append(lax.map(one_part, (own_parts, tiles, columns)).reshape(NODES, F))
    local_pick = jnp.take_along_axis(train_rows, shuffle, axis=1) + offsets
    selected = local_pick.reshape(N_DOM, N_DOM, GROUP).transpose(1, 0, 2).reshape(-1)
    stacked = jnp.stack([hop[selected] for hop in hop_list], axis=1)
    inputs = stacked.reshape(TRAIN, HOPS + 1, N_REP, SLAB).transpose(0, 2, 1, 3).reshape(TRAIN, (HOPS + 1) * F)
    pre_first = jnp.dot(inputs, first_weight.reshape((HOPS + 1) * F, HID), preferred_element_type=jnp.float32)
    act_first, slope_first = gelu_pair(pre_first)
    act_first = act_first.astype(jnp.bfloat16)
    pre_mid = jnp.dot(act_first, mid_weight, preferred_element_type=jnp.float32)
    act_mid, slope_mid = gelu_pair(pre_mid)
    act_mid = act_mid.astype(jnp.bfloat16)
    logits = jnp.dot(act_mid, out_weight, preferred_element_type=jnp.float32)
    exp_logits = jnp.exp(logits)
    softmax_out = exp_logits / lax.optimization_barrier(jnp.sum(exp_logits, axis=1, keepdims=True))
    onehot = (labels[:, None] == jnp.arange(C, dtype=jnp.int32)[None, :]).astype(jnp.float32)
    grad_logits = ((softmax_out - onehot) * (1.0 / math.sqrt(TRAIN))).astype(jnp.bfloat16)
    grad_mid = (inner_cols(grad_logits, out_weight) * slope_mid).astype(jnp.bfloat16)
    grad_first = (inner_cols(grad_mid, mid_weight) * slope_first).astype(jnp.bfloat16)
    out_grad = outer_rows(act_mid, grad_logits)
    mid_grad = outer_rows(act_first, grad_mid)
    first_grad = outer_rows(inputs, grad_first).reshape(N_REP, (HOPS + 1) * SLAB, HID)
    return (first_grad, mid_grad, out_grad)
```

```python
import functools
import math

import jax
import jax.numpy as jnp
from jax import lax
from jax.experimental import pallas as pl
from jax.experimental.pallas import tpu as pltpu
from jax.sharding import Mesh, PartitionSpec as P

HOPS = 3
TILE = 128
NB = 32
K = 8
R = 4096
HID = 1024
C = 153
CP = 256
Y, X, CORE, REP = 4, 4, 2, 4
DOM = Y * X * CORE
ROWS = R // REP
N_TRAIN = DOM * R
BF = jnp.bfloat16
F32 = jnp.float32
VM = 56 * 2**20

root_two_pi = 0.7978845608028654
cubic_term = 0.044715


def gelu_pair(v):
    sq = v * v
    t = jnp.tanh(root_two_pi * (v + cubic_term * sq * v))
    half = 0.5 * (1.0 + t)
    slope = half + (0.5 * root_two_pi) * v * (1.0 - t * t) * (
        1.0 + (3.0 * cubic_term) * sq
    )
    return v * half, slope


def dot(a, b, ca, cb):
    return lax.dot_general(a, b, (((ca,), (cb,)), ((), ())), preferred_element_type=F32)


def params():
    return pltpu.CompilerParams(vmem_limit_bytes=VM)


def whole(memory_space=pltpu.VMEM):
    return pl.BlockSpec(memory_space=memory_space)


def struct(shape, dtype=BF):
    return jax.ShapeDtypeStruct(shape, dtype)


def export_kernel(pos, hop, brow, export, q0, q1, q2, q3):
    row = lax.broadcasted_iota(jnp.int32, (TILE, R), 1)
    mask = (row == brow[...]).astype(BF)
    export[...] = dot(mask, hop[...], 1, 0).astype(BF)
    for d, q in enumerate((q0, q1, q2, q3)):
        start = pl.multiple_of(lax.rem(pos[0] + d, REP) * ROWS, ROWS)
        q[...] = hop[pl.ds(start, ROWS), :]


def export_first(pos, hop, brow):
    return pl.pallas_call(
        export_kernel,
        in_specs=[whole(pltpu.SMEM), whole(), whole()],
        out_specs=[whole()] * 5,
        out_shape=[struct((TILE, TILE))] + [struct((ROWS, TILE))] * 4,
        compiler_params=params(),
        name="export_first",
        cost_estimate=pl.CostEstimate(
            flops=2 * TILE * TILE * R, bytes_accessed=4 * 2**20, transcendentals=0
        ),
    )(pos, hop, brow)


STEP = 4


def prop_kernel(last, cols, tiles, hop, near, far, brow, *rest):
    if last:
        q0, q1, q2, q3, joined, out = rest
    else:
        out, export, q0, q1, q2, q3, joined, acc = rest
    i = pl.program_id(0)

    @pl.when(i == 0)
    def _():
        joined[:R] = hop[...]
        joined[R : R + R // 2] = near[...]
        joined[R + R // 2 :] = far[...]
        if not last:
            acc[...] = jnp.zeros_like(acc)

    for s in range(STEP):
        b = i * STEP + s
        parts = []
        for k in range(K):
            at = pl.multiple_of(cols[b * K + k] * TILE, TILE)
            parts.append(joined[pl.ds(at, TILE), :])
        left = jnp.concatenate([tiles[s, k] for k in range(K)], axis=1)
        got = dot(left, jnp.concatenate(parts, axis=0), 1, 0).astype(BF)
        out[pl.ds(pl.multiple_of(b * TILE, TILE), TILE), :] = got
        if not last:
            row = lax.broadcasted_iota(jnp.int32, (TILE, TILE), 1) + b * TILE
            mask = (row == brow[...]).astype(BF)
            acc[...] += dot(mask, got, 1, 0)

    @pl.when(i == NB // STEP - 1)
    def _():
        if not last:
            export[...] = acc[...].astype(BF)
        r = cols[NB * K]
        for d, q in enumerate((q0, q1, q2, q3)):
            start = pl.multiple_of(lax.rem(r + d, REP) * ROWS, ROWS)
            q[...] = out[pl.ds(start, ROWS), :]


def propagate(last, cols, tiles, hop, near, far, brow):
    def fixed(shape):
        return pl.BlockSpec(shape, lambda i, c: (0,) * len(shape))

    outs = [] if last else [(R, TILE), (TILE, TILE)]
    outs += [(ROWS, TILE)] * 4
    scratch = [pltpu.VMEM((2 * R, TILE), BF)]
    scratch += [pltpu.VMEM((R, TILE), BF) if last else pltpu.VMEM((TILE, TILE), F32)]
    return pl.pallas_call(
        functools.partial(prop_kernel, last),
        grid_spec=pltpu.PrefetchScalarGridSpec(
            num_scalar_prefetch=1,
            grid=(NB // STEP,),
            in_specs=[
                pl.BlockSpec((STEP, K, TILE, TILE), lambda i, c: (i, 0, 0, 0)),
                fixed((R, TILE)),
                fixed((R // 2, TILE)),
                fixed((R // 2, TILE)),
                fixed((TILE, TILE)),
            ],
            out_specs=[fixed(s) for s in outs],
            scratch_shapes=scratch,
        ),
        out_shape=[struct(s) for s in outs],
        compiler_params=params(),
        name="propagate_last" if last else "propagate",
        cost_estimate=pl.CostEstimate(
            flops=2 * NB * K * TILE**3, bytes_accessed=12 * 2**20, transcendentals=0
        ),
    )(cols, tiles, hop, near, far, brow)


def count_kernel(pos, labels, shuffle, train, out):
    first = lax.broadcasted_iota(jnp.int32, (DOM, TILE), 0)
    second = lax.broadcasted_iota(jnp.int32, (TILE, TILE), 0)
    slots = jnp.zeros((DOM, TILE), F32)
    for lo in range(0, DOM, 8):
        a, b = [], []
        for e in range(lo, lo + 8):
            slot = shuffle[e : e + 1, :]
            label = labels[e : e + 1, :].astype(F32)
            a.append(jnp.where(first == slot // TILE, label, 0.0).astype(BF))
            b.append((second == lax.rem(slot, TILE)).astype(BF))
        slots += dot(jnp.concatenate(a, axis=1), jnp.concatenate(b, axis=1), 1, 1)
    slots = slots.astype(jnp.int32)
    paper = lax.broadcasted_iota(jnp.int32, (ROWS, TILE), 0) + pos[0] * ROWS
    kind = lax.broadcasted_iota(jnp.int32, (CP, TILE), 0)
    total = jnp.zeros((ROWS, CP), F32)
    for lo in range(0, DOM, 8):
        a, b = [], []
        for e in range(lo, lo + 8):
            a.append((paper == train[e : e + 1, :]).astype(BF))
            b.append((kind == slots[e : e + 1, :]).astype(BF))
        total += dot(jnp.concatenate(a, axis=1), jnp.concatenate(b, axis=1), 1, 1)
    out[...] = total


def count_labels(pos, labels, shuffle, train):
    return pl.pallas_call(
        count_kernel,
        in_specs=[whole(pltpu.SMEM), whole(), whole(), whole()],
        out_specs=whole(),
        out_shape=struct((ROWS, CP), F32),
        compiler_params=params(),
        name="count_labels",
        cost_estimate=pl.CostEstimate(
            flops=2 * ROWS * R * CP, bytes_accessed=2 * 2**20, transcendentals=0
        ),
    )(pos, labels, shuffle, train)


MLP_ROWS = 256


def mlp_kernel(pos, *refs):
    pieces, (counts, w1, w2, w3, act1, act2, gl, gm, gf) = refs[:16], refs[16:]
    r = pos[0]
    pre1 = jnp.zeros((MLP_ROWS, HID), F32)
    for d in range(REP):
        slab = lax.rem(r + REP - d, REP)
        x = jnp.concatenate([pieces[4 * d + h][...] for h in range(HOPS + 1)], axis=1)
        pre1 += dot(x, w1[slab], 1, 0)
    a1, slope1 = gelu_pair(pre1)
    a1 = a1.astype(BF)
    act1[...] = a1
    a2, slope2 = gelu_pair(dot(a1, w2[...], 1, 0))
    a2 = a2.astype(BF)
    act2[...] = a2
    logits = dot(a2, w3[...], 1, 0)
    kind = lax.broadcasted_iota(jnp.int32, (MLP_ROWS, CP), 1)
    ex = jnp.where(kind < C, jnp.exp(logits), 0.0)
    probs = ex / jnp.sum(ex, axis=1, keepdims=True)
    drawn = counts[...]
    many = jnp.sum(drawn, axis=1, keepdims=True)
    g3 = ((probs * many - drawn) * (1.0 / math.sqrt(N_TRAIN))).astype(BF)
    gl[...] = g3
    g2 = (dot(g3, w3[...], 1, 1) * slope2).astype(BF)
    gm[...] = g2
    gf[...] = (dot(g2, w2[...], 1, 1) * slope1).astype(BF)


def mlp(pos, pieces, counts, w1, w2, w3):
    def fixed(shape):
        return pl.BlockSpec(shape, lambda i, c: (0,) * len(shape))

    def rows(width):
        return pl.BlockSpec((MLP_ROWS, width), lambda i, c: (i, 0))

    widths = (HID, HID, CP, HID, HID)
    return pl.pallas_call(
        mlp_kernel,
        grid_spec=pltpu.PrefetchScalarGridSpec(
            num_scalar_prefetch=1,
            grid=(ROWS // MLP_ROWS,),
            in_specs=[rows(TILE)] * 16
            + [rows(CP), fixed(w1.shape), fixed(w2.shape), fixed(w3.shape)],
            out_specs=[rows(w) for w in widths],
        ),
        out_shape=[struct((ROWS, w)) for w in widths],
        compiler_params=params(),
        name="mlp",
        cost_estimate=pl.CostEstimate(
            flops=2 * ROWS * HID * (4 * HID + 2 * CP),
            bytes_accessed=20 * 2**20,
            transcendentals=2 * ROWS * HID,
        ),
    )(pos, *pieces, counts, w1, w2, w3)


WIDE = (HID + CP) // 2


def outer_kernel(pos, act1, act2, gl, gm, keep, send):
    own = pos[1] == 0
    width = HID // Y
    for y in range(Y):
        cut = slice(y * width, (y + 1) * width)
        mid = dot(act1[:, cut], gm[...], 0, 0)
        out = dot(act2[:, cut], gl[...], 0, 0)
        both = jnp.concatenate([mid, out], axis=1).reshape(X, CORE, REP, 8, HID + CP)
        both = jnp.concatenate([both[..., :WIDE], both[..., WIDE:]], axis=3)
        zero, one = both[:, 0], both[:, 1]
        keep[y] = jnp.where(own, zero, one).astype(BF)
        send[y] = jnp.where(own, one, zero).astype(BF)


def outer_grads(pos, act1, act2, gl, gm):
    shape = (Y, X, REP, 16, WIDE)
    return pl.pallas_call(
        outer_kernel,
        in_specs=[whole(pltpu.SMEM)] + [whole()] * 4,
        out_specs=[whole()] * 2,
        out_shape=[struct(shape)] * 2,
        compiler_params=params(),
        name="outer_grads",
        cost_estimate=pl.CostEstimate(
            flops=2 * ROWS * HID * (HID + CP), bytes_accessed=8 * 2**20, transcendentals=0
        ),
    )(pos, act1, act2, gl, gm)


def first_kernel(pos, *refs):
    pieces, (gf, keep, send) = refs[:16], refs[16:]
    own = pos[1] == 0
    for d in range(REP):
        slab = lax.rem(pos[0] + REP - d, REP)
        for y in range(0, Y, 2):
            x = jnp.concatenate([pieces[4 * d + y][...], pieces[4 * d + y + 1][...]], axis=1)
            got = dot(x, gf[...], 0, 0).reshape(2, X, CORE, 16, HID)
            zero, one = got[:, :, 0], got[:, :, 1]
            kept = jnp.where(own, zero, one).astype(BF)
            sent = jnp.where(own, one, zero).astype(BF)
            for u in range(2):
                for v in range(X):
                    keep[y + u, v, slab] = kept[u, v]
                    send[y + u, v, slab] = sent[u, v]


def first_grads(pos, pieces, gf):
    shape = (Y, X, REP, 16, HID)
    return pl.pallas_call(
        first_kernel,
        in_specs=[whole(pltpu.SMEM)] + [whole()] * 17,
        out_specs=[whole()] * 2,
        out_shape=[struct(shape)] * 2,
        compiler_params=params(),
        name="first_grads",
        cost_estimate=pl.CostEstimate(
            flops=4 * ROWS * HID * HID, bytes_accessed=10 * 2**20, transcendentals=0
        ),
    )(pos, *pieces, gf)


def join_kernel(keep_f, got_f, keep_m, got_m, out):
    out[:, :, :HID] = (keep_f[...].astype(F32) + got_f[...].astype(F32)).astype(BF)
    out[:, :, HID:] = (keep_m[...].astype(F32) + got_m[...].astype(F32)).astype(BF)


def join_cores(keep_f, got_f, keep_m, got_m):
    n = Y * X * REP
    flat = [v.reshape(n, 16, v.shape[-1]) for v in (keep_f, got_f, keep_m, got_m)]

    def spec(width):
        return pl.BlockSpec((8, 16, width), lambda i: (i, 0, 0))

    return pl.pallas_call(
        join_kernel,
        grid=(n // 8,),
        in_specs=[spec(v.shape[-1]) for v in flat],
        out_specs=spec(HID + WIDE),
        out_shape=struct((n, 16, HID + WIDE)),
        compiler_params=params(),
        name="join_cores",
    )(*flat)


def total_kernel(parts, first, mid, out):
    total = jnp.sum(parts[...].astype(F32), axis=0)
    first[0] = total[:, :HID]
    rest = jnp.concatenate([total[:8, HID:], total[8:, HID:]], axis=1)
    mid[...] = rest[:, :HID]
    out[...] = rest[:, HID : HID + C]


def total_grads(parts):
    return pl.pallas_call(
        total_kernel,
        in_specs=[whole()],
        out_specs=[whole()] * 3,
        out_shape=[struct((1, 16, HID), F32), struct((8, HID), F32), struct((8, C), F32)],
        compiler_params=params(),
        name="total_grads",
    )(parts)


def shift(value, axis, by):
    size = lax.axis_size(axis)
    return lax.ppermute(value, axis, [(i, (i + by) % size) for i in range(size)])


def spread(export):
    for axis in ("y", "x"):
        export = jnp.concatenate([export] + [shift(export, axis, d) for d in (1, 2, 3)])
    return export, shift(export, "core", 1)


def per_device(
    features,
    tile_values,
    tile_columns,
    boundary_rows,
    train_rows,
    shuffle,
    labels,
    first_weight,
    mid_weight,
    out_weight,
):
    y, x, core, rep = (lax.axis_index(a) for a in ("y", "x", "core", "rep"))
    pos = jnp.stack([rep, core]).astype(jnp.int32)

    part = tile_columns - NB
    far = lax.rem(core + CORE - part % CORE, CORE)
    along_x = lax.rem(x + X - part // CORE % X, X)
    along_y = lax.rem(y + Y - part // (CORE * X), Y)
    halo_at = NB + (far * X + along_x) * Y + along_y
    cols = jnp.where(tile_columns < NB, tile_columns, halo_at).reshape(-1)
    cols = jnp.concatenate([cols, rep[None]]).astype(jnp.int32)
    brow = jnp.broadcast_to(boundary_rows.reshape(TILE, 1), (TILE, TILE))

    all_labels = lax.all_gather(labels, "rep", axis=0, tiled=True)
    all_labels = lax.all_gather(all_labels, ("y", "x", "core"), axis=0, tiled=True)
    dom = (y * X + x) * CORE + core
    own_labels = lax.dynamic_slice_in_dim(
        all_labels.reshape(DOM, DOM * TILE), dom * TILE, TILE, axis=1
    )
    counts = count_labels(
        pos, own_labels, shuffle.reshape(DOM, TILE), train_rows.reshape(DOM, TILE)
    )

    export, *quarters = export_first(pos, features, boundary_rows.reshape(TILE, 1))
    pieces = [[quarters[0]] + [shift(quarters[d], "rep", d) for d in (1, 2, 3)]]
    hop = features
    for h in range(HOPS):
        near, other = spread(export)
        last = h == HOPS - 1
        got = propagate(last, cols, tile_values, hop, near, other, brow)
        quarters = got[-4:]
        pieces.append([quarters[0]] + [shift(quarters[d], "rep", d) for d in (1, 2, 3)])
        if not last:
            hop, export = got[0], got[1]
    pieces = [pieces[h][d] for d in range(REP) for h in range(HOPS + 1)]

    w3 = jnp.pad(out_weight, ((0, 0), (0, CP - C)))
    act1, act2, gl, gm, gf = mlp(pos, pieces, counts, first_weight, mid_weight, w3)
    keep_m, send_m = outer_grads(pos, act1, act2, gl, gm)
    got_m = shift(send_m, "core", 1)
    keep_f, send_f = first_grads(pos, pieces, gf)
    got_f = shift(send_f, "core", 1)
    parts = join_cores(keep_f, got_f, keep_m, got_m)
    parts = lax.all_to_all(parts, ("y", "x", "rep"), split_axis=0, concat_axis=0, tiled=True)
    first, mid, out = total_grads(parts)
    return first, mid, out


def solution(mesh):
    fine = Mesh(mesh.devices.reshape(Y, X, CORE, REP), ("y", "x", "core", "rep"))
    dom = ("y", "x", "core")
    every = dom + ("rep",)
    placed = (
        P(dom, "rep"),
        P(dom, None, None, None),
        P(dom, None),
        P(dom, None),
        P(dom, None),
        P(dom, None),
        P(every),
        P(),
        P(),
        P(),
    )
    return jax.shard_map(
        per_device,
        mesh=fine,
        in_specs=placed,
        out_specs=(P("rep", dom, None), P(every, None), P(every, None)),
        check_vma=False,
    )
```

```python
import functools
import math

import jax
import jax.numpy as jnp
from jax import lax
from jax.experimental import pallas as pl
from jax.experimental.pallas import tpu as pltpu
from jax.sharding import Mesh, PartitionSpec as P

HOPS = 3
TILE = 128
NB = 32
K = 8
R = 4096
HID = 1024
C = 153
CP = 256
Y, X, CORE, REP = 4, 4, 2, 4
DOM = Y * X * CORE
ROWS = R // REP
N_TRAIN = DOM * R
BF = jnp.bfloat16
F32 = jnp.float32
LAB = 16
MIB = 2**20

root_two_pi = 0.7978845608028654
cubic_term = 0.044715


def gelu_pair(v):
    sq = v * v
    t = jnp.tanh(root_two_pi * (v + cubic_term * sq * v))
    half = 0.5 * (1.0 + t)
    slope = half + (0.5 * root_two_pi) * v * (1.0 - t * t) * (
        1.0 + (3.0 * cubic_term) * sq
    )
    return v * half, slope


def dot(a, b, ca, cb):
    return lax.dot_general(a, b, (((ca,), (cb,)), ((), ())), preferred_element_type=F32)


def params(mib):
    return pltpu.CompilerParams(vmem_limit_bytes=mib * MIB)


def whole(memory_space=pltpu.VMEM):
    return pl.BlockSpec(memory_space=memory_space)


def struct(shape, dtype=BF):
    return jax.ShapeDtypeStruct(shape, dtype)


def export_rows(hop, brow):
    row = lax.broadcasted_iota(jnp.int32, (TILE, R), 1)
    return dot((row == brow[...]).astype(BF), hop[...], 1, 0).astype(BF)


def take_quarters(rep, hop, quarters):
    for d, q in enumerate(quarters):
        start = pl.multiple_of(lax.rem(rep + d, REP) * ROWS, ROWS)
        q[:ROWS] = hop[pl.ds(start, ROWS), :]


def export_kernel(pos, hop, brow, labels, export, *quarters):
    got = export_rows(hop, brow)
    extra = jnp.concatenate([labels[...].astype(F32), jnp.zeros((8, TILE), F32)])
    extra = extra.astype(BF)
    for t in range(Y * X):
        export[t, :TILE] = got
        export[t, TILE:] = extra
    take_quarters(pos[0], hop, quarters)


def export_first(pos, hop, brow, labels):
    return pl.pallas_call(
        export_kernel,
        in_specs=[whole(pltpu.SMEM)] + [whole()] * 3,
        out_specs=[whole()] * 5,
        out_shape=[struct((Y * X, TILE + LAB, TILE))] + [struct((ROWS, TILE))] * 4,
        compiler_params=params(16),
        name="export_first",
        cost_estimate=pl.CostEstimate(
            flops=2 * TILE * TILE * R, bytes_accessed=2 * MIB, transcendentals=0
        ),
    )(pos, hop, brow, labels)


CUTS = 8
STEP = NB // CUTS


def prop_kernel(h, cols, tiles, hop, near, far, brow, *rest):
    last = h == HOPS - 1
    if last:
        q0, q1, q2, q3, joined, held, sem, out = rest
    else:
        out, export, q0, q1, q2, q3, joined, held, sem = rest
    r, core, inner = cols[NB * K], cols[NB * K + 1], cols[NB * K + 2]
    copies = [
        pltpu.make_async_copy(
            tiles.at[pl.ds(c * STEP, STEP)], held.at[pl.ds(c * STEP, STEP)], sem.at[c]
        )
        for c in range(CUTS)
    ]
    for copy in copies:
        copy.start()
    joined[:R] = hop[...]
    for t in range(Y * X):
        at = R + t * TILE
        joined[at : at + TILE] = near[t, :TILE]
        joined[at + R // 2 : at + R // 2 + TILE] = far[t, :TILE]
    for c in range(CUTS):
        copies[c].wait()

        @pl.loop(c * STEP, (c + 1) * STEP)
        def _(b):
            parts = []
            for k in range(K):
                at = pl.multiple_of(cols[b * K + k] * TILE, TILE)
                parts.append(joined[pl.ds(at, TILE), :])
            left = jnp.concatenate([held[b, k] for k in range(K)], axis=1)
            got = dot(left, jnp.concatenate(parts, axis=0), 1, 0).astype(BF)
            out[pl.ds(pl.multiple_of(b * TILE, TILE), TILE), :] = got

    if not last:
        got = export_rows(out, brow)
        for t in range(Y * X):
            export[t] = got
    quarters = (q0, q1, q2, q3)
    take_quarters(r, out, quarters)
    if h == 0:
        pick = lax.broadcasted_iota(jnp.int32, (LAB, TILE), 0) == inner
        labs = []
        for t in range(Y * X):
            two = [
                jnp.sum(jnp.where(pick, v[t, TILE:].astype(F32), 0.0), axis=0, keepdims=True)
                for v in (near, far)
            ]
            labs.append(jnp.where(core == 0, two[0], two[1]))
            labs.append(jnp.where(core == 0, two[1], two[0]))
        labs = jnp.concatenate(labs, axis=0).astype(BF)
        for q in quarters:
            q[ROWS:] = labs


def propagate(h, cols, tiles, hop, near, far, brow):
    last = h == HOPS - 1
    outs = [] if last else [(R, TILE), (Y * X, TILE, TILE)]
    outs += [(ROWS + DOM if h == 0 else ROWS, TILE)] * 4
    scratch = [
        pltpu.VMEM((2 * R, TILE), BF),
        pltpu.VMEM((NB, K, TILE, TILE), BF),
        pltpu.SemaphoreType.DMA((CUTS,)),
    ]
    scratch += [pltpu.VMEM((R, TILE), BF)] if last else []
    return pl.pallas_call(
        functools.partial(prop_kernel, h),
        in_specs=[whole(pltpu.SMEM), whole(pltpu.HBM)] + [whole()] * 4,
        out_specs=[whole()] * len(outs),
        scratch_shapes=scratch,
        out_shape=[struct(s) for s in outs],
        compiler_params=params(54),
        name="propagate_" + str(h),
        cost_estimate=pl.CostEstimate(
            flops=2 * NB * K * TILE**3, bytes_accessed=12 * MIB, transcendentals=0
        ),
    )(cols, tiles, hop, near, far, brow)


def count_kernel(pos, lab0, lab1, lab2, lab3, shuffle, train, out):
    labels = jnp.zeros((DOM, TILE), F32)
    for d, v in enumerate((lab0, lab1, lab2, lab3)):
        labels = jnp.where(pos[2] == d, v[...].astype(F32), labels)
    first = lax.broadcasted_iota(jnp.int32, (DOM, TILE), 0)
    second = lax.broadcasted_iota(jnp.int32, (TILE, TILE), 0)
    slots = jnp.zeros((DOM, TILE), F32)
    for lo in range(0, DOM, 8):
        a, b = [], []
        for e in range(lo, lo + 8):
            slot = shuffle[e : e + 1, :]
            label = labels[e : e + 1, :]
            a.append(jnp.where(first == slot // TILE, label, 0.0).astype(BF))
            b.append((second == lax.rem(slot, TILE)).astype(BF))
        slots += dot(jnp.concatenate(a, axis=1), jnp.concatenate(b, axis=1), 1, 1)
    slots = slots.astype(jnp.int32)
    paper = lax.broadcasted_iota(jnp.int32, (ROWS, TILE), 0) + pos[0] * ROWS
    kind = lax.broadcasted_iota(jnp.int32, (CP, TILE), 0)
    total = jnp.zeros((ROWS, CP), F32)
    for lo in range(0, DOM, 8):
        a, b = [], []
        for e in range(lo, lo + 8):
            a.append((paper == train[e : e + 1, :]).astype(BF))
            b.append((kind == slots[e : e + 1, :]).astype(BF))
        total += dot(jnp.concatenate(a, axis=1), jnp.concatenate(b, axis=1), 1, 1)
    out[...] = total


def count_labels(pos, both, shuffle, train):
    def fixed(shape):
        return pl.BlockSpec(shape, lambda i, c: (0, 0))

    tail = pl.BlockSpec((DOM, TILE), lambda i, c: (ROWS // DOM, 0))
    return pl.pallas_call(
        count_kernel,
        grid_spec=pltpu.PrefetchScalarGridSpec(
            num_scalar_prefetch=1,
            grid=(1,),
            in_specs=[tail] * 4 + [fixed((DOM, TILE))] * 2,
            out_specs=fixed((ROWS, CP)),
        ),
        out_shape=struct((ROWS, CP), F32),
        compiler_params=params(24),
        name="count_labels",
        cost_estimate=pl.CostEstimate(
            flops=2 * ROWS * R * CP, bytes_accessed=2 * MIB, transcendentals=0
        ),
    )(pos, *both, shuffle, train)


MLP_ROWS = 256


def slab_of(rep, d):
    return lax.rem(rep + REP - d, REP)


def early_kernel(pos, *refs):
    pieces, (w1, out) = refs[:12], refs[12:]
    total = jnp.zeros((MLP_ROWS, HID), F32)
    for d in range(REP):
        x = jnp.concatenate([pieces[3 * d + h][...] for h in range(HOPS)], axis=1)
        total += dot(x, w1[slab_of(pos[0], d), : HOPS * TILE], 1, 0)
    out[...] = total


def mlp_kernel(pos, *refs):
    pieces, (early, counts, w1, w2, w3, act1, act2, gl, gm, gf) = refs[:4], refs[4:]
    pre1 = early[...]
    for d in range(REP):
        pre1 += dot(pieces[d][...], w1[slab_of(pos[0], d), HOPS * TILE :], 1, 0)
    a1, slope1 = gelu_pair(pre1)
    a1 = a1.astype(BF)
    act1[...] = a1
    a2, slope2 = gelu_pair(dot(a1, w2[...], 1, 0))
    a2 = a2.astype(BF)
    act2[...] = a2
    logits = dot(a2, w3[...], 1, 0)
    kind = lax.broadcasted_iota(jnp.int32, (MLP_ROWS, CP), 1)
    ex = jnp.where(kind < C, jnp.exp(logits), 0.0)
    probs = ex / jnp.sum(ex, axis=1, keepdims=True)
    drawn = counts[...]
    many = jnp.sum(drawn, axis=1, keepdims=True)
    g3 = ((probs * many - drawn) * (1.0 / math.sqrt(N_TRAIN))).astype(BF)
    gl[...] = g3
    g2 = (dot(g3, w3[...], 1, 1) * slope2).astype(BF)
    gm[...] = g2
    gf[...] = (dot(g2, w2[...], 1, 1) * slope1).astype(BF)


def fixed_block(shape):
    return pl.BlockSpec(shape, lambda i, c: (0,) * len(shape))


def row_block(width):
    return pl.BlockSpec((MLP_ROWS, width), lambda i, c: (i, 0))


def first_layer_early(pos, pieces, w1):
    return pl.pallas_call(
        early_kernel,
        grid_spec=pltpu.PrefetchScalarGridSpec(
            num_scalar_prefetch=1,
            grid=(ROWS // MLP_ROWS,),
            in_specs=[row_block(TILE)] * 12 + [fixed_block(w1.shape)],
            out_specs=row_block(HID),
        ),
        out_shape=struct((ROWS, HID), F32),
        compiler_params=params(20),
        name="first_layer_early",
        cost_estimate=pl.CostEstimate(
            flops=2 * ROWS * HID * 3 * 512, bytes_accessed=11 * MIB, transcendentals=0
        ),
    )(pos, *pieces, w1)


def mlp(pos, pieces, early, counts, w1, w2, w3):
    widths = (HID, HID, CP, HID, HID)
    return pl.pallas_call(
        mlp_kernel,
        grid_spec=pltpu.PrefetchScalarGridSpec(
            num_scalar_prefetch=1,
            grid=(ROWS // MLP_ROWS,),
            in_specs=[row_block(TILE)] * 4
            + [row_block(HID), row_block(CP)]
            + [fixed_block(w.shape) for w in (w1, w2, w3)],
            out_specs=[row_block(w) for w in widths],
        ),
        out_shape=[struct((ROWS, w)) for w in widths],
        compiler_params=params(36),
        name="mlp",
        cost_estimate=pl.CostEstimate(
            flops=2 * ROWS * HID * (2 * HID + 512 + 2 * CP),
            bytes_accessed=20 * MIB,
            transcendentals=2 * ROWS * HID,
        ),
    )(pos, *pieces, early, counts, w1, w2, w3)


WIDE = (HID + CP) // 2


def outer_kernel(pos, act1, act2, gl, gm, keep, send):
    own = pos[1] == 0
    width = HID // Y
    for y in range(Y):
        cut = slice(y * width, (y + 1) * width)
        mid = dot(act1[:, cut], gm[...], 0, 0)
        out = dot(act2[:, cut], gl[...], 0, 0)
        both = jnp.concatenate([mid, out], axis=1).reshape(X, CORE, REP, 8, HID + CP)
        both = jnp.concatenate([both[..., :WIDE], both[..., WIDE:]], axis=3)
        zero, one = both[:, 0], both[:, 1]
        keep[y] = jnp.where(own, zero, one).astype(BF)
        send[y] = jnp.where(own, one, zero).astype(BF)


def outer_grads(pos, act1, act2, gl, gm):
    shape = (Y, X, REP, 16, WIDE)
    return pl.pallas_call(
        outer_kernel,
        in_specs=[whole(pltpu.SMEM)] + [whole()] * 4,
        out_specs=[whole()] * 2,
        out_shape=[struct(shape)] * 2,
        compiler_params=params(30),
        name="outer_grads",
        cost_estimate=pl.CostEstimate(
            flops=2 * ROWS * HID * (HID + CP), bytes_accessed=8 * MIB, transcendentals=0
        ),
    )(pos, act1, act2, gl, gm)


def first_kernel(pos, *refs):
    pieces, (gf, keep, send) = refs[:16], refs[16:]
    own = pos[1] == 0
    for d in range(REP):
        slab = lax.rem(pos[0] + REP - d, REP)
        for y in range(0, Y, 2):
            two = [pieces[4 * u + d][:ROWS] for u in (y, y + 1)]
            x = jnp.concatenate(two, axis=1)
            got = dot(x, gf[...], 0, 0).reshape(2, X, CORE, 16, HID)
            zero, one = got[:, :, 0], got[:, :, 1]
            kept = jnp.where(own, zero, one).astype(BF)
            sent = jnp.where(own, one, zero).astype(BF)
            for u in range(2):
                for v in range(X):
                    keep[y + u, v, slab] = kept[u, v]
                    send[y + u, v, slab] = sent[u, v]


def first_grads(pos, pieces, gf):
    shape = (Y, X, REP, 16, HID)
    return pl.pallas_call(
        first_kernel,
        in_specs=[whole(pltpu.SMEM)] + [whole()] * 17,
        out_specs=[whole()] * 2,
        out_shape=[struct(shape)] * 2,
        compiler_params=params(36),
        name="first_grads",
        cost_estimate=pl.CostEstimate(
            flops=4 * ROWS * HID * HID, bytes_accessed=10 * MIB, transcendentals=0
        ),
    )(pos, *pieces, gf)


def join_kernel(keep_f, got_f, keep_m, got_m, out):
    out[:, :, :HID] = (keep_f[...].astype(F32) + got_f[...].astype(F32)).astype(BF)
    out[:, :, HID:] = (keep_m[...].astype(F32) + got_m[...].astype(F32)).astype(BF)


def join_cores(keep_f, got_f, keep_m, got_m):
    n = Y * X * REP
    flat = [v.reshape(n, 16, v.shape[-1]) for v in (keep_f, got_f, keep_m, got_m)]

    def spec(width):
        return pl.BlockSpec((8, 16, width), lambda i: (i, 0, 0))

    return pl.pallas_call(
        join_kernel,
        grid=(n // 8,),
        in_specs=[spec(v.shape[-1]) for v in flat],
        out_specs=spec(HID + WIDE),
        out_shape=struct((n, 16, HID + WIDE)),
        compiler_params=params(8),
        name="join_cores",
    )(*flat)


def total_kernel(parts, first, mid, out):
    total = jnp.sum(parts[...].astype(F32), axis=0)
    first[0] = total[:, :HID]
    rest = jnp.concatenate([total[:8, HID:], total[8:, HID:]], axis=1)
    mid[...] = rest[:, :HID]
    out[...] = rest[:, HID : HID + C]


def total_grads(parts):
    return pl.pallas_call(
        total_kernel,
        in_specs=[whole()],
        out_specs=[whole()] * 3,
        out_shape=[struct((1, 16, HID), F32), struct((8, HID), F32), struct((8, C), F32)],
        compiler_params=params(16),
        name="total_grads",
    )(parts)


def shift(value, axis, by):
    size = lax.axis_size(axis)
    return lax.ppermute(value, axis, [(i, (i + by) % size) for i in range(size)])


def spread(export):
    return lax.all_to_all(export, ("y", "x"), split_axis=0, concat_axis=0, tiled=True)


def exchange(quarters):
    return [quarters[0]] + [shift(quarters[d], "rep", d) for d in (1, 2, 3)]


def per_device(
    features,
    tile_values,
    tile_columns,
    boundary_rows,
    train_rows,
    shuffle,
    labels,
    first_weight,
    mid_weight,
    out_weight,
):
    y, x, core, rep = (lax.axis_index(a) for a in ("y", "x", "core", "rep"))
    pos = jnp.stack([rep, core, lax.rem(rep + REP - y, REP)]).astype(jnp.int32)

    part = tile_columns - NB
    halo_at = NB + (part + core) % CORE * (NB // CORE) + part // CORE
    cols = jnp.where(tile_columns < NB, tile_columns, halo_at).reshape(-1)
    inner = lax.rem((y * X + x) * CORE + core, DOM // REP)
    cols = jnp.concatenate([cols, jnp.stack([rep, core, inner])]).astype(jnp.int32)
    brow = boundary_rows.reshape(TILE, 1)

    export, *quarters = export_first(pos, features, brow, labels.reshape(8, TILE))
    hop, pieces, counts = features, [], None
    for h in range(HOPS):
        got = exchange(quarters)
        if h == HOPS - 1:
            counts = count_labels(
                pos, pieces[1], shuffle.reshape(DOM, TILE), train_rows.reshape(DOM, TILE)
            )
        near, got, counts = lax.optimization_barrier((spread(export), got, counts))
        far = shift(near, "core", 1)
        pieces.append(got)
        made = propagate(h, cols, tile_values, hop, near, far, brow)
        hop, export, quarters = made[0], made[1], made[-4:]
    early = first_layer_early(
        pos, [pieces[h][d] for d in range(REP) for h in range(HOPS)], first_weight
    )
    pieces.append(exchange(quarters))

    w3 = jnp.pad(out_weight, ((0, 0), (0, CP - C)))
    act1, act2, gl, gm, gf = mlp(
        pos, pieces[3], early, counts, first_weight, mid_weight, w3
    )
    pieces = [v for got in pieces for v in got]
    keep_f, send_f = first_grads(pos, pieces, gf)
    got_f = shift(send_f, "core", 1)
    keep_m, send_m = outer_grads(pos, act1, act2, gl, gm)
    got_m = shift(send_m, "core", 1)
    parts = join_cores(keep_f, got_f, keep_m, got_m)
    parts = lax.all_to_all(parts, ("y", "x", "rep"), split_axis=0, concat_axis=0, tiled=True)
    first, mid, out = total_grads(parts)
    return first, mid, out


def solution(mesh):
    fine = Mesh(mesh.devices.reshape(Y, X, CORE, REP), ("y", "x", "core", "rep"))
    dom = ("y", "x", "core")
    every = dom + ("rep",)
    placed = (
        P(dom, "rep"),
        P(dom, None, None, None),
        P(dom, None),
        P(dom, None),
        P(dom, None),
        P(dom, None),
        P(every),
        P(),
        P(),
        P(),
    )
    return jax.shard_map(
        per_device,
        mesh=fine,
        in_specs=placed,
        out_specs=(P("rep", dom, None), P(every, None), P(every, None)),
        check_vma=False,
    )
```

```python
import functools
import math

import jax
import jax.numpy as jnp
from jax import lax
from jax.experimental import pallas as pl
from jax.experimental.pallas import tpu as pltpu
from jax.sharding import Mesh, PartitionSpec as P

HOPS = 3
TILE = 128
NB = 32
K = 8
R = 4096
HID = 1024
C = 153
CP = 256
Y, X, CORE, REP = 4, 4, 2, 4
DOM = Y * X * CORE
ROWS = R // REP
N_TRAIN = DOM * R
BF = jnp.bfloat16
F32 = jnp.float32
LAB = 16
MIB = 2**20

root_two_pi = 0.7978845608028654
cubic_term = 0.044715


def gelu_pair(v):
    sq = v * v
    t = jnp.tanh(root_two_pi * (v + cubic_term * sq * v))
    half = 0.5 * (1.0 + t)
    slope = half + (0.5 * root_two_pi) * v * (1.0 - t * t) * (
        1.0 + (3.0 * cubic_term) * sq
    )
    return v * half, slope


def dot(a, b, ca, cb):
    return lax.dot_general(a, b, (((ca,), (cb,)), ((), ())), preferred_element_type=F32)


def params(mib):
    return pltpu.CompilerParams(vmem_limit_bytes=mib * MIB)


def whole(memory_space=pltpu.VMEM):
    return pl.BlockSpec(memory_space=memory_space)


def struct(shape, dtype=BF):
    return jax.ShapeDtypeStruct(shape, dtype)


def export_rows(hop, brow):
    row = lax.broadcasted_iota(jnp.int32, (TILE, R), 1)
    return dot((row == brow[...]).astype(BF), hop[...], 1, 0).astype(BF)


def take_quarters(rep, hop, quarters):
    for d, q in enumerate(quarters):
        start = pl.multiple_of(lax.rem(rep + d, REP) * ROWS, ROWS)
        q[:ROWS] = hop[pl.ds(start, ROWS), :]


def export_kernel(pos, hop, brow, labels, export, *quarters):
    got = export_rows(hop, brow)
    extra = jnp.concatenate([labels[...].astype(F32), jnp.zeros((8, TILE), F32)])
    extra = extra.astype(BF)
    for t in range(Y * X):
        export[t, :TILE] = got
        export[t, TILE:] = extra
    take_quarters(pos[0], hop, quarters)


def export_first(pos, hop, brow, labels):
    return pl.pallas_call(
        export_kernel,
        in_specs=[whole(pltpu.SMEM)] + [whole()] * 3,
        out_specs=[whole()] * 5,
        out_shape=[struct((Y * X, TILE + LAB, TILE))] + [struct((ROWS, TILE))] * 4,
        compiler_params=params(16),
        name="export_first",
        cost_estimate=pl.CostEstimate(
            flops=2 * TILE * TILE * R, bytes_accessed=2 * MIB, transcendentals=0
        ),
    )(pos, hop, brow, labels)


CUTS = 8
STEP = NB // CUTS


def prop_kernel(h, cols, tiles, hop, near, far, brow, *rest):
    last = h == HOPS - 1
    if last:
        q0, q1, q2, q3, joined, held, sem, out = rest
    else:
        out, export, q0, q1, q2, q3, joined, held, sem = rest
    r, core, inner = cols[NB * K], cols[NB * K + 1], cols[NB * K + 2]
    copies = [
        pltpu.make_async_copy(
            tiles.at[pl.ds(c * STEP, STEP)], held.at[pl.ds(c * STEP, STEP)], sem.at[c]
        )
        for c in range(CUTS)
    ]
    for copy in copies:
        copy.start()
    joined[:R] = hop[...]
    for t in range(Y * X):
        at = R + t * TILE
        joined[at : at + TILE] = near[t, :TILE]
        joined[at + R // 2 : at + R // 2 + TILE] = far[t, :TILE]
    for b in range(NB):
        if b % STEP == 0:
            copies[b // STEP].wait()
        parts = []
        for k in range(K):
            at = pl.multiple_of(cols[b * K + k] * TILE, TILE)
            parts.append(joined[pl.ds(at, TILE), :])
        left = jnp.concatenate([held[b, k] for k in range(K)], axis=1)
        got = dot(left, jnp.concatenate(parts, axis=0), 1, 0)
        out[b * TILE : (b + 1) * TILE, :] = got.astype(BF)

    if not last:
        got = export_rows(out, brow)
        for t in range(Y * X):
            export[t] = got
    quarters = (q0, q1, q2, q3)
    take_quarters(r, out, quarters)
    if h == 0:
        pick = lax.broadcasted_iota(jnp.int32, (LAB, TILE), 0) == inner
        labs = []
        for t in range(Y * X):
            two = [
                jnp.sum(jnp.where(pick, v[t, TILE:].astype(F32), 0.0), axis=0, keepdims=True)
                for v in (near, far)
            ]
            labs.append(jnp.where(core == 0, two[0], two[1]))
            labs.append(jnp.where(core == 0, two[1], two[0]))
        labs = jnp.concatenate(labs, axis=0).astype(BF)
        for q in quarters:
            q[ROWS:] = labs


def propagate(h, cols, tiles, hop, near, far, brow):
    last = h == HOPS - 1
    outs = [] if last else [(R, TILE), (Y * X, TILE, TILE)]
    outs += [(ROWS + DOM if h == 0 else ROWS, TILE)] * 4
    scratch = [
        pltpu.VMEM((2 * R, TILE), BF),
        pltpu.VMEM((NB, K, TILE, TILE), BF),
        pltpu.SemaphoreType.DMA((CUTS,)),
    ]
    scratch += [pltpu.VMEM((R, TILE), BF)] if last else []
    return pl.pallas_call(
        functools.partial(prop_kernel, h),
        in_specs=[whole(pltpu.SMEM), whole(pltpu.HBM)] + [whole()] * 4,
        out_specs=[whole()] * len(outs),
        scratch_shapes=scratch,
        out_shape=[struct(s) for s in outs],
        compiler_params=params(54),
        name="propagate_" + str(h),
        cost_estimate=pl.CostEstimate(
            flops=2 * NB * K * TILE**3, bytes_accessed=12 * MIB, transcendentals=0
        ),
    )(cols, tiles, hop, near, far, brow)


def count_kernel(pos, lab0, lab1, lab2, lab3, shuffle, train, out):
    labels = jnp.zeros((DOM, TILE), F32)
    for d, v in enumerate((lab0, lab1, lab2, lab3)):
        labels = jnp.where(pos[2] == d, v[...].astype(F32), labels)
    first = lax.broadcasted_iota(jnp.int32, (DOM, TILE), 0)
    second = lax.broadcasted_iota(jnp.int32, (TILE, TILE), 0)
    slots = jnp.zeros((DOM, TILE), F32)
    for lo in range(0, DOM, 8):
        a, b = [], []
        for e in range(lo, lo + 8):
            slot = shuffle[e : e + 1, :]
            label = labels[e : e + 1, :]
            a.append(jnp.where(first == slot // TILE, label, 0.0).astype(BF))
            b.append((second == lax.rem(slot, TILE)).astype(BF))
        slots += dot(jnp.concatenate(a, axis=1), jnp.concatenate(b, axis=1), 1, 1)
    slots = slots.astype(jnp.int32)
    paper = lax.broadcasted_iota(jnp.int32, (ROWS, TILE), 0) + pos[0] * ROWS
    kind = lax.broadcasted_iota(jnp.int32, (CP, TILE), 0)
    total = jnp.zeros((ROWS, CP), F32)
    for lo in range(0, DOM, 8):
        a, b = [], []
        for e in range(lo, lo + 8):
            a.append((paper == train[e : e + 1, :]).astype(BF))
            b.append((kind == slots[e : e + 1, :]).astype(BF))
        total += dot(jnp.concatenate(a, axis=1), jnp.concatenate(b, axis=1), 1, 1)
    out[...] = total


def count_labels(pos, both, shuffle, train):
    def fixed(shape):
        return pl.BlockSpec(shape, lambda i, c: (0, 0))

    tail = pl.BlockSpec((DOM, TILE), lambda i, c: (ROWS // DOM, 0))
    return pl.pallas_call(
        count_kernel,
        grid_spec=pltpu.PrefetchScalarGridSpec(
            num_scalar_prefetch=1,
            grid=(1,),
            in_specs=[tail] * 4 + [fixed((DOM, TILE))] * 2,
            out_specs=fixed((ROWS, CP)),
        ),
        out_shape=struct((ROWS, CP), F32),
        compiler_params=params(24),
        name="count_labels",
        cost_estimate=pl.CostEstimate(
            flops=2 * ROWS * R * CP, bytes_accessed=2 * MIB, transcendentals=0
        ),
    )(pos, *both, shuffle, train)


MLP_ROWS = 256


def slab_of(rep, d):
    return lax.rem(rep + REP - d, REP)


def early_kernel(pos, *refs):
    pieces, (w1, out) = refs[:12], refs[12:]
    total = jnp.zeros((MLP_ROWS, HID), F32)
    for d in range(REP):
        x = jnp.concatenate([pieces[3 * d + h][...] for h in range(HOPS)], axis=1)
        total += dot(x, w1[slab_of(pos[0], d), : HOPS * TILE], 1, 0)
    out[...] = total


def mlp_kernel(pos, *refs):
    pieces, (early, counts, w1, w2, w3, act1, act2, gl, gm, gf) = refs[:4], refs[4:]
    pre1 = early[...]
    for d in range(REP):
        pre1 += dot(pieces[d][...], w1[slab_of(pos[0], d), HOPS * TILE :], 1, 0)
    a1, slope1 = gelu_pair(pre1)
    a1 = a1.astype(BF)
    act1[...] = a1
    a2, slope2 = gelu_pair(dot(a1, w2[...], 1, 0))
    a2 = a2.astype(BF)
    act2[...] = a2
    logits = dot(a2, w3[...], 1, 0)
    kind = lax.broadcasted_iota(jnp.int32, (MLP_ROWS, CP), 1)
    ex = jnp.where(kind < C, jnp.exp(logits), 0.0)
    probs = ex / jnp.sum(ex, axis=1, keepdims=True)
    drawn = counts[...]
    many = jnp.sum(drawn, axis=1, keepdims=True)
    g3 = ((probs * many - drawn) * (1.0 / math.sqrt(N_TRAIN))).astype(BF)
    gl[...] = g3
    g2 = (dot(g3, w3[...], 1, 1) * slope2).astype(BF)
    gm[...] = g2
    gf[...] = (dot(g2, w2[...], 1, 1) * slope1).astype(BF)


def fixed_block(shape):
    return pl.BlockSpec(shape, lambda i, c: (0,) * len(shape))


def row_block(width):
    return pl.BlockSpec((MLP_ROWS, width), lambda i, c: (i, 0))


def first_layer_early(pos, pieces, w1):
    return pl.pallas_call(
        early_kernel,
        grid_spec=pltpu.PrefetchScalarGridSpec(
            num_scalar_prefetch=1,
            grid=(ROWS // MLP_ROWS,),
            in_specs=[row_block(TILE)] * 12 + [fixed_block(w1.shape)],
            out_specs=row_block(HID),
        ),
        out_shape=struct((ROWS, HID), F32),
        compiler_params=params(20),
        name="first_layer_early",
        cost_estimate=pl.CostEstimate(
            flops=2 * ROWS * HID * 3 * 512, bytes_accessed=11 * MIB, transcendentals=0
        ),
    )(pos, *pieces, w1)


def mlp(pos, pieces, early, counts, w1, w2, w3):
    widths = (HID, HID, CP, HID, HID)
    return pl.pallas_call(
        mlp_kernel,
        grid_spec=pltpu.PrefetchScalarGridSpec(
            num_scalar_prefetch=1,
            grid=(ROWS // MLP_ROWS,),
            in_specs=[row_block(TILE)] * 4
            + [row_block(HID), row_block(CP)]
            + [fixed_block(w.shape) for w in (w1, w2, w3)],
            out_specs=[row_block(w) for w in widths],
        ),
        out_shape=[struct((ROWS, w)) for w in widths],
        compiler_params=params(36),
        name="mlp",
        cost_estimate=pl.CostEstimate(
            flops=2 * ROWS * HID * (2 * HID + 512 + 2 * CP),
            bytes_accessed=20 * MIB,
            transcendentals=2 * ROWS * HID,
        ),
    )(pos, *pieces, early, counts, w1, w2, w3)


WIDE = (HID + CP) // 2


def outer_kernel(pos, act1, act2, gl, gm, keep, send):
    own = pos[1] == 0
    width = HID // Y
    for y in range(Y):
        cut = slice(y * width, (y + 1) * width)
        mid = dot(act1[:, cut], gm[...], 0, 0)
        out = dot(act2[:, cut], gl[...], 0, 0)
        both = jnp.concatenate([mid, out], axis=1).reshape(X, CORE, REP, 8, HID + CP)
        both = jnp.concatenate([both[..., :WIDE], both[..., WIDE:]], axis=3)
        zero, one = both[:, 0], both[:, 1]
        keep[y] = jnp.where(own, zero, one).astype(BF)
        send[y] = jnp.where(own, one, zero).astype(BF)


def outer_grads(pos, act1, act2, gl, gm):
    shape = (Y, X, REP, 16, WIDE)
    return pl.pallas_call(
        outer_kernel,
        in_specs=[whole(pltpu.SMEM)] + [whole()] * 4,
        out_specs=[whole()] * 2,
        out_shape=[struct(shape)] * 2,
        compiler_params=params(30),
        name="outer_grads",
        cost_estimate=pl.CostEstimate(
            flops=2 * ROWS * HID * (HID + CP), bytes_accessed=8 * MIB, transcendentals=0
        ),
    )(pos, act1, act2, gl, gm)


def first_kernel(pos, *refs):
    pieces, (gf, keep, send) = refs[:16], refs[16:]
    own = pos[1] == 0
    for d in range(REP):
        slab = lax.rem(pos[0] + REP - d, REP)
        for y in range(0, Y, 2):
            two = [pieces[4 * u + d][:ROWS] for u in (y, y + 1)]
            x = jnp.concatenate(two, axis=1)
            got = dot(x, gf[...], 0, 0).reshape(2, X, CORE, 16, HID)
            zero, one = got[:, :, 0], got[:, :, 1]
            kept = jnp.where(own, zero, one).astype(BF)
            sent = jnp.where(own, one, zero).astype(BF)
            for u in range(2):
                for v in range(X):
                    keep[y + u, v, slab] = kept[u, v]
                    send[y + u, v, slab] = sent[u, v]


def first_grads(pos, pieces, gf):
    shape = (Y, X, REP, 16, HID)
    return pl.pallas_call(
        first_kernel,
        in_specs=[whole(pltpu.SMEM)] + [whole()] * 17,
        out_specs=[whole()] * 2,
        out_shape=[struct(shape)] * 2,
        compiler_params=params(36),
        name="first_grads",
        cost_estimate=pl.CostEstimate(
            flops=4 * ROWS * HID * HID, bytes_accessed=10 * MIB, transcendentals=0
        ),
    )(pos, *pieces, gf)


def join_kernel(keep_f, got_f, keep_m, got_m, out):
    out[:, :, :HID] = (keep_f[...].astype(F32) + got_f[...].astype(F32)).astype(BF)
    out[:, :, HID:] = (keep_m[...].astype(F32) + got_m[...].astype(F32)).astype(BF)


def join_cores(keep_f, got_f, keep_m, got_m):
    n = Y * X * REP
    flat = [v.reshape(n, 16, v.shape[-1]) for v in (keep_f, got_f, keep_m, got_m)]

    def spec(width):
        return pl.BlockSpec((8, 16, width), lambda i: (i, 0, 0))

    return pl.pallas_call(
        join_kernel,
        grid=(n // 8,),
        in_specs=[spec(v.shape[-1]) for v in flat],
        out_specs=spec(HID + WIDE),
        out_shape=struct((n, 16, HID + WIDE)),
        compiler_params=params(8),
        name="join_cores",
    )(*flat)


def total_kernel(parts, first, mid, out):
    total = jnp.sum(parts[...].astype(F32), axis=0)
    first[0] = total[:, :HID]
    rest = jnp.concatenate([total[:8, HID:], total[8:, HID:]], axis=1)
    mid[...] = rest[:, :HID]
    out[...] = rest[:, HID : HID + C]


def total_grads(parts):
    return pl.pallas_call(
        total_kernel,
        in_specs=[whole()],
        out_specs=[whole()] * 3,
        out_shape=[struct((1, 16, HID), F32), struct((8, HID), F32), struct((8, C), F32)],
        compiler_params=params(16),
        name="total_grads",
    )(parts)


def shift(value, axis, by):
    size = lax.axis_size(axis)
    return lax.ppermute(value, axis, [(i, (i + by) % size) for i in range(size)])


def spread(export):
    return lax.all_to_all(export, ("y", "x"), split_axis=0, concat_axis=0, tiled=True)


def exchange(quarters):
    return [quarters[0]] + [shift(quarters[d], "rep", d) for d in (1, 2, 3)]


def per_device(
    features,
    tile_values,
    tile_columns,
    boundary_rows,
    train_rows,
    shuffle,
    labels,
    first_weight,
    mid_weight,
    out_weight,
):
    y, x, core, rep = (lax.axis_index(a) for a in ("y", "x", "core", "rep"))
    pos = jnp.stack([rep, core, lax.rem(rep + REP - y, REP)]).astype(jnp.int32)

    part = tile_columns - NB
    halo_at = NB + (part + core) % CORE * (NB // CORE) + part // CORE
    cols = jnp.where(tile_columns < NB, tile_columns, halo_at).reshape(-1)
    inner = lax.rem((y * X + x) * CORE + core, DOM // REP)
    cols = jnp.concatenate([cols, jnp.stack([rep, core, inner])]).astype(jnp.int32)
    brow = boundary_rows.reshape(TILE, 1)

    export, *quarters = export_first(pos, features, brow, labels.reshape(8, TILE))
    hop, pieces, counts = features, [], None
    for h in range(HOPS):
        got = exchange(quarters)
        if h == HOPS - 1:
            counts = count_labels(
                pos, pieces[1], shuffle.reshape(DOM, TILE), train_rows.reshape(DOM, TILE)
            )
        near, got, counts = lax.optimization_barrier((spread(export), got, counts))
        far = shift(near, "core", 1)
        pieces.append(got)
        made = propagate(h, cols, tile_values, hop, near, far, brow)
        hop, export, quarters = made[0], made[1], made[-4:]
    early = first_layer_early(
        pos, [pieces[h][d] for d in range(REP) for h in range(HOPS)], first_weight
    )
    pieces.append(exchange(quarters))

    w3 = jnp.pad(out_weight, ((0, 0), (0, CP - C)))
    act1, act2, gl, gm, gf = mlp(
        pos, pieces[3], early, counts, first_weight, mid_weight, w3
    )
    pieces = [v for got in pieces for v in got]
    keep_f, send_f = first_grads(pos, pieces, gf)
    got_f = shift(send_f, "core", 1)
    keep_m, send_m = outer_grads(pos, act1, act2, gl, gm)
    got_m = shift(send_m, "core", 1)
    parts = join_cores(keep_f, got_f, keep_m, got_m)
    parts = lax.all_to_all(parts, ("y", "x", "rep"), split_axis=0, concat_axis=0, tiled=True)
    first, mid, out = total_grads(parts)
    return first, mid, out


def solution(mesh):
    fine = Mesh(mesh.devices.reshape(Y, X, CORE, REP), ("y", "x", "core", "rep"))
    dom = ("y", "x", "core")
    every = dom + ("rep",)
    placed = (
        P(dom, "rep"),
        P(dom, None, None, None),
        P(dom, None),
        P(dom, None),
        P(dom, None),
        P(dom, None),
        P(every),
        P(),
        P(),
        P(),
    )
    return jax.shard_map(
        per_device,
        mesh=fine,
        in_specs=placed,
        out_specs=(P("rep", dom, None), P(every, None), P(every, None)),
        check_vma=False,
    )
```

```python
import functools
import math

import jax
import jax.numpy as jnp
from jax import lax
from jax.experimental import pallas as pl
from jax.experimental.pallas import tpu as pltpu
from jax.sharding import Mesh, PartitionSpec as P

HOPS = 3
TILE = 128
NB = 32
K = 8
R = 4096
HID = 1024
C = 153
CP = 256
Y, X, CORE, REP = 4, 4, 2, 4
DOM = Y * X * CORE
ROWS = R // REP
N_TRAIN = DOM * R
BF = jnp.bfloat16
F32 = jnp.float32
LAB = 16
MIB = 2**20

root_two_pi = 0.7978845608028654
cubic_term = 0.044715


def gelu_pair(v):
    sq = v * v
    t = jnp.tanh(root_two_pi * (v + cubic_term * sq * v))
    half = 0.5 * (1.0 + t)
    slope = half + (0.5 * root_two_pi) * v * (1.0 - t * t) * (
        1.0 + (3.0 * cubic_term) * sq
    )
    return v * half, slope


def dot(a, b, ca, cb):
    return lax.dot_general(a, b, (((ca,), (cb,)), ((), ())), preferred_element_type=F32)


def params(mib):
    return pltpu.CompilerParams(vmem_limit_bytes=mib * MIB)


def whole(memory_space=pltpu.VMEM):
    return pl.BlockSpec(memory_space=memory_space)


def struct(shape, dtype=BF):
    return jax.ShapeDtypeStruct(shape, dtype)


def export_rows(hop, brow):
    row = lax.broadcasted_iota(jnp.int32, (TILE, R), 1)
    return dot((row == brow[...]).astype(BF), hop[...], 1, 0).astype(BF)


def take_quarters(rep, hop, quarters):
    for d, q in enumerate(quarters):
        start = pl.multiple_of(lax.rem(rep + d, REP) * ROWS, ROWS)
        q[:ROWS] = hop[pl.ds(start, ROWS), :]


def export_kernel(pos, hop, brow, labels, export, *quarters):
    got = export_rows(hop, brow)
    extra = jnp.concatenate([labels[...].astype(F32), jnp.zeros((8, TILE), F32)])
    extra = extra.astype(BF)
    for t in range(Y * X):
        export[t, :TILE] = got
        export[t, TILE:] = extra
    take_quarters(pos[0], hop, quarters)


def export_first(pos, hop, brow, labels):
    return pl.pallas_call(
        export_kernel,
        in_specs=[whole(pltpu.SMEM)] + [whole()] * 3,
        out_specs=[whole()] * 5,
        out_shape=[struct((Y * X, TILE + LAB, TILE))] + [struct((ROWS, TILE))] * 4,
        compiler_params=params(16),
        name="export_first",
        cost_estimate=pl.CostEstimate(
            flops=2 * TILE * TILE * R, bytes_accessed=2 * MIB, transcendentals=0
        ),
    )(pos, hop, brow, labels)


CUTS = 8
STEP = NB // CUTS


def prop_kernel(h, cols, tiles, hop, near, far, brow, *rest):
    last = h == HOPS - 1
    if last:
        q0, q1, q2, q3, joined, held, sem, out = rest
    else:
        out, export, q0, q1, q2, q3, joined, held, sem = rest
    r, core, inner = cols[NB * K], cols[NB * K + 1], cols[NB * K + 2]
    copies = [
        pltpu.make_async_copy(
            tiles.at[pl.ds(c * STEP, STEP)], held.at[pl.ds(c * STEP, STEP)], sem.at[c]
        )
        for c in range(CUTS)
    ]
    for copy in copies:
        copy.start()
    joined[:R] = hop[...]
    for t in range(Y * X):
        at = R + t * TILE
        joined[at : at + TILE] = near[t, :TILE]
        joined[at + R // 2 : at + R // 2 + TILE] = far[t, :TILE]
    for b in range(NB):
        if b % STEP == 0:
            copies[b // STEP].wait()
        parts = []
        for k in range(K):
            at = pl.multiple_of(cols[b * K + k] * TILE, TILE)
            parts.append(joined[pl.ds(at, TILE), :])
        left = jnp.concatenate([held[b, k] for k in range(K)], axis=1)
        got = dot(left, jnp.concatenate(parts, axis=0), 1, 0)
        out[b * TILE : (b + 1) * TILE, :] = got.astype(BF)

    if not last:
        got = export_rows(out, brow)
        for t in range(Y * X):
            export[t] = got
    quarters = (q0, q1, q2, q3)
    take_quarters(r, out, quarters)
    if h == 0:
        pick = lax.broadcasted_iota(jnp.int32, (LAB, TILE), 0) == inner
        labs = []
        for t in range(Y * X):
            two = [
                jnp.sum(jnp.where(pick, v[t, TILE:].astype(F32), 0.0), axis=0, keepdims=True)
                for v in (near, far)
            ]
            labs.append(jnp.where(core == 0, two[0], two[1]))
            labs.append(jnp.where(core == 0, two[1], two[0]))
        labs = jnp.concatenate(labs, axis=0).astype(BF)
        for q in quarters:
            q[ROWS:] = labs


def propagate(h, cols, tiles, hop, near, far, brow):
    last = h == HOPS - 1
    outs = [] if last else [(R, TILE), (Y * X, TILE, TILE)]
    outs += [(ROWS + DOM if h == 0 else ROWS, TILE)] * 4
    scratch = [
        pltpu.VMEM((2 * R, TILE), BF),
        pltpu.VMEM((NB, K, TILE, TILE), BF),
        pltpu.SemaphoreType.DMA((CUTS,)),
    ]
    scratch += [pltpu.VMEM((R, TILE), BF)] if last else []
    return pl.pallas_call(
        functools.partial(prop_kernel, h),
        in_specs=[whole(pltpu.SMEM), whole(pltpu.HBM)] + [whole()] * 4,
        out_specs=[whole()] * len(outs),
        scratch_shapes=scratch,
        out_shape=[struct(s) for s in outs],
        compiler_params=params(54),
        name="propagate_" + str(h),
        cost_estimate=pl.CostEstimate(
            flops=2 * NB * K * TILE**3, bytes_accessed=12 * MIB, transcendentals=0
        ),
    )(cols, tiles, hop, near, far, brow)


def count_kernel(pos, lab0, lab1, lab2, lab3, shuffle, train, out):
    labels = jnp.zeros((DOM, TILE), F32)
    for d, v in enumerate((lab0, lab1, lab2, lab3)):
        labels = jnp.where(pos[2] == d, v[...].astype(F32), labels)
    first = lax.broadcasted_iota(jnp.int32, (DOM, TILE), 0)
    second = lax.broadcasted_iota(jnp.int32, (TILE, TILE), 0)
    slots = jnp.zeros((DOM, TILE), F32)
    for lo in range(0, DOM, 8):
        a, b = [], []
        for e in range(lo, lo + 8):
            slot = shuffle[e : e + 1, :]
            label = labels[e : e + 1, :]
            a.append(jnp.where(first == slot // TILE, label, 0.0).astype(BF))
            b.append((second == lax.rem(slot, TILE)).astype(BF))
        slots += dot(jnp.concatenate(a, axis=1), jnp.concatenate(b, axis=1), 1, 1)
    slots = slots.astype(jnp.int32)
    paper = lax.broadcasted_iota(jnp.int32, (ROWS, TILE), 0) + pos[0] * ROWS
    kind = lax.broadcasted_iota(jnp.int32, (CP, TILE), 0)
    total = jnp.zeros((ROWS, CP), F32)
    for lo in range(0, DOM, 8):
        a, b = [], []
        for e in range(lo, lo + 8):
            a.append((paper == train[e : e + 1, :]).astype(BF))
            b.append((kind == slots[e : e + 1, :]).astype(BF))
        total += dot(jnp.concatenate(a, axis=1), jnp.concatenate(b, axis=1), 1, 1)
    out[...] = total


def count_labels(pos, both, shuffle, train):
    def fixed(shape):
        return pl.BlockSpec(shape, lambda i, c: (0, 0))

    tail = pl.BlockSpec((DOM, TILE), lambda i, c: (ROWS // DOM, 0))
    return pl.pallas_call(
        count_kernel,
        grid_spec=pltpu.PrefetchScalarGridSpec(
            num_scalar_prefetch=1,
            grid=(1,),
            in_specs=[tail] * 4 + [fixed((DOM, TILE))] * 2,
            out_specs=fixed((ROWS, CP)),
        ),
        out_shape=struct((ROWS, CP), F32),
        compiler_params=params(24),
        name="count_labels",
        cost_estimate=pl.CostEstimate(
            flops=2 * ROWS * R * CP, bytes_accessed=2 * MIB, transcendentals=0
        ),
    )(pos, *both, shuffle, train)


MLP_ROWS = 256


def slab_of(rep, d):
    return lax.rem(rep + REP - d, REP)


def early_kernel(pos, *refs):
    pieces, (w1, out) = refs[:12], refs[12:]
    total = jnp.zeros((MLP_ROWS, HID), F32)
    for d in range(REP):
        x = jnp.concatenate([pieces[3 * d + h][...] for h in range(HOPS)], axis=1)
        total += dot(x, w1[slab_of(pos[0], d), : HOPS * TILE], 1, 0)
    out[...] = total


def mlp_kernel(pos, *refs):
    pieces, (early, counts, w1, w2, w3, act1, act2, gl, gm, gf) = refs[:4], refs[4:]
    pre1 = early[...]
    for d in range(REP):
        pre1 += dot(pieces[d][...], w1[slab_of(pos[0], d), HOPS * TILE :], 1, 0)
    a1, slope1 = gelu_pair(pre1)
    a1 = a1.astype(BF)
    act1[...] = a1
    a2, slope2 = gelu_pair(dot(a1, w2[...], 1, 0))
    a2 = a2.astype(BF)
    act2[...] = a2
    logits = dot(a2, w3[...], 1, 0)
    kind = lax.broadcasted_iota(jnp.int32, (MLP_ROWS, CP), 1)
    ex = jnp.where(kind < C, jnp.exp(logits), 0.0)
    probs = ex / jnp.sum(ex, axis=1, keepdims=True)
    drawn = counts[...]
    many = jnp.sum(drawn, axis=1, keepdims=True)
    g3 = ((probs * many - drawn) * (1.0 / math.sqrt(N_TRAIN))).astype(BF)
    gl[...] = g3
    g2 = (dot(g3, w3[...], 1, 1) * slope2).astype(BF)
    gm[...] = g2
    gf[...] = (dot(g2, w2[...], 1, 1) * slope1).astype(BF)


def fixed_block(shape):
    return pl.BlockSpec(shape, lambda i, c: (0,) * len(shape))


def row_block(width):
    return pl.BlockSpec((MLP_ROWS, width), lambda i, c: (i, 0))


def first_layer_early(pos, pieces, w1):
    return pl.pallas_call(
        early_kernel,
        grid_spec=pltpu.PrefetchScalarGridSpec(
            num_scalar_prefetch=1,
            grid=(ROWS // MLP_ROWS,),
            in_specs=[row_block(TILE)] * 12 + [fixed_block(w1.shape)],
            out_specs=row_block(HID),
        ),
        out_shape=struct((ROWS, HID), F32),
        compiler_params=params(20),
        name="first_layer_early",
        cost_estimate=pl.CostEstimate(
            flops=2 * ROWS * HID * 3 * 512, bytes_accessed=11 * MIB, transcendentals=0
        ),
    )(pos, *pieces, w1)


def mlp(pos, pieces, early, counts, w1, w2, w3):
    widths = (HID, HID, CP, HID, HID)
    return pl.pallas_call(
        mlp_kernel,
        grid_spec=pltpu.PrefetchScalarGridSpec(
            num_scalar_prefetch=1,
            grid=(ROWS // MLP_ROWS,),
            in_specs=[row_block(TILE)] * 4
            + [row_block(HID), row_block(CP)]
            + [fixed_block(w.shape) for w in (w1, w2, w3)],
            out_specs=[row_block(w) for w in widths],
        ),
        out_shape=[struct((ROWS, w)) for w in widths],
        compiler_params=params(36),
        name="mlp",
        cost_estimate=pl.CostEstimate(
            flops=2 * ROWS * HID * (2 * HID + 512 + 2 * CP),
            bytes_accessed=20 * MIB,
            transcendentals=2 * ROWS * HID,
        ),
    )(pos, *pieces, early, counts, w1, w2, w3)


WIDE = (HID + CP) // 2
SIDE = 16


def outer_kernel(pos, act1, act2, gl, gm, keep, send):
    own = pos[1] == 0
    width = HID // Y
    for k in range(Y):
        at = pl.multiple_of(lax.rem(pos[3] + k, Y) * width, width)
        mid = dot(act1[:, pl.ds(at, width)], gm[...], 0, 0)
        out = dot(act2[:, pl.ds(at, width)], gl[...], 0, 0)
        both = jnp.concatenate([mid, out], axis=1).reshape(X, CORE, REP, 8, HID + CP)
        both = jnp.concatenate([both[..., :WIDE], both[..., WIDE:]], axis=3)
        zero, one = both[:, 0], both[:, 1]
        shape = (SIDE, 16, WIDE)
        keep[k] = jnp.where(own, zero, one).astype(BF).reshape(shape)
        send[k] = jnp.where(own, one, zero).astype(BF).reshape(shape)


def outer_grads(pos, act1, act2, gl, gm):
    return pl.pallas_call(
        outer_kernel,
        in_specs=[whole(pltpu.SMEM)] + [whole()] * 4,
        out_specs=[whole()] * 2,
        out_shape=[struct((Y, SIDE, 16, WIDE))] * 2,
        compiler_params=params(30),
        name="outer_grads",
        cost_estimate=pl.CostEstimate(
            flops=2 * ROWS * HID * (HID + CP), bytes_accessed=8 * MIB, transcendentals=0
        ),
    )(pos, act1, act2, gl, gm)


def first_kernel(pos, *refs):
    pieces, (gf, keep, send) = refs[:16], refs[16:]
    own = pos[1] == 0
    for k in range(REP):
        d = (REP - k) % REP
        for y in range(0, Y, 2):
            two = [pieces[4 * u + d][:ROWS] for u in (y, y + 1)]
            x = jnp.concatenate(two, axis=1)
            got = dot(x, gf[...], 0, 0).reshape(2 * X, CORE, 16, HID)
            zero, one = got[:, 0], got[:, 1]
            here = slice(y * X, (y + 2) * X)
            keep[k, here] = jnp.where(own, zero, one).astype(BF)
            send[k, here] = jnp.where(own, one, zero).astype(BF)


def first_grads(pos, pieces, gf):
    return pl.pallas_call(
        first_kernel,
        in_specs=[whole(pltpu.SMEM)] + [whole()] * 17,
        out_specs=[whole()] * 2,
        out_shape=[struct((REP, SIDE, 16, HID))] * 2,
        compiler_params=params(36),
        name="first_grads",
        cost_estimate=pl.CostEstimate(
            flops=4 * ROWS * HID * HID, bytes_accessed=10 * MIB, transcendentals=0
        ),
    )(pos, *pieces, gf)


def plus(*values):
    return sum(v.astype(F32) for v in values)


def cores_kernel(keep, got, p0, p1, p3, ahead, behind):
    half = SIDE // 2
    p0[...] = plus(keep[0], got[0]).astype(BF)
    p1[...] = plus(keep[1], got[1]).astype(BF)
    p3[...] = plus(keep[3], got[3]).astype(BF)
    ahead[...] = plus(keep[2, :half], got[2, :half]).astype(BF)
    behind[...] = plus(keep[2, half:], got[2, half:]).astype(BF)


def near_kernel(p1, p3, ahead, behind, q1, q3):
    half = SIDE // 2
    q1[:half] = plus(p1[:half], ahead[...]).astype(BF)
    q1[half:] = p1[half:]
    q3[:half] = p3[:half]
    q3[half:] = plus(p3[half:], behind[...]).astype(BF)


def own_kernel(p0, r1, r3, out):
    out[...] = plus(p0[...], r1[...], r3[...]).astype(BF)


def small(kernel, outs, name, *args):
    moved = sum(a.size for a in args) * 2
    return pl.pallas_call(
        kernel,
        in_specs=[whole()] * len(args),
        out_specs=[whole()] * len(outs),
        out_shape=[struct(s) for s in outs],
        compiler_params=params(14),
        name=name,
        cost_estimate=pl.CostEstimate(
            flops=moved, bytes_accessed=2 * moved, transcendentals=0
        ),
    )(*args)


def reduce_ring(keep, send, axis, tag):
    full = keep.shape[1:]
    half = (SIDE // 2,) + full[1:]
    got = shift(send, "core", 1)
    outs = [full, full, full, half, half]
    p0, p1, p3, ahead, behind = small(cores_kernel, outs, "cores_" + tag, keep, got)
    ahead, behind = shift(ahead, axis, 1), shift(behind, axis, 3)
    q1, q3 = small(near_kernel, [full, full], "near_" + tag, p1, p3, ahead, behind)
    r1, r3 = shift(q1, axis, 1), shift(q3, axis, 3)
    return small(own_kernel, [full], "own_" + tag, p0, r1, r3)[0]


def total_kernel(part_f, part_m, first, mid, out):
    first[0] = jnp.sum(part_f[...].astype(F32), axis=0)
    total = jnp.sum(part_m[...].astype(F32), axis=0)
    rest = jnp.concatenate([total[:8], total[8:]], axis=1)
    mid[...] = rest[:, :HID]
    out[...] = rest[:, HID : HID + C]


def total_grads(part_f, part_m):
    return pl.pallas_call(
        total_kernel,
        in_specs=[whole()] * 2,
        out_specs=[whole()] * 3,
        out_shape=[struct((1, 16, HID), F32), struct((8, HID), F32), struct((8, C), F32)],
        compiler_params=params(12),
        name="total_grads",
    )(part_f, part_m)


def shift(value, axis, by):
    size = lax.axis_size(axis)
    return lax.ppermute(value, axis, [(i, (i + by) % size) for i in range(size)])


def swap(value, axes):
    return lax.all_to_all(value, axes, split_axis=0, concat_axis=0, tiled=True)


def exchange(quarters):
    return [quarters[0]] + [shift(quarters[d], "rep", d) for d in (1, 2, 3)]


def per_device(
    features,
    tile_values,
    tile_columns,
    boundary_rows,
    train_rows,
    shuffle,
    labels,
    first_weight,
    mid_weight,
    out_weight,
):
    y, x, core, rep = (lax.axis_index(a) for a in ("y", "x", "core", "rep"))
    pos = jnp.stack([rep, core, lax.rem(rep + REP - y, REP), y]).astype(jnp.int32)

    part = tile_columns - NB
    halo_at = NB + (part + core) % CORE * (NB // CORE) + part // CORE
    cols = jnp.where(tile_columns < NB, tile_columns, halo_at).reshape(-1)
    inner = lax.rem((y * X + x) * CORE + core, DOM // REP)
    cols = jnp.concatenate([cols, jnp.stack([rep, core, inner])]).astype(jnp.int32)
    brow = boundary_rows.reshape(TILE, 1)

    export, *quarters = export_first(pos, features, brow, labels.reshape(8, TILE))
    hop, pieces, counts = features, [], None
    for h in range(HOPS):
        got = exchange(quarters)
        if h == HOPS - 1:
            counts = count_labels(
                pos, pieces[1], shuffle.reshape(DOM, TILE), train_rows.reshape(DOM, TILE)
            )
        near, got, counts = lax.optimization_barrier((swap(export, ("y", "x")), got, counts))
        far = shift(near, "core", 1)
        pieces.append(got)
        made = propagate(h, cols, tile_values, hop, near, far, brow)
        hop, export, quarters = made[0], made[1], made[-4:]
    early = first_layer_early(
        pos, [pieces[h][d] for d in range(REP) for h in range(HOPS)], first_weight
    )
    pieces.append(exchange(quarters))

    w3 = jnp.pad(out_weight, ((0, 0), (0, CP - C)))
    act1, act2, gl, gm, gf = mlp(
        pos, pieces[3], early, counts, first_weight, mid_weight, w3
    )
    pieces = [v for got in pieces for v in got]
    keep_m, send_m = outer_grads(pos, act1, act2, gl, gm)
    keep_m, send_m, gf = lax.optimization_barrier((keep_m, send_m, gf))
    part_m = reduce_ring(keep_m, send_m, "y", "middle")
    part_m = swap(part_m, ("x", "rep"))
    part_f = reduce_ring(*first_grads(pos, pieces, gf), "rep", "first")
    part_f = swap(part_f, ("y", "x"))
    first, mid, out = total_grads(part_f, part_m)
    return first, mid, out


def solution(mesh):
    fine = Mesh(mesh.devices.reshape(Y, X, CORE, REP), ("y", "x", "core", "rep"))
    dom = ("y", "x", "core")
    every = dom + ("rep",)
    placed = (
        P(dom, "rep"),
        P(dom, None, None, None),
        P(dom, None),
        P(dom, None),
        P(dom, None),
        P(dom, None),
        P(every),
        P(),
        P(),
        P(),
    )
    return jax.shard_map(
        per_device,
        mesh=fine,
        in_specs=placed,
        out_specs=(P("rep", dom, None), P(every, None), P(every, None)),
        check_vma=False,
    )
```

```python
import functools
import math

import jax
import jax.numpy as jnp
from jax import lax
from jax.experimental import pallas as pl
from jax.experimental.pallas import tpu as pltpu
from jax.sharding import Mesh, PartitionSpec as P

HOPS = 3
TILE = 128
NB = 32
K = 8
R = 4096
HID = 1024
C = 153
CP = 256
Y, X, CORE, REP = 4, 4, 2, 4
DOM = Y * X * CORE
ROWS = R // REP
N_TRAIN = DOM * R
BF = jnp.bfloat16
F32 = jnp.float32
LAB = 16
MIB = 2**20

root_two_pi = 0.7978845608028654
cubic_term = 0.044715


def gelu_pair(v):
    sq = v * v
    t = jnp.tanh(root_two_pi * (v + cubic_term * sq * v))
    half = 0.5 * (1.0 + t)
    slope = half + (0.5 * root_two_pi) * v * (1.0 - t * t) * (
        1.0 + (3.0 * cubic_term) * sq
    )
    return v * half, slope


def dot(a, b, ca, cb):
    return lax.dot_general(a, b, (((ca,), (cb,)), ((), ())), preferred_element_type=F32)


def params(mib):
    return pltpu.CompilerParams(vmem_limit_bytes=mib * MIB)


def whole(memory_space=pltpu.VMEM):
    return pl.BlockSpec(memory_space=memory_space)


def struct(shape, dtype=BF):
    return jax.ShapeDtypeStruct(shape, dtype)


def export_rows(hop, brow):
    here = lax.broadcasted_iota(jnp.int32, (TILE, TILE), 0)
    there = lax.broadcasted_iota(jnp.int32, (TILE, TILE), 1)
    column = jnp.sum(jnp.where(here == there, brow[...], 0), axis=1, keepdims=True)
    row = lax.broadcasted_iota(jnp.int32, (TILE, R), 1)
    return dot((row == column).astype(BF), hop[...], 1, 0).astype(BF)


def take_quarters(rep, hop, quarters):
    for d, q in enumerate(quarters):
        start = pl.multiple_of(lax.rem(rep + d, REP) * ROWS, ROWS)
        q[:ROWS] = hop[pl.ds(start, ROWS), :]


def export_kernel(pos, hop, brow, labels, export, *quarters):
    got = export_rows(hop, brow)
    extra = jnp.concatenate([labels[...].astype(F32), jnp.zeros((8, TILE), F32)])
    extra = extra.astype(BF)
    for t in range(Y * X):
        export[t, :TILE] = got
        export[t, TILE:] = extra
    take_quarters(pos[0], hop, quarters)


def export_first(pos, hop, brow, labels):
    return pl.pallas_call(
        export_kernel,
        in_specs=[whole(pltpu.SMEM)] + [whole()] * 3,
        out_specs=[whole()] * 5,
        out_shape=[struct((Y * X, TILE + LAB, TILE))] + [struct((ROWS, TILE))] * 4,
        compiler_params=params(16),
        name="export_first",
        cost_estimate=pl.CostEstimate(
            flops=2 * TILE * TILE * R, bytes_accessed=2 * MIB, transcendentals=0
        ),
    )(pos, hop, brow, labels)


CUTS = 8
STEP = NB // CUTS


def prop_kernel(h, cols, tiles, hop, near, far, brow, *rest):
    last = h == HOPS - 1
    if last:
        q0, q1, q2, q3, joined, held, sem, out = rest
    else:
        out, export, q0, q1, q2, q3, joined, held, sem = rest
    r, core, inner = cols[NB * K], cols[NB * K + 1], cols[NB * K + 2]
    copies = [
        pltpu.make_async_copy(
            tiles.at[pl.ds(c * STEP, STEP)], held.at[pl.ds(c * STEP, STEP)], sem.at[c]
        )
        for c in range(CUTS)
    ]
    for copy in copies:
        copy.start()
    joined[:R] = hop[...]
    for t in range(Y * X):
        at = R + t * TILE
        joined[at : at + TILE] = near[t, :TILE]
        joined[at + R // 2 : at + R // 2 + TILE] = far[t, :TILE]
    for b in range(NB):
        if b % STEP == 0:
            copies[b // STEP].wait()
        parts = []
        for k in range(K):
            at = pl.multiple_of(cols[b * K + k] * TILE, TILE)
            parts.append(joined[pl.ds(at, TILE), :])
        left = jnp.concatenate([held[b, k] for k in range(K)], axis=1)
        got = dot(left, jnp.concatenate(parts, axis=0), 1, 0)
        out[b * TILE : (b + 1) * TILE, :] = got.astype(BF)

    if not last:
        got = export_rows(out, brow)
        for t in range(Y * X):
            export[t] = got
    quarters = (q0, q1, q2, q3)
    take_quarters(r, out, quarters)
    if h == 0:
        pick = lax.broadcasted_iota(jnp.int32, (LAB, TILE), 0) == inner
        labs = []
        for t in range(Y * X):
            two = [
                jnp.sum(jnp.where(pick, v[t, TILE:].astype(F32), 0.0), axis=0, keepdims=True)
                for v in (near, far)
            ]
            labs.append(jnp.where(core == 0, two[0], two[1]))
            labs.append(jnp.where(core == 0, two[1], two[0]))
        labs = jnp.concatenate(labs, axis=0).astype(BF)
        for q in quarters:
            q[ROWS:] = labs


def propagate(h, cols, tiles, hop, near, far, brow):
    last = h == HOPS - 1
    outs = [] if last else [(R, TILE), (Y * X, TILE, TILE)]
    outs += [(ROWS + DOM if h == 0 else ROWS, TILE)] * 4
    scratch = [
        pltpu.VMEM((2 * R, TILE), BF),
        pltpu.VMEM((NB, K, TILE, TILE), BF),
        pltpu.SemaphoreType.DMA((CUTS,)),
    ]
    scratch += [pltpu.VMEM((R, TILE), BF)] if last else []
    return pl.pallas_call(
        functools.partial(prop_kernel, h),
        in_specs=[whole(pltpu.SMEM), whole(pltpu.HBM)] + [whole()] * 4,
        out_specs=[whole()] * len(outs),
        scratch_shapes=scratch,
        out_shape=[struct(s) for s in outs],
        compiler_params=params(54),
        name="propagate_" + str(h),
        cost_estimate=pl.CostEstimate(
            flops=2 * NB * K * TILE**3, bytes_accessed=12 * MIB, transcendentals=0
        ),
    )(cols, tiles, hop, near, far, brow)


def count_kernel(pos, lab0, lab1, lab2, lab3, shuffle, train, out):
    labels = jnp.zeros((DOM, TILE), F32)
    for d, v in enumerate((lab0, lab1, lab2, lab3)):
        labels = jnp.where(pos[2] == d, v[...].astype(F32), labels)
    first = lax.broadcasted_iota(jnp.int32, (DOM, TILE), 0)
    second = lax.broadcasted_iota(jnp.int32, (TILE, TILE), 0)
    slots = jnp.zeros((DOM, TILE), F32)
    for lo in range(0, DOM, 8):
        a, b = [], []
        for e in range(lo, lo + 8):
            slot = shuffle[e : e + 1, :]
            label = labels[e : e + 1, :]
            a.append(jnp.where(first == slot // TILE, label, 0.0).astype(BF))
            b.append((second == lax.rem(slot, TILE)).astype(BF))
        slots += dot(jnp.concatenate(a, axis=1), jnp.concatenate(b, axis=1), 1, 1)
    slots = slots.astype(jnp.int32)
    paper = lax.broadcasted_iota(jnp.int32, (ROWS, TILE), 0) + pos[0] * ROWS
    kind = lax.broadcasted_iota(jnp.int32, (CP, TILE), 0)
    total = jnp.zeros((ROWS, CP), F32)
    for lo in range(0, DOM, 8):
        a, b = [], []
        for e in range(lo, lo + 8):
            a.append((paper == train[e : e + 1, :]).astype(BF))
            b.append((kind == slots[e : e + 1, :]).astype(BF))
        total += dot(jnp.concatenate(a, axis=1), jnp.concatenate(b, axis=1), 1, 1)
    out[...] = total


def count_labels(pos, both, shuffle, train):
    def fixed(shape):
        return pl.BlockSpec(shape, lambda i, c: (0, 0))

    tail = pl.BlockSpec((DOM, TILE), lambda i, c: (ROWS // DOM, 0))
    return pl.pallas_call(
        count_kernel,
        grid_spec=pltpu.PrefetchScalarGridSpec(
            num_scalar_prefetch=1,
            grid=(1,),
            in_specs=[tail] * 4 + [fixed((DOM, TILE))] * 2,
            out_specs=fixed((ROWS, CP)),
        ),
        out_shape=struct((ROWS, CP), F32),
        compiler_params=params(24),
        name="count_labels",
        cost_estimate=pl.CostEstimate(
            flops=2 * ROWS * R * CP, bytes_accessed=2 * MIB, transcendentals=0
        ),
    )(pos, *both, shuffle, train)


MLP_ROWS = 256


def slab_of(rep, d):
    return lax.rem(rep + REP - d, REP)


def early_kernel(pos, *refs):
    pieces, (w1, out) = refs[:12], refs[12:]
    total = jnp.zeros((MLP_ROWS, HID), F32)
    for d in range(REP):
        x = jnp.concatenate([pieces[3 * d + h][...] for h in range(HOPS)], axis=1)
        total += dot(x, w1[slab_of(pos[0], d), : HOPS * TILE], 1, 0)
    out[...] = total


def mlp_kernel(pos, *refs):
    pieces, (early, counts, w1, w2, w3, act1, act2, gl, gm, gf) = refs[:4], refs[4:]
    pre1 = early[...]
    for d in range(REP):
        pre1 += dot(pieces[d][...], w1[slab_of(pos[0], d), HOPS * TILE :], 1, 0)
    a1, slope1 = gelu_pair(pre1)
    a1 = a1.astype(BF)
    act1[...] = a1
    a2, slope2 = gelu_pair(dot(a1, w2[...], 1, 0))
    a2 = a2.astype(BF)
    act2[...] = a2
    logits = dot(a2, w3[...], 1, 0)
    kind = lax.broadcasted_iota(jnp.int32, (MLP_ROWS, CP), 1)
    ex = jnp.where(kind < C, jnp.exp(logits), 0.0)
    probs = ex / jnp.sum(ex, axis=1, keepdims=True)
    drawn = counts[...]
    many = jnp.sum(drawn, axis=1, keepdims=True)
    g3 = ((probs * many - drawn) * (1.0 / math.sqrt(N_TRAIN))).astype(BF)
    gl[...] = g3
    g2 = (dot(g3, w3[...], 1, 1) * slope2).astype(BF)
    gm[...] = g2
    gf[...] = (dot(g2, w2[...], 1, 1) * slope1).astype(BF)


def fixed_block(shape):
    return pl.BlockSpec(shape, lambda i, c: (0,) * len(shape))


def row_block(width):
    return pl.BlockSpec((MLP_ROWS, width), lambda i, c: (i, 0))


def first_layer_early(pos, pieces, w1):
    return pl.pallas_call(
        early_kernel,
        grid_spec=pltpu.PrefetchScalarGridSpec(
            num_scalar_prefetch=1,
            grid=(ROWS // MLP_ROWS,),
            in_specs=[row_block(TILE)] * 12 + [fixed_block(w1.shape)],
            out_specs=row_block(HID),
        ),
        out_shape=struct((ROWS, HID), F32),
        compiler_params=params(20),
        name="first_layer_early",
        cost_estimate=pl.CostEstimate(
            flops=2 * ROWS * HID * 3 * 512, bytes_accessed=11 * MIB, transcendentals=0
        ),
    )(pos, *pieces, w1)


def mlp(pos, pieces, early, counts, w1, w2, w3):
    widths = (HID, HID, CP, HID, HID)
    return pl.pallas_call(
        mlp_kernel,
        grid_spec=pltpu.PrefetchScalarGridSpec(
            num_scalar_prefetch=1,
            grid=(ROWS // MLP_ROWS,),
            in_specs=[row_block(TILE)] * 4
            + [row_block(HID), row_block(CP)]
            + [fixed_block(w.shape) for w in (w1, w2, w3)],
            out_specs=[row_block(w) for w in widths],
        ),
        out_shape=[struct((ROWS, w)) for w in widths],
        compiler_params=params(36),
        name="mlp",
        cost_estimate=pl.CostEstimate(
            flops=2 * ROWS * HID * (2 * HID + 512 + 2 * CP),
            bytes_accessed=20 * MIB,
            transcendentals=2 * ROWS * HID,
        ),
    )(pos, *pieces, early, counts, w1, w2, w3)


WIDE = (HID + CP) // 2
SIDE = 16


def outer_kernel(pos, act1, act2, gl, gm, *outs):
    keep, send = outs[:REP], outs[REP:]
    own = pos[1] == 0
    width = HID // Y
    for y in range(Y):
        cut = slice(y * width, (y + 1) * width)
        mid = dot(act1[:, cut], gm[...], 0, 0)
        out = dot(act2[:, cut], gl[...], 0, 0)
        both = jnp.concatenate([mid, out], axis=1).reshape(X, CORE, REP, 8, HID + CP)
        both = jnp.concatenate([both[..., :WIDE], both[..., WIDE:]], axis=3)
        zero, one = both[:, 0], both[:, 1]
        kept = jnp.where(own, zero, one).astype(BF)
        sent = jnp.where(own, one, zero).astype(BF)
        for z in range(REP):
            k = lax.rem(z + REP - pos[0], REP)
            for at in range(REP):

                @pl.when(k == at)
                def _():
                    keep[at][y * X : (y + 1) * X] = kept[:, z]
                    send[at][y * X : (y + 1) * X] = sent[:, z]


def outer_grads(pos, act1, act2, gl, gm):
    return pl.pallas_call(
        outer_kernel,
        in_specs=[whole(pltpu.SMEM)] + [whole()] * 4,
        out_specs=[whole()] * (2 * REP),
        out_shape=[struct((SIDE, 16, WIDE))] * (2 * REP),
        compiler_params=params(30),
        name="outer_grads",
        cost_estimate=pl.CostEstimate(
            flops=2 * ROWS * HID * (HID + CP), bytes_accessed=8 * MIB, transcendentals=0
        ),
    )(pos, act1, act2, gl, gm)


def first_kernel(steps, pos, *refs):
    n = (HOPS + 1) * len(steps)
    pieces, gf, outs = refs[:n], refs[n], refs[n + 1 :]
    keep, send = outs[: len(steps)], outs[len(steps) :]
    own = pos[1] == 0
    for at in range(len(steps)):
        for y in range(0, Y, 2):
            two = [pieces[at * (HOPS + 1) + u][:ROWS] for u in (y, y + 1)]
            x = jnp.concatenate(two, axis=1)
            got = dot(x, gf[...], 0, 0).reshape(2 * X, CORE, 16, HID)
            zero, one = got[:, 0], got[:, 1]
            here = slice(y * X, (y + 2) * X)
            keep[at][here] = jnp.where(own, zero, one).astype(BF)
            send[at][here] = jnp.where(own, one, zero).astype(BF)


def first_grads(pos, pieces, gf, steps):
    used = [pieces[h][(REP - k) % REP] for k in steps for h in range(HOPS + 1)]
    return pl.pallas_call(
        functools.partial(first_kernel, steps),
        in_specs=[whole(pltpu.SMEM)] + [whole()] * (len(used) + 1),
        out_specs=[whole()] * (2 * len(steps)),
        out_shape=[struct((SIDE, 16, HID))] * (2 * len(steps)),
        compiler_params=params(24),
        name="first_grads_" + "".join(str(k) for k in steps),
        cost_estimate=pl.CostEstimate(
            flops=len(steps) * ROWS * HID * HID, bytes_accessed=6 * MIB, transcendentals=0
        ),
    )(pos, *used, gf)


def plus(*values):
    return sum(v.astype(F32) for v in values)


def cores_far_kernel(keep, got, ahead, behind):
    half = SIDE // 2
    ahead[...] = plus(keep[:half], got[:half]).astype(BF)
    behind[...] = plus(keep[half:], got[half:]).astype(BF)


def near_kernel(k1, g1, k3, g3, ahead, behind, q1, q3):
    half = SIDE // 2
    q1[:half] = plus(k1[:half], g1[:half], ahead[...]).astype(BF)
    q1[half:] = plus(k1[half:], g1[half:]).astype(BF)
    q3[:half] = plus(k3[:half], g3[:half]).astype(BF)
    q3[half:] = plus(k3[half:], g3[half:], behind[...]).astype(BF)


def own_kernel(kf, gf, rf1, rf3, km, gm, rm1, rm3, out):
    out[:, :, :HID] = plus(kf[...], gf[...], rf1[...], rf3[...]).astype(BF)
    out[:, :, HID:] = plus(km[...], gm[...], rm1[...], rm3[...]).astype(BF)


def small(kernel, outs, name, *args):
    moved = sum(a.size for a in args) * 2
    return pl.pallas_call(
        kernel,
        in_specs=[whole()] * len(args),
        out_specs=[whole()] * len(outs),
        out_shape=[struct(s) for s in outs],
        compiler_params=params(14),
        name=name,
        cost_estimate=pl.CostEstimate(
            flops=moved, bytes_accessed=2 * moved, transcendentals=0
        ),
    )(*args)


def send_far(keep, got, tag):
    half = (SIDE // 2,) + keep.shape[1:]
    ahead, behind = small(cores_far_kernel, [half, half], "far_" + tag, keep, got)
    return shift(ahead, "rep", 1), shift(behind, "rep", 3)


def send_near(k1, g1, k3, g3, far, tag):
    q1, q3 = small(near_kernel, [k1.shape] * 2, "near_" + tag, k1, g1, k3, g3, *far)
    return shift(q1, "rep", 1), shift(q3, "rep", 3)


def total_kernel(parts, first, mid, out):
    total = jnp.sum(parts[...].astype(F32), axis=0)
    first[0] = total[:, :HID]
    rest = jnp.concatenate([total[:8, HID:], total[8:, HID:]], axis=1)
    mid[...] = rest[:, :HID]
    out[...] = rest[:, HID : HID + C]


def total_grads(parts):
    return pl.pallas_call(
        total_kernel,
        in_specs=[whole()],
        out_specs=[whole()] * 3,
        out_shape=[struct((1, 16, HID), F32), struct((8, HID), F32), struct((8, C), F32)],
        compiler_params=params(12),
        name="total_grads",
    )(parts)


def shift(value, axis, by):
    size = lax.axis_size(axis)
    return lax.ppermute(value, axis, [(i, (i + by) % size) for i in range(size)])


def swap(value, axes):
    return lax.all_to_all(value, axes, split_axis=0, concat_axis=0, tiled=True)


def exchange(quarters):
    return [quarters[0]] + [shift(quarters[d], "rep", d) for d in (1, 2, 3)]


def per_device(
    features,
    tile_values,
    tile_columns,
    boundary_rows,
    train_rows,
    shuffle,
    labels,
    first_weight,
    mid_weight,
    out_weight,
):
    y, x, core, rep = (lax.axis_index(a) for a in ("y", "x", "core", "rep"))
    pos = jnp.stack([rep, core, lax.rem(rep + REP - y, REP), y]).astype(jnp.int32)

    part = tile_columns - NB
    halo_at = NB + (part + core) % CORE * (NB // CORE) + part // CORE
    cols = jnp.where(tile_columns < NB, tile_columns, halo_at).reshape(-1)
    inner = lax.rem((y * X + x) * CORE + core, DOM // REP)
    cols = jnp.concatenate([cols, jnp.stack([rep, core, inner])]).astype(jnp.int32)
    brow = boundary_rows

    export, *quarters = export_first(pos, features, brow, labels.reshape(8, TILE))
    hop, pieces, counts = features, [], None
    for h in range(HOPS):
        got = exchange(quarters)
        if h == HOPS - 1:
            counts = count_labels(
                pos, pieces[1], shuffle.reshape(DOM, TILE), train_rows.reshape(DOM, TILE)
            )
        near, got[1], got[3], counts = lax.optimization_barrier(
            (swap(export, ("y", "x")), got[1], got[3], counts)
        )
        far = shift(near, "core", 1)
        pieces.append(got)
        made = propagate(h, cols, tile_values, hop, near, far, brow)
        made, got[2] = lax.optimization_barrier((made, got[2]))
        hop, export, quarters = made[0], made[1], made[-4:]
    early = first_layer_early(
        pos, [pieces[h][d] for d in range(REP) for h in range(HOPS)], first_weight
    )
    pieces.append(exchange(quarters))

    w3 = jnp.pad(out_weight, ((0, 0), (0, CP - C)))
    act1, act2, gl, gm, gf = mlp(
        pos, pieces[3], early, counts, first_weight, mid_weight, w3
    )
    made = outer_grads(pos, act1, act2, gl, gm)
    km, gm = made[:REP], [shift(v, "core", 1) for v in made[REP:]]
    k2, s2 = first_grads(pos, pieces, gf, (2,))
    g2 = shift(s2, "core", 1)
    gm, gf = lax.optimization_barrier((gm, gf))
    far_m = send_far(km[2], gm[2], "middle")
    k1, k3, s1, s3 = first_grads(pos, pieces, gf, (1, 3))
    g1, g3 = shift(s1, "core", 1), shift(s3, "core", 1)
    g2, far_m, gf = lax.optimization_barrier((g2, far_m, gf))
    far_f = send_far(k2, g2, "first")
    k0, s0 = first_grads(pos, pieces, gf, (0,))
    g0 = shift(s0, "core", 1)
    near_m = send_near(km[1], gm[1], km[3], gm[3], far_m, "middle")
    near_f = send_near(k1, g1, k3, g3, far_f, "first")
    shape = (SIDE, 16, HID + WIDE)
    args = (k0, g0, *near_f, km[0], gm[0], *near_m)
    parts = small(own_kernel, [shape], "own_share", *args)[0]
    first, mid, out = total_grads(swap(parts, ("y", "x")))
    return first, mid, out


def solution(mesh):
    fine = Mesh(mesh.devices.reshape(Y, X, CORE, REP), ("y", "x", "core", "rep"))
    dom = ("y", "x", "core")
    every = dom + ("rep",)
    placed = (
        P(dom, "rep"),
        P(dom, None, None, None),
        P(dom, None),
        P(dom, None),
        P(dom, None),
        P(dom, None),
        P(every),
        P(),
        P(),
        P(),
    )
    return jax.shard_map(
        per_device,
        mesh=fine,
        in_specs=placed,
        out_specs=(P("rep", dom, None), P(every, None), P(every, None)),
        check_vma=False,
    )
```

```python
import functools
import math

import jax
import jax.numpy as jnp
from jax import lax
from jax.experimental import pallas as pl
from jax.experimental.pallas import tpu as pltpu
from jax.sharding import Mesh, PartitionSpec as P

HOPS = 3
TILE = 128
NB = 32
K = 8
R = 4096
HID = 1024
C = 153
CP = 256
Y, X, CORE, REP = 4, 4, 2, 4
DOM = Y * X * CORE
ROWS = R // REP
N_TRAIN = DOM * R
BF = jnp.bfloat16
F32 = jnp.float32
LAB = 16
MIB = 2**20

root_two_pi = 0.7978845608028654
cubic_term = 0.044715


def gelu_pair(v):
    sq = v * v
    t = jnp.tanh(root_two_pi * (v + cubic_term * sq * v))
    half = 0.5 * (1.0 + t)
    slope = half + (0.5 * root_two_pi) * v * (1.0 - t * t) * (
        1.0 + (3.0 * cubic_term) * sq
    )
    return v * half, slope


def dot(a, b, ca, cb):
    return lax.dot_general(a, b, (((ca,), (cb,)), ((), ())), preferred_element_type=F32)


def params(mib):
    return pltpu.CompilerParams(vmem_limit_bytes=mib * MIB)


def whole(memory_space=pltpu.VMEM):
    return pl.BlockSpec(memory_space=memory_space)


def struct(shape, dtype=BF):
    return jax.ShapeDtypeStruct(shape, dtype)


def export_rows(hop, brow):
    here = lax.broadcasted_iota(jnp.int32, (TILE, TILE), 0)
    there = lax.broadcasted_iota(jnp.int32, (TILE, TILE), 1)
    column = jnp.sum(jnp.where(here == there, brow[...], 0), axis=1, keepdims=True)
    row = lax.broadcasted_iota(jnp.int32, (TILE, R), 1)
    return dot((row == column).astype(BF), hop[...], 1, 0).astype(BF)


def take_quarters(rep, hop, quarters):
    for d, q in enumerate(quarters):
        start = pl.multiple_of(lax.rem(rep + d, REP) * ROWS, ROWS)
        q[:ROWS] = hop[pl.ds(start, ROWS), :]


def export_kernel(pos, hop, brow, labels, export, *quarters):
    got = export_rows(hop, brow)
    extra = jnp.concatenate([labels[...].astype(F32), jnp.zeros((8, TILE), F32)])
    extra = extra.astype(BF)
    for t in range(Y * X):
        export[t, :TILE] = got
        export[t, TILE:] = extra
    take_quarters(pos[0], hop, quarters)


def export_first(pos, hop, brow, labels):
    return pl.pallas_call(
        export_kernel,
        in_specs=[whole(pltpu.SMEM)] + [whole()] * 3,
        out_specs=[whole()] * 5,
        out_shape=[struct((Y * X, TILE + LAB, TILE))] + [struct((ROWS, TILE))] * 4,
        compiler_params=params(16),
        name="export_first",
        cost_estimate=pl.CostEstimate(
            flops=2 * TILE * TILE * R, bytes_accessed=2 * MIB, transcendentals=0
        ),
    )(pos, hop, brow, labels)


CUTS = 8
STEP = NB // CUTS


def prop_kernel(h, cols, tiles, hop, near, far, brow, *rest):
    last = h == HOPS - 1
    if last:
        q0, q1, q2, q3, joined, held, sem, out = rest
    else:
        out, export, q0, q1, q2, q3, joined, held, sem = rest
    r, core, inner = cols[NB * K], cols[NB * K + 1], cols[NB * K + 2]
    copies = [
        pltpu.make_async_copy(
            tiles.at[pl.ds(c * STEP, STEP)], held.at[pl.ds(c * STEP, STEP)], sem.at[c]
        )
        for c in range(CUTS)
    ]
    for copy in copies:
        copy.start()
    joined[:R] = hop[...]
    for t in range(Y * X):
        at = R + t * TILE
        joined[at : at + TILE] = near[t, :TILE]
        joined[at + R // 2 : at + R // 2 + TILE] = far[t, :TILE]
    for b in range(NB):
        if b % STEP == 0:
            copies[b // STEP].wait()
        parts = []
        for k in range(K):
            at = pl.multiple_of(cols[b * K + k] * TILE, TILE)
            parts.append(joined[pl.ds(at, TILE), :])
        left = jnp.concatenate([held[b, k] for k in range(K)], axis=1)
        got = dot(left, jnp.concatenate(parts, axis=0), 1, 0)
        out[b * TILE : (b + 1) * TILE, :] = got.astype(BF)

    if not last:
        got = export_rows(out, brow)
        for t in range(Y * X):
            export[t] = got
    quarters = (q0, q1, q2, q3)
    take_quarters(r, out, quarters)
    if h == 0:
        pick = lax.broadcasted_iota(jnp.int32, (LAB, TILE), 0) == inner
        labs = []
        for t in range(Y * X):
            two = [
                jnp.sum(jnp.where(pick, v[t, TILE:].astype(F32), 0.0), axis=0, keepdims=True)
                for v in (near, far)
            ]
            labs.append(jnp.where(core == 0, two[0], two[1]))
            labs.append(jnp.where(core == 0, two[1], two[0]))
        labs = jnp.concatenate(labs, axis=0).astype(BF)
        for q in quarters:
            q[ROWS:] = labs


def propagate(h, cols, tiles, hop, near, far, brow):
    last = h == HOPS - 1
    outs = [] if last else [(R, TILE), (Y * X, TILE, TILE)]
    outs += [(ROWS + DOM if h == 0 else ROWS, TILE)] * 4
    scratch = [
        pltpu.VMEM((2 * R, TILE), BF),
        pltpu.VMEM((NB, K, TILE, TILE), BF),
        pltpu.SemaphoreType.DMA((CUTS,)),
    ]
    scratch += [pltpu.VMEM((R, TILE), BF)] if last else []
    return pl.pallas_call(
        functools.partial(prop_kernel, h),
        in_specs=[whole(pltpu.SMEM), whole(pltpu.HBM)] + [whole()] * 4,
        out_specs=[whole()] * len(outs),
        scratch_shapes=scratch,
        out_shape=[struct(s) for s in outs],
        compiler_params=params(54),
        name="propagate_" + str(h),
        cost_estimate=pl.CostEstimate(
            flops=2 * NB * K * TILE**3, bytes_accessed=12 * MIB, transcendentals=0
        ),
    )(cols, tiles, hop, near, far, brow)


def count_kernel(pos, lab0, lab1, lab2, lab3, shuffle, train, out):
    labels = jnp.zeros((DOM, TILE), F32)
    for d, v in enumerate((lab0, lab1, lab2, lab3)):
        labels = jnp.where(pos[2] == d, v[...].astype(F32), labels)
    first = lax.broadcasted_iota(jnp.int32, (DOM, TILE), 0)
    second = lax.broadcasted_iota(jnp.int32, (TILE, TILE), 0)
    slots = jnp.zeros((DOM, TILE), F32)
    for lo in range(0, DOM, 8):
        a, b = [], []
        for e in range(lo, lo + 8):
            slot = shuffle[e : e + 1, :]
            label = labels[e : e + 1, :]
            a.append(jnp.where(first == slot // TILE, label, 0.0).astype(BF))
            b.append((second == lax.rem(slot, TILE)).astype(BF))
        slots += dot(jnp.concatenate(a, axis=1), jnp.concatenate(b, axis=1), 1, 1)
    slots = slots.astype(jnp.int32)
    paper = lax.broadcasted_iota(jnp.int32, (ROWS, TILE), 0) + pos[0] * ROWS
    kind = lax.broadcasted_iota(jnp.int32, (CP, TILE), 0)
    total = jnp.zeros((ROWS, CP), F32)
    for lo in range(0, DOM, 8):
        a, b = [], []
        for e in range(lo, lo + 8):
            a.append((paper == train[e : e + 1, :]).astype(BF))
            b.append((kind == slots[e : e + 1, :]).astype(BF))
        total += dot(jnp.concatenate(a, axis=1), jnp.concatenate(b, axis=1), 1, 1)
    out[...] = total


def count_labels(pos, both, shuffle, train):
    def fixed(shape):
        return pl.BlockSpec(shape, lambda i, c: (0, 0))

    tail = pl.BlockSpec((DOM, TILE), lambda i, c: (ROWS // DOM, 0))
    return pl.pallas_call(
        count_kernel,
        grid_spec=pltpu.PrefetchScalarGridSpec(
            num_scalar_prefetch=1,
            grid=(1,),
            in_specs=[tail] * 4 + [fixed((DOM, TILE))] * 2,
            out_specs=fixed((ROWS, CP)),
        ),
        out_shape=struct((ROWS, CP), F32),
        compiler_params=params(24),
        name="count_labels",
        cost_estimate=pl.CostEstimate(
            flops=2 * ROWS * R * CP, bytes_accessed=2 * MIB, transcendentals=0
        ),
    )(pos, *both, shuffle, train)


MLP_ROWS = 256


def slab_of(rep, d):
    return lax.rem(rep + REP - d, REP)


def early_kernel(pos, *refs):
    pieces, (w1, out) = refs[:12], refs[12:]
    total = jnp.zeros((MLP_ROWS, HID), F32)
    for d in range(REP):
        x = jnp.concatenate([pieces[3 * d + h][...] for h in range(HOPS)], axis=1)
        total += dot(x, w1[slab_of(pos[0], d), : HOPS * TILE], 1, 0)
    out[...] = total


def mlp_kernel(pos, *refs):
    pieces, (early, counts, w1, w2, w3, act1, act2, gl, gm, gf) = refs[:4], refs[4:]
    pre1 = early[...]
    for d in range(REP):
        pre1 += dot(pieces[d][...], w1[slab_of(pos[0], d), HOPS * TILE :], 1, 0)
    a1, slope1 = gelu_pair(pre1)
    a1 = a1.astype(BF)
    act1[...] = a1
    a2, slope2 = gelu_pair(dot(a1, w2[...], 1, 0))
    a2 = a2.astype(BF)
    act2[...] = a2
    logits = dot(a2, w3[...], 1, 0)
    kind = lax.broadcasted_iota(jnp.int32, (MLP_ROWS, CP), 1)
    ex = jnp.where(kind < C, jnp.exp(logits), 0.0)
    probs = ex / jnp.sum(ex, axis=1, keepdims=True)
    drawn = counts[...]
    many = jnp.sum(drawn, axis=1, keepdims=True)
    g3 = ((probs * many - drawn) * (1.0 / math.sqrt(N_TRAIN))).astype(BF)
    gl[...] = g3
    g2 = (dot(g3, w3[...], 1, 1) * slope2).astype(BF)
    gm[...] = g2
    gf[...] = (dot(g2, w2[...], 1, 1) * slope1).astype(BF)


def fixed_block(shape):
    return pl.BlockSpec(shape, lambda i, c: (0,) * len(shape))


def row_block(width):
    return pl.BlockSpec((MLP_ROWS, width), lambda i, c: (i, 0))


def first_layer_early(pos, pieces, w1):
    return pl.pallas_call(
        early_kernel,
        grid_spec=pltpu.PrefetchScalarGridSpec(
            num_scalar_prefetch=1,
            grid=(ROWS // MLP_ROWS,),
            in_specs=[row_block(TILE)] * 12 + [fixed_block(w1.shape)],
            out_specs=row_block(HID),
        ),
        out_shape=struct((ROWS, HID), F32),
        compiler_params=params(20),
        name="first_layer_early",
        cost_estimate=pl.CostEstimate(
            flops=2 * ROWS * HID * 3 * 512, bytes_accessed=11 * MIB, transcendentals=0
        ),
    )(pos, *pieces, w1)


def mlp(pos, pieces, early, counts, w1, w2, w3):
    widths = (HID, HID, CP, HID, HID)
    return pl.pallas_call(
        mlp_kernel,
        grid_spec=pltpu.PrefetchScalarGridSpec(
            num_scalar_prefetch=1,
            grid=(ROWS // MLP_ROWS,),
            in_specs=[row_block(TILE)] * 4
            + [row_block(HID), row_block(CP)]
            + [fixed_block(w.shape) for w in (w1, w2, w3)],
            out_specs=[row_block(w) for w in widths],
        ),
        out_shape=[struct((ROWS, w)) for w in widths],
        compiler_params=params(36),
        name="mlp",
        cost_estimate=pl.CostEstimate(
            flops=2 * ROWS * HID * (2 * HID + 512 + 2 * CP),
            bytes_accessed=20 * MIB,
            transcendentals=2 * ROWS * HID,
        ),
    )(pos, *pieces, early, counts, w1, w2, w3)


WIDE = (HID + CP) // 2
SIDE = 16


def outer_kernel(pos, act1, act2, gl, gm, keep, send):
    own = pos[1] == 0
    width = HID // Y
    for k in range(Y):
        at = pl.multiple_of(lax.rem(pos[3] + k, Y) * width, width)
        mid = dot(act1[:, pl.ds(at, width)], gm[...], 0, 0)
        out = dot(act2[:, pl.ds(at, width)], gl[...], 0, 0)
        both = jnp.concatenate([mid, out], axis=1).reshape(X, CORE, REP, 8, HID + CP)
        both = jnp.concatenate([both[..., :WIDE], both[..., WIDE:]], axis=3)
        zero, one = both[:, 0], both[:, 1]
        shape = (SIDE, 16, WIDE)
        keep[k] = jnp.where(own, zero, one).astype(BF).reshape(shape)
        send[k] = jnp.where(own, one, zero).astype(BF).reshape(shape)


def outer_grads(pos, act1, act2, gl, gm):
    return pl.pallas_call(
        outer_kernel,
        in_specs=[whole(pltpu.SMEM)] + [whole()] * 4,
        out_specs=[whole()] * 2,
        out_shape=[struct((Y, SIDE, 16, WIDE))] * 2,
        compiler_params=params(30),
        name="outer_grads",
        cost_estimate=pl.CostEstimate(
            flops=2 * ROWS * HID * (HID + CP), bytes_accessed=8 * MIB, transcendentals=0
        ),
    )(pos, act1, act2, gl, gm)


def first_kernel(steps, pos, *refs):
    n = (HOPS + 1) * len(steps)
    pieces, (gf, keep, send) = refs[:n], refs[n:]
    own = pos[1] == 0
    for at in range(len(steps)):
        for y in range(0, Y, 2):
            two = [pieces[at * (HOPS + 1) + u][:ROWS] for u in (y, y + 1)]
            x = jnp.concatenate(two, axis=1)
            got = dot(x, gf[...], 0, 0).reshape(2 * X, CORE, 16, HID)
            zero, one = got[:, 0], got[:, 1]
            here = slice(y * X, (y + 2) * X)
            keep[at, here] = jnp.where(own, zero, one).astype(BF)
            send[at, here] = jnp.where(own, one, zero).astype(BF)


def first_grads(pos, pieces, gf, steps):
    used = [pieces[h][(REP - k) % REP] for k in steps for h in range(HOPS + 1)]
    return pl.pallas_call(
        functools.partial(first_kernel, steps),
        in_specs=[whole(pltpu.SMEM)] + [whole()] * (len(used) + 1),
        out_specs=[whole()] * 2,
        out_shape=[struct((len(steps), SIDE, 16, HID))] * 2,
        compiler_params=params(24),
        name="first_grads_" + "".join(str(k) for k in steps),
        cost_estimate=pl.CostEstimate(
            flops=len(steps) * ROWS * HID * HID, bytes_accessed=6 * MIB, transcendentals=0
        ),
    )(pos, *used, gf)


def plus(*values):
    return sum(v.astype(F32) for v in values)


def far_kernel(at, keep, got, ahead, behind):
    half = SIDE // 2
    ahead[...] = plus(keep[at, :half], got[at, :half]).astype(BF)
    behind[...] = plus(keep[at, half:], got[at, half:]).astype(BF)


def near_kernel(one, three, keep, got, ahead, behind, q1, q3):
    half = SIDE // 2
    q1[:half] = plus(keep[one, :half], got[one, :half], ahead[...]).astype(BF)
    q1[half:] = plus(keep[one, half:], got[one, half:]).astype(BF)
    q3[:half] = plus(keep[three, :half], got[three, :half]).astype(BF)
    q3[half:] = plus(keep[three, half:], got[three, half:], behind[...]).astype(BF)


def own_kernel(keep, got, r1, r3, out):
    out[...] = plus(keep[0], got[0], r1[...], r3[...]).astype(BF)


def small(kernel, outs, name, *args):
    moved = sum(a.size for a in args) * 2
    return pl.pallas_call(
        kernel,
        in_specs=[whole()] * len(args),
        out_specs=[whole()] * len(outs),
        out_shape=[struct(s) for s in outs],
        compiler_params=params(14),
        name=name,
        cost_estimate=pl.CostEstimate(
            flops=moved, bytes_accessed=2 * moved, transcendentals=0
        ),
    )(*args)


def send_far(at, keep, got, axis, tag):
    half = (SIDE // 2,) + keep.shape[2:]
    kernel = functools.partial(far_kernel, at)
    ahead, behind = small(kernel, [half, half], "far_" + tag, keep, got)
    return shift(ahead, axis, 1), shift(behind, axis, 3)


def send_near(one, three, keep, got, far, axis, tag):
    kernel = functools.partial(near_kernel, one, three)
    q1, q3 = small(kernel, [keep.shape[1:]] * 2, "near_" + tag, keep, got, *far)
    return shift(q1, axis, 1), shift(q3, axis, 3)


def own_share(keep, got, near, tag):
    return small(own_kernel, [keep.shape[1:]], "own_" + tag, keep, got, *near)[0]


def total_kernel(part_f, part_m, first, mid, out):
    first[0] = jnp.sum(part_f[...].astype(F32), axis=0)
    total = jnp.sum(part_m[...].astype(F32), axis=0)
    rest = jnp.concatenate([total[:8], total[8:]], axis=1)
    mid[...] = rest[:, :HID]
    out[...] = rest[:, HID : HID + C]


def total_grads(part_f, part_m):
    return pl.pallas_call(
        total_kernel,
        in_specs=[whole()] * 2,
        out_specs=[whole()] * 3,
        out_shape=[struct((1, 16, HID), F32), struct((8, HID), F32), struct((8, C), F32)],
        compiler_params=params(12),
        name="total_grads",
    )(part_f, part_m)


def shift(value, axis, by):
    size = lax.axis_size(axis)
    return lax.ppermute(value, axis, [(i, (i + by) % size) for i in range(size)])


def swap(value, axes):
    return lax.all_to_all(value, axes, split_axis=0, concat_axis=0, tiled=True)


def exchange(quarters):
    return [quarters[0]] + [shift(quarters[d], "rep", d) for d in (1, 2, 3)]


def per_device(
    features,
    tile_values,
    tile_columns,
    boundary_rows,
    train_rows,
    shuffle,
    labels,
    first_weight,
    mid_weight,
    out_weight,
):
    y, x, core, rep = (lax.axis_index(a) for a in ("y", "x", "core", "rep"))
    pos = jnp.stack([rep, core, lax.rem(rep + REP - y, REP), y]).astype(jnp.int32)

    part = tile_columns - NB
    halo_at = NB + (part + core) % CORE * (NB // CORE) + part // CORE
    cols = jnp.where(tile_columns < NB, tile_columns, halo_at).reshape(-1)
    inner = lax.rem((y * X + x) * CORE + core, DOM // REP)
    cols = jnp.concatenate([cols, jnp.stack([rep, core, inner])]).astype(jnp.int32)
    brow = boundary_rows

    export, *quarters = export_first(pos, features, brow, labels.reshape(8, TILE))
    hop, pieces, counts = features, [], None
    for h in range(HOPS):
        got = exchange(quarters)
        if h == HOPS - 1:
            counts = count_labels(
                pos, pieces[1], shuffle.reshape(DOM, TILE), train_rows.reshape(DOM, TILE)
            )
        near, got[1], got[3], counts = lax.optimization_barrier(
            (swap(export, ("y", "x")), got[1], got[3], counts)
        )
        far = shift(near, "core", 1)
        pieces.append(got)
        made = propagate(h, cols, tile_values, hop, near, far, brow)
        made, got[2] = lax.optimization_barrier((made, got[2]))
        hop, export, quarters = made[0], made[1], made[-4:]
    early = first_layer_early(
        pos, [pieces[h][d] for d in range(REP) for h in range(HOPS)], first_weight
    )
    pieces.append(exchange(quarters))

    w3 = jnp.pad(out_weight, ((0, 0), (0, CP - C)))
    act1, act2, gl, gm, gf = mlp(
        pos, pieces[3], early, counts, first_weight, mid_weight, w3
    )
    keep_m, send_m = outer_grads(pos, act1, act2, gl, gm)
    got_m = shift(send_m, "core", 1)
    keep2, send2 = first_grads(pos, pieces, gf, (2,))
    got_m, send2, gf = lax.optimization_barrier((got_m, send2, gf))
    got2 = shift(send2, "core", 1)
    far_m = send_far(2, keep_m, got_m, "y", "middle")
    keep13, send13 = first_grads(pos, pieces, gf, (1, 3))
    got13 = shift(send13, "core", 1)
    got2, far_m, gf = lax.optimization_barrier((got2, far_m, gf))
    far_f = send_far(0, keep2, got2, "rep", "first")
    keep0, send0 = first_grads(pos, pieces, gf, (0,))
    got0 = shift(send0, "core", 1)
    near_m = send_near(1, 3, keep_m, got_m, far_m, "y", "middle")
    part_m = swap(own_share(keep_m, got_m, near_m, "middle"), ("x", "rep"))
    near_f = send_near(0, 1, keep13, got13, far_f, "rep", "first")
    part_f = swap(own_share(keep0, got0, near_f, "first"), ("y", "x"))
    first, mid, out = total_grads(part_f, part_m)
    return first, mid, out


def solution(mesh):
    fine = Mesh(mesh.devices.reshape(Y, X, CORE, REP), ("y", "x", "core", "rep"))
    dom = ("y", "x", "core")
    every = dom + ("rep",)
    placed = (
        P(dom, "rep"),
        P(dom, None, None, None),
        P(dom, None),
        P(dom, None),
        P(dom, None),
        P(dom, None),
        P(every),
        P(),
        P(),
        P(),
    )
    return jax.shard_map(
        per_device,
        mesh=fine,
        in_specs=placed,
        out_specs=(P("rep", dom, None), P(every, None), P(every, None)),
        check_vma=False,
    )
```

```python
import functools
import math

import jax
import jax.numpy as jnp
from jax import lax
from jax.experimental import pallas as pl
from jax.experimental.pallas import tpu as pltpu
from jax.sharding import Mesh, PartitionSpec as P

HOPS = 3
TILE = 128
NB = 32
K = 8
R = 4096
HID = 1024
C = 153
CP = 256
Y, X, CORE, REP = 4, 4, 2, 4
DOM = Y * X * CORE
ROWS = R // REP
N_TRAIN = DOM * R
BF = jnp.bfloat16
F32 = jnp.float32
LAB = 16
MIB = 2**20

root_two_pi = 0.7978845608028654
cubic_term = 0.044715


def gelu_pair(v):
    sq = v * v
    t = jnp.tanh(root_two_pi * (v + cubic_term * sq * v))
    half = 0.5 * (1.0 + t)
    slope = half + (0.5 * root_two_pi) * v * (1.0 - t * t) * (
        1.0 + (3.0 * cubic_term) * sq
    )
    return v * half, slope


def dot(a, b, ca, cb):
    return lax.dot_general(a, b, (((ca,), (cb,)), ((), ())), preferred_element_type=F32)


def params(mib):
    return pltpu.CompilerParams(vmem_limit_bytes=mib * MIB)


def whole(memory_space=pltpu.VMEM):
    return pl.BlockSpec(memory_space=memory_space)


def struct(shape, dtype=BF):
    return jax.ShapeDtypeStruct(shape, dtype)


def export_rows(hop, brow):
    here = lax.broadcasted_iota(jnp.int32, (TILE, TILE), 0)
    there = lax.broadcasted_iota(jnp.int32, (TILE, TILE), 1)
    column = jnp.sum(jnp.where(here == there, brow[...], 0), axis=1, keepdims=True)
    row = lax.broadcasted_iota(jnp.int32, (TILE, R), 1)
    return dot((row == column).astype(BF), hop[...], 1, 0).astype(BF)


def take_quarters(rep, hop, quarters):
    for d, q in enumerate(quarters):
        start = pl.multiple_of(lax.rem(rep + d, REP) * ROWS, ROWS)
        q[:ROWS] = hop[pl.ds(start, ROWS), :]


def export_kernel(pos, hop, brow, labels, export, *quarters):
    got = export_rows(hop, brow)
    extra = jnp.concatenate([labels[...].astype(F32), jnp.zeros((8, TILE), F32)])
    extra = extra.astype(BF)
    for t in range(Y * X):
        export[t, :TILE] = got
        export[t, TILE:] = extra
    take_quarters(pos[0], hop, quarters)


def export_first(pos, hop, brow, labels):
    return pl.pallas_call(
        export_kernel,
        in_specs=[whole(pltpu.SMEM)] + [whole()] * 3,
        out_specs=[whole()] * 5,
        out_shape=[struct((Y * X, TILE + LAB, TILE))] + [struct((ROWS, TILE))] * 4,
        compiler_params=params(16),
        name="export_first",
        cost_estimate=pl.CostEstimate(
            flops=2 * TILE * TILE * R, bytes_accessed=2 * MIB, transcendentals=0
        ),
    )(pos, hop, brow, labels)


CUTS = 8
STEP = NB // CUTS


def prop_kernel(h, cols, tiles, hop, near, far, brow, *rest):
    last = h == HOPS - 1
    if last:
        q0, q1, q2, q3, joined, held, sem, out = rest
    else:
        out, export, q0, q1, q2, q3, joined, held, sem = rest
    r, core, inner = cols[NB * K], cols[NB * K + 1], cols[NB * K + 2]

    def copy(c):
        here = pl.ds(c * STEP, STEP)
        return pltpu.make_async_copy(tiles.at[here], held.at[here], sem.at[c])

    for c in range(CUTS):
        copy(c).start()
    joined[:R] = hop[...]
    for t in range(Y * X):
        at = R + t * TILE
        joined[at : at + TILE] = near[t, :TILE]
        joined[at + R // 2 : at + R // 2 + TILE] = far[t, :TILE]

    @pl.loop(0, CUTS)
    def _(c):
        copy(c).wait()
        for b in range(STEP):
            b = c * STEP + b
            parts = []
            for k in range(K):
                at = pl.multiple_of(cols[b * K + k] * TILE, TILE)
                parts.append(joined[pl.ds(at, TILE), :])
            left = jnp.concatenate([held[b, k] for k in range(K)], axis=1)
            got = dot(left, jnp.concatenate(parts, axis=0), 1, 0)
            out[pl.ds(pl.multiple_of(b * TILE, TILE), TILE), :] = got.astype(BF)

    if not last:
        got = export_rows(out, brow)
        for t in range(Y * X):
            export[t] = got
    quarters = (q0, q1, q2, q3)
    take_quarters(r, out, quarters)
    if h == 0:
        pick = lax.broadcasted_iota(jnp.int32, (LAB, TILE), 0) == inner
        labs = []
        for t in range(Y * X):
            two = [
                jnp.sum(jnp.where(pick, v[t, TILE:].astype(F32), 0.0), axis=0, keepdims=True)
                for v in (near, far)
            ]
            labs.append(jnp.where(core == 0, two[0], two[1]))
            labs.append(jnp.where(core == 0, two[1], two[0]))
        labs = jnp.concatenate(labs, axis=0).astype(BF)
        for q in quarters:
            q[ROWS:] = labs


def propagate(h, cols, tiles, hop, near, far, brow):
    last = h == HOPS - 1
    outs = [] if last else [(R, TILE), (Y * X, TILE, TILE)]
    outs += [(ROWS + DOM if h == 0 else ROWS, TILE)] * 4
    scratch = [
        pltpu.VMEM((2 * R, TILE), BF),
        pltpu.VMEM((NB, K, TILE, TILE), BF),
        pltpu.SemaphoreType.DMA((CUTS,)),
    ]
    scratch += [pltpu.VMEM((R, TILE), BF)] if last else []
    return pl.pallas_call(
        functools.partial(prop_kernel, h),
        in_specs=[whole(pltpu.SMEM), whole(pltpu.HBM)] + [whole()] * 4,
        out_specs=[whole()] * len(outs),
        scratch_shapes=scratch,
        out_shape=[struct(s) for s in outs],
        compiler_params=params(54),
        name="propagate_" + str(h),
        cost_estimate=pl.CostEstimate(
            flops=2 * NB * K * TILE**3, bytes_accessed=12 * MIB, transcendentals=0
        ),
    )(cols, tiles, hop, near, far, brow)


def count_kernel(pos, lab0, lab1, lab2, lab3, shuffle, train, out):
    labels = jnp.zeros((DOM, TILE), F32)
    for d, v in enumerate((lab0, lab1, lab2, lab3)):
        labels = jnp.where(pos[2] == d, v[...].astype(F32), labels)
    first = lax.broadcasted_iota(jnp.int32, (DOM, TILE), 0)
    second = lax.broadcasted_iota(jnp.int32, (TILE, TILE), 0)
    slots = jnp.zeros((DOM, TILE), F32)
    for lo in range(0, DOM, 8):
        a, b = [], []
        for e in range(lo, lo + 8):
            slot = shuffle[e : e + 1, :]
            label = labels[e : e + 1, :]
            a.append(jnp.where(first == slot // TILE, label, 0.0).astype(BF))
            b.append((second == lax.rem(slot, TILE)).astype(BF))
        slots += dot(jnp.concatenate(a, axis=1), jnp.concatenate(b, axis=1), 1, 1)
    slots = slots.astype(jnp.int32)
    paper = lax.broadcasted_iota(jnp.int32, (ROWS, TILE), 0) + pos[0] * ROWS
    kind = lax.broadcasted_iota(jnp.int32, (CP, TILE), 0)
    total = jnp.zeros((ROWS, CP), F32)
    for lo in range(0, DOM, 8):
        a, b = [], []
        for e in range(lo, lo + 8):
            a.append((paper == train[e : e + 1, :]).astype(BF))
            b.append((kind == slots[e : e + 1, :]).astype(BF))
        total += dot(jnp.concatenate(a, axis=1), jnp.concatenate(b, axis=1), 1, 1)
    out[...] = total


def count_labels(pos, both, shuffle, train):
    def fixed(shape):
        return pl.BlockSpec(shape, lambda i, c: (0, 0))

    tail = pl.BlockSpec((DOM, TILE), lambda i, c: (ROWS // DOM, 0))
    return pl.pallas_call(
        count_kernel,
        grid_spec=pltpu.PrefetchScalarGridSpec(
            num_scalar_prefetch=1,
            grid=(1,),
            in_specs=[tail] * 4 + [fixed((DOM, TILE))] * 2,
            out_specs=fixed((ROWS, CP)),
        ),
        out_shape=struct((ROWS, CP), F32),
        compiler_params=params(24),
        name="count_labels",
        cost_estimate=pl.CostEstimate(
            flops=2 * ROWS * R * CP, bytes_accessed=2 * MIB, transcendentals=0
        ),
    )(pos, *both, shuffle, train)


MLP_ROWS = 256


def slab_of(rep, d):
    return lax.rem(rep + REP - d, REP)


def early_kernel(pos, *refs):
    pieces, (w1, out) = refs[:12], refs[12:]
    total = jnp.zeros((MLP_ROWS, HID), F32)
    for d in range(REP):
        x = jnp.concatenate([pieces[3 * d + h][...] for h in range(HOPS)], axis=1)
        total += dot(x, w1[slab_of(pos[0], d), : HOPS * TILE], 1, 0)
    out[...] = total


def mlp_kernel(pos, *refs):
    pieces, (early, counts, w1, w2, w3, act1, act2, gl, gm, gf) = refs[:4], refs[4:]
    pre1 = early[...]
    for d in range(REP):
        pre1 += dot(pieces[d][...], w1[slab_of(pos[0], d), HOPS * TILE :], 1, 0)
    a1, slope1 = gelu_pair(pre1)
    a1 = a1.astype(BF)
    act1[...] = a1
    a2, slope2 = gelu_pair(dot(a1, w2[...], 1, 0))
    a2 = a2.astype(BF)
    act2[...] = a2
    logits = dot(a2, w3[...], 1, 0)
    kind = lax.broadcasted_iota(jnp.int32, (MLP_ROWS, CP), 1)
    ex = jnp.where(kind < C, jnp.exp(logits), 0.0)
    probs = ex / jnp.sum(ex, axis=1, keepdims=True)
    drawn = counts[...]
    many = jnp.sum(drawn, axis=1, keepdims=True)
    g3 = ((probs * many - drawn) * (1.0 / math.sqrt(N_TRAIN))).astype(BF)
    gl[...] = g3
    g2 = (dot(g3, w3[...], 1, 1) * slope2).astype(BF)
    gm[...] = g2
    gf[...] = (dot(g2, w2[...], 1, 1) * slope1).astype(BF)


def fixed_block(shape):
    return pl.BlockSpec(shape, lambda i, c: (0,) * len(shape))


def row_block(width):
    return pl.BlockSpec((MLP_ROWS, width), lambda i, c: (i, 0))


def first_layer_early(pos, pieces, w1):
    return pl.pallas_call(
        early_kernel,
        grid_spec=pltpu.PrefetchScalarGridSpec(
            num_scalar_prefetch=1,
            grid=(ROWS // MLP_ROWS,),
            in_specs=[row_block(TILE)] * 12 + [fixed_block(w1.shape)],
            out_specs=row_block(HID),
        ),
        out_shape=struct((ROWS, HID), F32),
        compiler_params=params(20),
        name="first_layer_early",
        cost_estimate=pl.CostEstimate(
            flops=2 * ROWS * HID * 3 * 512, bytes_accessed=11 * MIB, transcendentals=0
        ),
    )(pos, *pieces, w1)


def mlp(pos, pieces, early, counts, w1, w2, w3):
    widths = (HID, HID, CP, HID, HID)
    return pl.pallas_call(
        mlp_kernel,
        grid_spec=pltpu.PrefetchScalarGridSpec(
            num_scalar_prefetch=1,
            grid=(ROWS // MLP_ROWS,),
            in_specs=[row_block(TILE)] * 4
            + [row_block(HID), row_block(CP)]
            + [fixed_block(w.shape) for w in (w1, w2, w3)],
            out_specs=[row_block(w) for w in widths],
        ),
        out_shape=[struct((ROWS, w)) for w in widths],
        compiler_params=params(36),
        name="mlp",
        cost_estimate=pl.CostEstimate(
            flops=2 * ROWS * HID * (2 * HID + 512 + 2 * CP),
            bytes_accessed=20 * MIB,
            transcendentals=2 * ROWS * HID,
        ),
    )(pos, *pieces, early, counts, w1, w2, w3)


WIDE = (HID + CP) // 2
SIDE = 16


def outer_kernel(pos, act1, act2, gl, gm, keep, send):
    own = pos[1] == 0
    width = HID // Y
    for k in range(Y):
        at = pl.multiple_of(lax.rem(pos[3] + k, Y) * width, width)
        mid = dot(act1[:, pl.ds(at, width)], gm[...], 0, 0)
        out = dot(act2[:, pl.ds(at, width)], gl[...], 0, 0)
        both = jnp.concatenate([mid, out], axis=1).reshape(X, CORE, REP, 8, HID + CP)
        both = jnp.concatenate([both[..., :WIDE], both[..., WIDE:]], axis=3)
        zero, one = both[:, 0], both[:, 1]
        shape = (SIDE, 16, WIDE)
        keep[k] = jnp.where(own, zero, one).astype(BF).reshape(shape)
        send[k] = jnp.where(own, one, zero).astype(BF).reshape(shape)


def outer_grads(pos, act1, act2, gl, gm):
    return pl.pallas_call(
        outer_kernel,
        in_specs=[whole(pltpu.SMEM)] + [whole()] * 4,
        out_specs=[whole()] * 2,
        out_shape=[struct((Y, SIDE, 16, WIDE))] * 2,
        compiler_params=params(30),
        name="outer_grads",
        cost_estimate=pl.CostEstimate(
            flops=2 * ROWS * HID * (HID + CP), bytes_accessed=8 * MIB, transcendentals=0
        ),
    )(pos, act1, act2, gl, gm)


def first_kernel(steps, pos, *refs):
    n = (HOPS + 1) * len(steps)
    pieces, (gf, keep, send) = refs[:n], refs[n:]
    own = pos[1] == 0
    for at in range(len(steps)):
        for y in range(0, Y, 2):
            two = [pieces[at * (HOPS + 1) + u][:ROWS] for u in (y, y + 1)]
            x = jnp.concatenate(two, axis=1)
            got = dot(x, gf[...], 0, 0).reshape(2 * X, CORE, 16, HID)
            zero, one = got[:, 0], got[:, 1]
            here = slice(y * X, (y + 2) * X)
            keep[at, here] = jnp.where(own, zero, one).astype(BF)
            send[at, here] = jnp.where(own, one, zero).astype(BF)


def first_grads(pos, pieces, gf, steps):
    used = [pieces[h][(REP - k) % REP] for k in steps for h in range(HOPS + 1)]
    return pl.pallas_call(
        functools.partial(first_kernel, steps),
        in_specs=[whole(pltpu.SMEM)] + [whole()] * (len(used) + 1),
        out_specs=[whole()] * 2,
        out_shape=[struct((len(steps), SIDE, 16, HID))] * 2,
        compiler_params=params(24),
        name="first_grads_" + "".join(str(k) for k in steps),
        cost_estimate=pl.CostEstimate(
            flops=len(steps) * ROWS * HID * HID, bytes_accessed=6 * MIB, transcendentals=0
        ),
    )(pos, *used, gf)


def plus(*values):
    return sum(v.astype(F32) for v in values)


def far_kernel(at, keep, got, ahead, behind):
    half = SIDE // 2
    ahead[...] = plus(keep[at, :half], got[at, :half]).astype(BF)
    behind[...] = plus(keep[at, half:], got[at, half:]).astype(BF)


def near_kernel(one, three, keep, got, ahead, behind, q1, q3):
    half = SIDE // 2
    q1[:half] = plus(keep[one, :half], got[one, :half], ahead[...]).astype(BF)
    q1[half:] = plus(keep[one, half:], got[one, half:]).astype(BF)
    q3[:half] = plus(keep[three, :half], got[three, :half]).astype(BF)
    q3[half:] = plus(keep[three, half:], got[three, half:], behind[...]).astype(BF)


def own_kernel(keep, got, r1, r3, out):
    out[...] = plus(keep[0], got[0], r1[...], r3[...]).astype(BF)


def small(kernel, outs, name, *args):
    moved = sum(a.size for a in args) * 2
    return pl.pallas_call(
        kernel,
        in_specs=[whole()] * len(args),
        out_specs=[whole()] * len(outs),
        out_shape=[struct(s) for s in outs],
        compiler_params=params(14),
        name=name,
        cost_estimate=pl.CostEstimate(
            flops=moved, bytes_accessed=2 * moved, transcendentals=0
        ),
    )(*args)


def send_far(at, keep, got, axis, tag):
    half = (SIDE // 2,) + keep.shape[2:]
    kernel = functools.partial(far_kernel, at)
    ahead, behind = small(kernel, [half, half], "far_" + tag, keep, got)
    return shift(ahead, axis, 1), shift(behind, axis, 3)


def send_near(one, three, keep, got, far, axis, tag):
    kernel = functools.partial(near_kernel, one, three)
    q1, q3 = small(kernel, [keep.shape[1:]] * 2, "near_" + tag, keep, got, *far)
    return shift(q1, axis, 1), shift(q3, axis, 3)


def own_share(keep, got, near, tag):
    return small(own_kernel, [keep.shape[1:]], "own_" + tag, keep, got, *near)[0]


def total_kernel(part_f, part_m, first, mid, out):
    first[0] = jnp.sum(part_f[...].astype(F32), axis=0)
    total = jnp.sum(part_m[...].astype(F32), axis=0)
    rest = jnp.concatenate([total[:8], total[8:]], axis=1)
    mid[...] = rest[:, :HID]
    out[...] = rest[:, HID : HID + C]


def total_grads(part_f, part_m):
    return pl.pallas_call(
        total_kernel,
        in_specs=[whole()] * 2,
        out_specs=[whole()] * 3,
        out_shape=[struct((1, 16, HID), F32), struct((8, HID), F32), struct((8, C), F32)],
        compiler_params=params(12),
        name="total_grads",
    )(part_f, part_m)


def shift(value, axis, by):
    size = lax.axis_size(axis)
    return lax.ppermute(value, axis, [(i, (i + by) % size) for i in range(size)])


def swap(value, axes):
    return lax.all_to_all(value, axes, split_axis=0, concat_axis=0, tiled=True)


def exchange(quarters):
    return [quarters[0]] + [shift(quarters[d], "rep", d) for d in (1, 2, 3)]


def per_device(
    features,
    tile_values,
    tile_columns,
    boundary_rows,
    train_rows,
    shuffle,
    labels,
    first_weight,
    mid_weight,
    out_weight,
):
    y, x, core, rep = (lax.axis_index(a) for a in ("y", "x", "core", "rep"))
    pos = jnp.stack([rep, core, lax.rem(rep + REP - y, REP), y]).astype(jnp.int32)

    part = tile_columns - NB
    halo_at = NB + (part + core) % CORE * (NB // CORE) + part // CORE
    cols = jnp.where(tile_columns < NB, tile_columns, halo_at).reshape(-1)
    inner = lax.rem((y * X + x) * CORE + core, DOM // REP)
    cols = jnp.concatenate([cols, jnp.stack([rep, core, inner])]).astype(jnp.int32)
    brow = boundary_rows

    export, *quarters = export_first(pos, features, brow, labels.reshape(8, TILE))
    hop, pieces, counts = features, [], None
    for h in range(HOPS):
        got = exchange(quarters)
        if h == HOPS - 1:
            counts = count_labels(
                pos, pieces[1], shuffle.reshape(DOM, TILE), train_rows.reshape(DOM, TILE)
            )
        near, got[1], got[3], counts = lax.optimization_barrier(
            (swap(export, ("y", "x")), got[1], got[3], counts)
        )
        far = shift(near, "core", 1)
        pieces.append(got)
        made = propagate(h, cols, tile_values, hop, near, far, brow)
        made, got[2] = lax.optimization_barrier((made, got[2]))
        hop, export, quarters = made[0], made[1], made[-4:]
    early = first_layer_early(
        pos, [pieces[h][d] for d in range(REP) for h in range(HOPS)], first_weight
    )
    pieces.append(exchange(quarters))

    w3 = jnp.pad(out_weight, ((0, 0), (0, CP - C)))
    act1, act2, gl, gm, gf = mlp(
        pos, pieces[3], early, counts, first_weight, mid_weight, w3
    )
    keep_m, send_m = outer_grads(pos, act1, act2, gl, gm)
    got_m = shift(send_m, "core", 1)
    keep2, send2 = first_grads(pos, pieces, gf, (2,))
    got_m, send2, gf = lax.optimization_barrier((got_m, send2, gf))
    got2 = shift(send2, "core", 1)
    far_m = send_far(2, keep_m, got_m, "y", "middle")
    keep13, send13 = first_grads(pos, pieces, gf, (1, 3))
    got13 = shift(send13, "core", 1)
    got2, far_m, gf = lax.optimization_barrier((got2, far_m, gf))
    far_f = send_far(0, keep2, got2, "rep", "first")
    keep0, send0 = first_grads(pos, pieces, gf, (0,))
    got0 = shift(send0, "core", 1)
    near_m = send_near(1, 3, keep_m, got_m, far_m, "y", "middle")
    part_m = swap(own_share(keep_m, got_m, near_m, "middle"), ("x", "rep"))
    near_f = send_near(0, 1, keep13, got13, far_f, "rep", "first")
    part_f = swap(own_share(keep0, got0, near_f, "first"), ("y", "x"))
    first, mid, out = total_grads(part_f, part_m)
    return first, mid, out


def solution(mesh):
    fine = Mesh(mesh.devices.reshape(Y, X, CORE, REP), ("y", "x", "core", "rep"))
    dom = ("y", "x", "core")
    every = dom + ("rep",)
    placed = (
        P(dom, "rep"),
        P(dom, None, None, None),
        P(dom, None),
        P(dom, None),
        P(dom, None),
        P(dom, None),
        P(every),
        P(),
        P(),
        P(),
    )
    return jax.shard_map(
        per_device,
        mesh=fine,
        in_specs=placed,
        out_specs=(P("rep", dom, None), P(every, None), P(every, None)),
        check_vma=False,
    )
```

```python
import functools
import math

import jax
import jax.numpy as jnp
from jax import lax
from jax.experimental import pallas as pl
from jax.experimental.pallas import tpu as pltpu
from jax.sharding import Mesh, PartitionSpec as P

HOPS = 3
TILE = 128
NB = 32
K = 8
R = 4096
HID = 1024
C = 153
CP = 256
Y, X, CORE, REP = 4, 4, 2, 4
DOM = Y * X * CORE
ROWS = R // REP
N_TRAIN = DOM * R
BF = jnp.bfloat16
F32 = jnp.float32
LAB = 16
MIB = 2**20

root_two_pi = 0.7978845608028654
cubic_term = 0.044715


def gelu_pair(v):
    sq = v * v
    t = jnp.tanh(root_two_pi * (v + cubic_term * sq * v))
    half = 0.5 * (1.0 + t)
    slope = half + (0.5 * root_two_pi) * v * (1.0 - t * t) * (
        1.0 + (3.0 * cubic_term) * sq
    )
    return v * half, slope


def dot(a, b, ca, cb):
    return lax.dot_general(a, b, (((ca,), (cb,)), ((), ())), preferred_element_type=F32)


def params(mib):
    return pltpu.CompilerParams(vmem_limit_bytes=mib * MIB)


def whole(memory_space=pltpu.VMEM):
    return pl.BlockSpec(memory_space=memory_space)


def struct(shape, dtype=BF):
    return jax.ShapeDtypeStruct(shape, dtype)


def export_rows(hop, brow):
    here = lax.broadcasted_iota(jnp.int32, (TILE, TILE), 0)
    there = lax.broadcasted_iota(jnp.int32, (TILE, TILE), 1)
    column = jnp.sum(jnp.where(here == there, brow[...], 0), axis=1, keepdims=True)
    row = lax.broadcasted_iota(jnp.int32, (TILE, R), 1)
    return dot((row == column).astype(BF), hop[...], 1, 0).astype(BF)


def take_quarters(rep, hop, quarters):
    for d, q in enumerate(quarters):
        start = pl.multiple_of(lax.rem(rep + d, REP) * ROWS, ROWS)
        q[:ROWS] = hop[pl.ds(start, ROWS), :]


def export_kernel(pos, hop, brow, labels, export, *quarters):
    got = export_rows(hop, brow)
    extra = jnp.concatenate([labels[...].astype(F32), jnp.zeros((8, TILE), F32)])
    extra = extra.astype(BF)
    for t in range(Y * X):
        export[t, :TILE] = got
        export[t, TILE:] = extra
    take_quarters(pos[0], hop, quarters)


def export_first(pos, hop, brow, labels):
    return pl.pallas_call(
        export_kernel,
        in_specs=[whole(pltpu.SMEM)] + [whole()] * 3,
        out_specs=[whole()] * 5,
        out_shape=[struct((Y * X, TILE + LAB, TILE))] + [struct((ROWS, TILE))] * 4,
        compiler_params=params(16),
        name="export_first",
        cost_estimate=pl.CostEstimate(
            flops=2 * TILE * TILE * R, bytes_accessed=2 * MIB, transcendentals=0
        ),
    )(pos, hop, brow, labels)


CUTS = 8
STEP = NB // CUTS


def prop_kernel(h, cols, tiles, hop, near, far, brow, *rest):
    last = h == HOPS - 1
    if last:
        q0, q1, q2, q3, joined, held, sem, out = rest
    else:
        out, export, q0, q1, q2, q3, joined, held, sem = rest
    r, core, inner = cols[NB * K], cols[NB * K + 1], cols[NB * K + 2]

    def copy(c):
        here = pl.ds(c * STEP, STEP)
        return pltpu.make_async_copy(tiles.at[here], held.at[here], sem.at[c])

    for c in range(CUTS):
        copy(c).start()
    joined[:R] = hop[...]
    for t in range(Y * X):
        at = R + t * TILE
        joined[at : at + TILE] = near[t, :TILE]
        joined[at + R // 2 : at + R // 2 + TILE] = far[t, :TILE]

    @pl.loop(0, CUTS)
    def _(c):
        copy(c).wait()
        for b in range(STEP):
            b = c * STEP + b
            parts = []
            for k in range(K):
                at = pl.multiple_of(cols[b * K + k] * TILE, TILE)
                parts.append(joined[pl.ds(at, TILE), :])
            left = jnp.concatenate([held[b, k] for k in range(K)], axis=1)
            got = dot(left, jnp.concatenate(parts, axis=0), 1, 0)
            out[pl.ds(pl.multiple_of(b * TILE, TILE), TILE), :] = got.astype(BF)

    if not last:
        got = export_rows(out, brow)
        for t in range(Y * X):
            export[t] = got
    quarters = (q0, q1, q2, q3)
    take_quarters(r, out, quarters)
    if h == 0:
        pick = lax.broadcasted_iota(jnp.int32, (LAB, TILE), 0) == inner
        labs = []
        for t in range(Y * X):
            two = [
                jnp.sum(jnp.where(pick, v[t, TILE:].astype(F32), 0.0), axis=0, keepdims=True)
                for v in (near, far)
            ]
            labs.append(jnp.where(core == 0, two[0], two[1]))
            labs.append(jnp.where(core == 0, two[1], two[0]))
        labs = jnp.concatenate(labs, axis=0).astype(BF)
        for q in quarters:
            q[ROWS:] = labs


def propagate(h, cols, tiles, hop, near, far, brow):
    last = h == HOPS - 1
    outs = [] if last else [(R, TILE), (Y * X, TILE, TILE)]
    outs += [(ROWS + DOM if h == 0 else ROWS, TILE)] * 4
    scratch = [
        pltpu.VMEM((2 * R, TILE), BF),
        pltpu.VMEM((NB, K, TILE, TILE), BF),
        pltpu.SemaphoreType.DMA((CUTS,)),
    ]
    scratch += [pltpu.VMEM((R, TILE), BF)] if last else []
    return pl.pallas_call(
        functools.partial(prop_kernel, h),
        in_specs=[whole(pltpu.SMEM), whole(pltpu.HBM)] + [whole()] * 4,
        out_specs=[whole()] * len(outs),
        scratch_shapes=scratch,
        out_shape=[struct(s) for s in outs],
        compiler_params=params(54),
        name="propagate_" + str(h),
        cost_estimate=pl.CostEstimate(
            flops=2 * NB * K * TILE**3, bytes_accessed=12 * MIB, transcendentals=0
        ),
    )(cols, tiles, hop, near, far, brow)


def count_kernel(pos, lab0, lab1, lab2, lab3, shuffle, train, out):
    labels = jnp.zeros((DOM, TILE), F32)
    for d, v in enumerate((lab0, lab1, lab2, lab3)):
        labels = jnp.where(pos[2] == d, v[...].astype(F32), labels)
    first = lax.broadcasted_iota(jnp.int32, (DOM, TILE), 0)
    second = lax.broadcasted_iota(jnp.int32, (TILE, TILE), 0)
    slots = jnp.zeros((DOM, TILE), F32)
    for lo in range(0, DOM, 8):
        a, b = [], []
        for e in range(lo, lo + 8):
            slot = shuffle[e : e + 1, :]
            label = labels[e : e + 1, :]
            a.append(jnp.where(first == slot // TILE, label, 0.0).astype(BF))
            b.append((second == lax.rem(slot, TILE)).astype(BF))
        slots += dot(jnp.concatenate(a, axis=1), jnp.concatenate(b, axis=1), 1, 1)
    slots = slots.astype(jnp.int32)
    paper = lax.broadcasted_iota(jnp.int32, (ROWS, TILE), 0) + pos[0] * ROWS
    kind = lax.broadcasted_iota(jnp.int32, (CP, TILE), 0)
    total = jnp.zeros((ROWS, CP), F32)
    for lo in range(0, DOM, 8):
        a, b = [], []
        for e in range(lo, lo + 8):
            a.append((paper == train[e : e + 1, :]).astype(BF))
            b.append((kind == slots[e : e + 1, :]).astype(BF))
        total += dot(jnp.concatenate(a, axis=1), jnp.concatenate(b, axis=1), 1, 1)
    out[...] = total


def count_labels(pos, both, shuffle, train):
    def fixed(shape):
        return pl.BlockSpec(shape, lambda i, c: (0, 0))

    tail = pl.BlockSpec((DOM, TILE), lambda i, c: (ROWS // DOM, 0))
    return pl.pallas_call(
        count_kernel,
        grid_spec=pltpu.PrefetchScalarGridSpec(
            num_scalar_prefetch=1,
            grid=(1,),
            in_specs=[tail] * 4 + [fixed((DOM, TILE))] * 2,
            out_specs=fixed((ROWS, CP)),
        ),
        out_shape=struct((ROWS, CP), F32),
        compiler_params=params(24),
        name="count_labels",
        cost_estimate=pl.CostEstimate(
            flops=2 * ROWS * R * CP, bytes_accessed=2 * MIB, transcendentals=0
        ),
    )(pos, *both, shuffle, train)


MLP_ROWS = 256


def slab_of(rep, d):
    return lax.rem(rep + REP - d, REP)


def early_kernel(pos, *refs):
    pieces, (w1, out) = refs[:12], refs[12:]
    total = jnp.zeros((MLP_ROWS, HID), F32)
    for d in range(REP):
        x = jnp.concatenate([pieces[3 * d + h][...] for h in range(HOPS)], axis=1)
        total += dot(x, w1[slab_of(pos[0], d), : HOPS * TILE], 1, 0)
    out[...] = total


def mlp_kernel(pos, *refs):
    pieces, (early, counts, w1, w2, w3, act1, act2, gl, gm, gf) = refs[:4], refs[4:]
    pre1 = early[...]
    for d in range(REP):
        pre1 += dot(pieces[d][...], w1[slab_of(pos[0], d), HOPS * TILE :], 1, 0)
    a1, slope1 = gelu_pair(pre1)
    a1 = a1.astype(BF)
    act1[...] = a1
    a2, slope2 = gelu_pair(dot(a1, w2[...], 1, 0))
    a2 = a2.astype(BF)
    act2[...] = a2
    logits = dot(a2, w3[...], 1, 0)
    kind = lax.broadcasted_iota(jnp.int32, (MLP_ROWS, CP), 1)
    ex = jnp.where(kind < C, jnp.exp(logits), 0.0)
    probs = ex / jnp.sum(ex, axis=1, keepdims=True)
    drawn = counts[...]
    many = jnp.sum(drawn, axis=1, keepdims=True)
    g3 = ((probs * many - drawn) * (1.0 / math.sqrt(N_TRAIN))).astype(BF)
    gl[...] = g3
    g2 = (dot(g3, w3[...], 1, 1) * slope2).astype(BF)
    gm[...] = g2
    gf[...] = (dot(g2, w2[...], 1, 1) * slope1).astype(BF)


def fixed_block(shape):
    return pl.BlockSpec(shape, lambda i, c: (0,) * len(shape))


def row_block(width):
    return pl.BlockSpec((MLP_ROWS, width), lambda i, c: (i, 0))


def first_layer_early(pos, pieces, w1):
    return pl.pallas_call(
        early_kernel,
        grid_spec=pltpu.PrefetchScalarGridSpec(
            num_scalar_prefetch=1,
            grid=(ROWS // MLP_ROWS,),
            in_specs=[row_block(TILE)] * 12 + [fixed_block(w1.shape)],
            out_specs=row_block(HID),
        ),
        out_shape=struct((ROWS, HID), F32),
        compiler_params=params(20),
        name="first_layer_early",
        cost_estimate=pl.CostEstimate(
            flops=2 * ROWS * HID * 3 * 512, bytes_accessed=11 * MIB, transcendentals=0
        ),
    )(pos, *pieces, w1)


def mlp(pos, pieces, early, counts, w1, w2, w3):
    widths = (HID, HID, CP, HID, HID)
    return pl.pallas_call(
        mlp_kernel,
        grid_spec=pltpu.PrefetchScalarGridSpec(
            num_scalar_prefetch=1,
            grid=(ROWS // MLP_ROWS,),
            in_specs=[row_block(TILE)] * 4
            + [row_block(HID), row_block(CP)]
            + [fixed_block(w.shape) for w in (w1, w2, w3)],
            out_specs=[row_block(w) for w in widths],
        ),
        out_shape=[struct((ROWS, w)) for w in widths],
        compiler_params=params(36),
        name="mlp",
        cost_estimate=pl.CostEstimate(
            flops=2 * ROWS * HID * (2 * HID + 512 + 2 * CP),
            bytes_accessed=20 * MIB,
            transcendentals=2 * ROWS * HID,
        ),
    )(pos, *pieces, early, counts, w1, w2, w3)


WIDE = (HID + CP) // 2
SIDE = 16


def outer_kernel(pos, act1, act2, gl, gm, keep, send):
    own = pos[1] == 0
    width = HID // Y
    for k in range(Y):
        at = pl.multiple_of(lax.rem(pos[3] + k, Y) * width, width)
        mid = dot(act1[:, pl.ds(at, width)], gm[...], 0, 0)
        out = dot(act2[:, pl.ds(at, width)], gl[...], 0, 0)
        both = jnp.concatenate([mid, out], axis=1).reshape(X, CORE, REP, 8, HID + CP)
        both = jnp.concatenate([both[..., :WIDE], both[..., WIDE:]], axis=3)
        zero, one = both[:, 0], both[:, 1]
        shape = (SIDE, 16, WIDE)
        keep[k] = jnp.where(own, zero, one).astype(BF).reshape(shape)
        send[k] = jnp.where(own, one, zero).astype(BF).reshape(shape)


def outer_grads(pos, act1, act2, gl, gm):
    return pl.pallas_call(
        outer_kernel,
        in_specs=[whole(pltpu.SMEM)] + [whole()] * 4,
        out_specs=[whole()] * 2,
        out_shape=[struct((Y, SIDE, 16, WIDE))] * 2,
        compiler_params=params(30),
        name="outer_grads",
        cost_estimate=pl.CostEstimate(
            flops=2 * ROWS * HID * (HID + CP), bytes_accessed=8 * MIB, transcendentals=0
        ),
    )(pos, act1, act2, gl, gm)


def first_kernel(steps, pos, *refs):
    n = (HOPS + 1) * len(steps)
    pieces, (gf, keep, send) = refs[:n], refs[n:]
    own = pos[1] == 0
    for at in range(len(steps)):
        for y in range(0, Y, 2):
            two = [pieces[at * (HOPS + 1) + u][:ROWS] for u in (y, y + 1)]
            x = jnp.concatenate(two, axis=1)
            got = dot(x, gf[...], 0, 0).reshape(2 * X, CORE, 16, HID)
            zero, one = got[:, 0], got[:, 1]
            here = slice(y * X, (y + 2) * X)
            keep[at, here] = jnp.where(own, zero, one).astype(BF)
            send[at, here] = jnp.where(own, one, zero).astype(BF)


def first_grads(pos, pieces, gf, steps):
    used = [pieces[h][(REP - k) % REP] for k in steps for h in range(HOPS + 1)]
    return pl.pallas_call(
        functools.partial(first_kernel, steps),
        in_specs=[whole(pltpu.SMEM)] + [whole()] * (len(used) + 1),
        out_specs=[whole()] * 2,
        out_shape=[struct((len(steps), SIDE, 16, HID))] * 2,
        compiler_params=params(24),
        name="first_grads_" + "".join(str(k) for k in steps),
        cost_estimate=pl.CostEstimate(
            flops=len(steps) * ROWS * HID * HID, bytes_accessed=6 * MIB, transcendentals=0
        ),
    )(pos, *used, gf)


def plus(*values):
    return sum(v.astype(F32) for v in values)


def far_kernel(at, keep, got, ahead, behind):
    half = SIDE // 2
    ahead[...] = plus(keep[at, :half], got[at, :half]).astype(BF)
    behind[...] = plus(keep[at, half:], got[at, half:]).astype(BF)


def near_kernel(one, three, keep, got, ahead, behind, q1, q3):
    half = SIDE // 2
    q1[:half] = plus(keep[one, :half], got[one, :half], ahead[...]).astype(BF)
    q1[half:] = plus(keep[one, half:], got[one, half:]).astype(BF)
    q3[:half] = plus(keep[three, :half], got[three, :half]).astype(BF)
    q3[half:] = plus(keep[three, half:], got[three, half:], behind[...]).astype(BF)


def own_kernel(keep, got, r1, r3, out):
    out[...] = plus(keep[0], got[0], r1[...], r3[...]).astype(BF)


def small(kernel, outs, name, *args):
    moved = sum(a.size for a in args) * 2
    return pl.pallas_call(
        kernel,
        in_specs=[whole()] * len(args),
        out_specs=[whole()] * len(outs),
        out_shape=[struct(s) for s in outs],
        compiler_params=params(14),
        name=name,
        cost_estimate=pl.CostEstimate(
            flops=moved, bytes_accessed=2 * moved, transcendentals=0
        ),
    )(*args)


def send_far(at, keep, got, axis, tag):
    half = (SIDE // 2,) + keep.shape[2:]
    kernel = functools.partial(far_kernel, at)
    ahead, behind = small(kernel, [half, half], "far_" + tag, keep, got)
    return shift(ahead, axis, 1), shift(behind, axis, 3)


def send_near(one, three, keep, got, far, axis, tag):
    kernel = functools.partial(near_kernel, one, three)
    q1, q3 = small(kernel, [keep.shape[1:]] * 2, "near_" + tag, keep, got, *far)
    return shift(q1, axis, 1), shift(q3, axis, 3)


def own_share(keep, got, near, tag):
    return small(own_kernel, [keep.shape[1:]], "own_" + tag, keep, got, *near)[0]


def total_kernel(part_f, part_m, first, mid, out):
    first[0] = jnp.sum(part_f[...].astype(F32), axis=0)
    total = jnp.sum(part_m[...].astype(F32), axis=0)
    rest = jnp.concatenate([total[:8], total[8:]], axis=1)
    mid[...] = rest[:, :HID]
    out[...] = rest[:, HID : HID + C]


def total_grads(part_f, part_m):
    return pl.pallas_call(
        total_kernel,
        in_specs=[whole()] * 2,
        out_specs=[whole()] * 3,
        out_shape=[struct((1, 16, HID), F32), struct((8, HID), F32), struct((8, C), F32)],
        compiler_params=params(12),
        name="total_grads",
    )(part_f, part_m)


def shift(value, axis, by):
    size = lax.axis_size(axis)
    return lax.ppermute(value, axis, [(i, (i + by) % size) for i in range(size)])


def swap(value, axes):
    return lax.all_to_all(value, axes, split_axis=0, concat_axis=0, tiled=True)


def exchange(quarters):
    return [quarters[0]] + [shift(quarters[d], "rep", d) for d in (1, 2, 3)]


def per_device(
    features,
    tile_values,
    tile_columns,
    boundary_rows,
    train_rows,
    shuffle,
    labels,
    first_weight,
    mid_weight,
    out_weight,
):
    y, x, core, rep = (lax.axis_index(a) for a in ("y", "x", "core", "rep"))
    pos = jnp.stack([rep, core, lax.rem(rep + REP - y, REP), y]).astype(jnp.int32)

    part = tile_columns - NB
    halo_at = NB + (part + core) % CORE * (NB // CORE) + part // CORE
    cols = jnp.where(tile_columns < NB, tile_columns, halo_at).reshape(-1)
    inner = lax.rem((y * X + x) * CORE + core, DOM // REP)
    cols = jnp.concatenate([cols, jnp.stack([rep, core, inner])]).astype(jnp.int32)
    brow = boundary_rows

    export, *quarters = export_first(pos, features, brow, labels.reshape(8, TILE))
    hop, pieces, counts = features, [], None
    for h in range(HOPS):
        got = exchange(quarters)
        if h == HOPS - 1:
            counts = count_labels(
                pos, pieces[1], shuffle.reshape(DOM, TILE), train_rows.reshape(DOM, TILE)
            )
        near, got[1], got[3], counts = lax.optimization_barrier(
            (swap(export, ("y", "x")), got[1], got[3], counts)
        )
        far = shift(near, "core", 1)
        pieces.append(got)
        made = propagate(h, cols, tile_values, hop, near, far, brow)
        made, got[2] = lax.optimization_barrier((made, got[2]))
        hop, export, quarters = made[0], made[1], made[-4:]
    early = first_layer_early(
        pos, [pieces[h][d] for d in range(REP) for h in range(HOPS)], first_weight
    )
    pieces.append(exchange(quarters))

    w3 = jnp.pad(out_weight, ((0, 0), (0, CP - C)))
    act1, act2, gl, gm, gf = mlp(
        pos, pieces[3], early, counts, first_weight, mid_weight, w3
    )
    keep_m, send_m = outer_grads(pos, act1, act2, gl, gm)
    got_m = shift(send_m, "core", 1)
    keep2, send2 = first_grads(pos, pieces, gf, (2,))
    got2 = shift(send2, "core", 1)
    keep2, gf = lax.optimization_barrier((keep2, gf))
    keep13, send13 = first_grads(pos, pieces, gf, (1, 3))
    got13 = shift(send13, "core", 1)
    got_m, got2, keep13, gf = lax.optimization_barrier((got_m, got2, keep13, gf))
    far_m = send_far(2, keep_m, got_m, "y", "middle")
    far_f = send_far(0, keep2, got2, "rep", "first")
    keep0, send0 = first_grads(pos, pieces, gf, (0,))
    got0 = shift(send0, "core", 1)
    near_m = send_near(1, 3, keep_m, got_m, far_m, "y", "middle")
    part_m = swap(own_share(keep_m, got_m, near_m, "middle"), ("x", "rep"))
    near_f = send_near(0, 1, keep13, got13, far_f, "rep", "first")
    part_f = swap(own_share(keep0, got0, near_f, "first"), ("y", "x"))
    first, mid, out = total_grads(part_f, part_m)
    return first, mid, out


def solution(mesh):
    fine = Mesh(mesh.devices.reshape(Y, X, CORE, REP), ("y", "x", "core", "rep"))
    dom = ("y", "x", "core")
    every = dom + ("rep",)
    placed = (
        P(dom, "rep"),
        P(dom, None, None, None),
        P(dom, None),
        P(dom, None),
        P(dom, None),
        P(dom, None),
        P(every),
        P(),
        P(),
        P(),
    )
    return jax.shard_map(
        per_device,
        mesh=fine,
        in_specs=placed,
        out_specs=(P("rep", dom, None), P(every, None), P(every, None)),
        check_vma=False,
    )
```

```python
import functools
import math

import jax
import jax.numpy as jnp
from jax import lax
from jax.experimental import pallas as pl
from jax.experimental.pallas import tpu as pltpu
from jax.sharding import Mesh, PartitionSpec as P

HOPS = 3
TILE = 128
NB = 32
K = 8
R = 4096
HID = 1024
C = 153
CP = 256
Y, X, CORE, REP = 4, 4, 2, 4
DOM = Y * X * CORE
ROWS = R // REP
N_TRAIN = DOM * R
BF = jnp.bfloat16
F32 = jnp.float32
LAB = 16
MIB = 2**20

root_two_pi = 0.7978845608028654
cubic_term = 0.044715


def gelu_pair(v):
    sq = v * v
    t = jnp.tanh(root_two_pi * (v + cubic_term * sq * v))
    half = 0.5 * (1.0 + t)
    slope = half + (0.5 * root_two_pi) * v * (1.0 - t * t) * (
        1.0 + (3.0 * cubic_term) * sq
    )
    return v * half, slope


def dot(a, b, ca, cb):
    return lax.dot_general(a, b, (((ca,), (cb,)), ((), ())), preferred_element_type=F32)


def params(mib):
    return pltpu.CompilerParams(vmem_limit_bytes=mib * MIB)


def whole(memory_space=pltpu.VMEM):
    return pl.BlockSpec(memory_space=memory_space)


def struct(shape, dtype=BF):
    return jax.ShapeDtypeStruct(shape, dtype)


def export_rows(hop, brow):
    here = lax.broadcasted_iota(jnp.int32, (TILE, TILE), 0)
    there = lax.broadcasted_iota(jnp.int32, (TILE, TILE), 1)
    column = jnp.sum(jnp.where(here == there, brow[...], 0), axis=1, keepdims=True)
    row = lax.broadcasted_iota(jnp.int32, (TILE, R), 1)
    return dot((row == column).astype(BF), hop[...], 1, 0).astype(BF)


def take_quarters(rep, hop, quarters):
    for d, q in enumerate(quarters):
        start = pl.multiple_of(lax.rem(rep + d, REP) * ROWS, ROWS)
        q[:ROWS] = hop[pl.ds(start, ROWS), :]


def export_kernel(pos, hop, brow, labels, export, *quarters):
    got = export_rows(hop, brow)
    extra = jnp.concatenate([labels[...].astype(F32), jnp.zeros((8, TILE), F32)])
    extra = extra.astype(BF)
    for t in range(Y * X):
        export[t, :TILE] = got
        export[t, TILE:] = extra
    take_quarters(pos[0], hop, quarters)


def export_first(pos, hop, brow, labels):
    return pl.pallas_call(
        export_kernel,
        in_specs=[whole(pltpu.SMEM)] + [whole()] * 3,
        out_specs=[whole()] * 5,
        out_shape=[struct((Y * X, TILE + LAB, TILE))] + [struct((ROWS, TILE))] * 4,
        compiler_params=params(16),
        name="export_first",
        cost_estimate=pl.CostEstimate(
            flops=2 * TILE * TILE * R, bytes_accessed=2 * MIB, transcendentals=0
        ),
    )(pos, hop, brow, labels)


CUTS = 8
STEP = NB // CUTS


def prop_kernel(h, cols, tiles, hop, near, far, brow, *rest):
    last = h == HOPS - 1
    if last:
        q0, q1, q2, q3, joined, held, sem, out = rest
    else:
        out, export, q0, q1, q2, q3, joined, held, sem = rest
    r, core, inner = cols[NB * K], cols[NB * K + 1], cols[NB * K + 2]

    def copy(c):
        here = pl.ds(c * STEP, STEP)
        return pltpu.make_async_copy(tiles.at[here], held.at[here], sem.at[c])

    for c in range(CUTS):
        copy(c).start()
    joined[:R] = hop[...]
    for t in range(Y * X):
        at = R + t * TILE
        joined[at : at + TILE] = near[t, :TILE]
        joined[at + R // 2 : at + R // 2 + TILE] = far[t, :TILE]

    @pl.loop(0, CUTS)
    def _(c):
        copy(c).wait()
        for b in range(STEP):
            b = c * STEP + b
            parts = []
            for k in range(K):
                at = pl.multiple_of(cols[b * K + k] * TILE, TILE)
                parts.append(joined[pl.ds(at, TILE), :])
            left = jnp.concatenate([held[b, k] for k in range(K)], axis=1)
            got = dot(left, jnp.concatenate(parts, axis=0), 1, 0)
            out[pl.ds(pl.multiple_of(b * TILE, TILE), TILE), :] = got.astype(BF)

    if not last:
        got = export_rows(out, brow)
        for t in range(Y * X):
            export[t] = got
    quarters = (q0, q1, q2, q3)
    take_quarters(r, out, quarters)
    if h == 0:
        pick = lax.broadcasted_iota(jnp.int32, (LAB, TILE), 0) == inner
        labs = []
        for t in range(Y * X):
            two = [
                jnp.sum(jnp.where(pick, v[t, TILE:].astype(F32), 0.0), axis=0, keepdims=True)
                for v in (near, far)
            ]
            labs.append(jnp.where(core == 0, two[0], two[1]))
            labs.append(jnp.where(core == 0, two[1], two[0]))
        labs = jnp.concatenate(labs, axis=0).astype(BF)
        for q in quarters:
            q[ROWS:] = labs


def propagate(h, cols, tiles, hop, near, far, brow):
    last = h == HOPS - 1
    outs = [] if last else [(R, TILE), (Y * X, TILE, TILE)]
    outs += [(ROWS + DOM if h == 0 else ROWS, TILE)] * 4
    scratch = [
        pltpu.VMEM((2 * R, TILE), BF),
        pltpu.VMEM((NB, K, TILE, TILE), BF),
        pltpu.SemaphoreType.DMA((CUTS,)),
    ]
    scratch += [pltpu.VMEM((R, TILE), BF)] if last else []
    return pl.pallas_call(
        functools.partial(prop_kernel, h),
        in_specs=[whole(pltpu.SMEM), whole(pltpu.HBM)] + [whole()] * 4,
        out_specs=[whole()] * len(outs),
        scratch_shapes=scratch,
        out_shape=[struct(s) for s in outs],
        compiler_params=params(54),
        name="propagate_" + str(h),
        cost_estimate=pl.CostEstimate(
            flops=2 * NB * K * TILE**3, bytes_accessed=12 * MIB, transcendentals=0
        ),
    )(cols, tiles, hop, near, far, brow)


def count_kernel(pos, lab0, lab1, lab2, lab3, shuffle, train, out):
    labels = jnp.zeros((DOM, TILE), F32)
    for d, v in enumerate((lab0, lab1, lab2, lab3)):
        labels = jnp.where(pos[2] == d, v[...].astype(F32), labels)
    first = lax.broadcasted_iota(jnp.int32, (DOM, TILE), 0)
    second = lax.broadcasted_iota(jnp.int32, (TILE, TILE), 0)
    slots = jnp.zeros((DOM, TILE), F32)
    for lo in range(0, DOM, 8):
        a, b = [], []
        for e in range(lo, lo + 8):
            slot = shuffle[e : e + 1, :]
            label = labels[e : e + 1, :]
            a.append(jnp.where(first == slot // TILE, label, 0.0).astype(BF))
            b.append((second == lax.rem(slot, TILE)).astype(BF))
        slots += dot(jnp.concatenate(a, axis=1), jnp.concatenate(b, axis=1), 1, 1)
    slots = slots.astype(jnp.int32)
    paper = lax.broadcasted_iota(jnp.int32, (ROWS, TILE), 0) + pos[0] * ROWS
    kind = lax.broadcasted_iota(jnp.int32, (CP, TILE), 0)
    total = jnp.zeros((ROWS, CP), F32)
    for lo in range(0, DOM, 8):
        a, b = [], []
        for e in range(lo, lo + 8):
            a.append((paper == train[e : e + 1, :]).astype(BF))
            b.append((kind == slots[e : e + 1, :]).astype(BF))
        total += dot(jnp.concatenate(a, axis=1), jnp.concatenate(b, axis=1), 1, 1)
    out[...] = total


def count_labels(pos, both, shuffle, train):
    def fixed(shape):
        return pl.BlockSpec(shape, lambda i, c: (0, 0))

    tail = pl.BlockSpec((DOM, TILE), lambda i, c: (ROWS // DOM, 0))
    return pl.pallas_call(
        count_kernel,
        grid_spec=pltpu.PrefetchScalarGridSpec(
            num_scalar_prefetch=1,
            grid=(1,),
            in_specs=[tail] * 4 + [fixed((DOM, TILE))] * 2,
            out_specs=fixed((ROWS, CP)),
        ),
        out_shape=struct((ROWS, CP), F32),
        compiler_params=params(24),
        name="count_labels",
        cost_estimate=pl.CostEstimate(
            flops=2 * ROWS * R * CP, bytes_accessed=2 * MIB, transcendentals=0
        ),
    )(pos, *both, shuffle, train)


MLP_ROWS = 256


def slab_of(rep, d):
    return lax.rem(rep + REP - d, REP)


def early_kernel(pos, *refs):
    pieces, (w1, out) = refs[:12], refs[12:]
    total = jnp.zeros((MLP_ROWS, HID), F32)
    for d in range(REP):
        x = jnp.concatenate([pieces[3 * d + h][...] for h in range(HOPS)], axis=1)
        total += dot(x, w1[slab_of(pos[0], d), : HOPS * TILE], 1, 0)
    out[...] = total


def mlp_kernel(pos, *refs):
    pieces, (early, counts, w1, w2, w3, act1, act2, gl, gm, gf) = refs[:4], refs[4:]
    pre1 = early[...]
    for d in range(REP):
        pre1 += dot(pieces[d][...], w1[slab_of(pos[0], d), HOPS * TILE :], 1, 0)
    a1, slope1 = gelu_pair(pre1)
    a1 = a1.astype(BF)
    act1[...] = a1
    a2, slope2 = gelu_pair(dot(a1, w2[...], 1, 0))
    a2 = a2.astype(BF)
    act2[...] = a2
    logits = dot(a2, w3[...], 1, 0)
    kind = lax.broadcasted_iota(jnp.int32, (MLP_ROWS, CP), 1)
    ex = jnp.where(kind < C, jnp.exp(logits), 0.0)
    probs = ex / jnp.sum(ex, axis=1, keepdims=True)
    drawn = counts[...]
    many = jnp.sum(drawn, axis=1, keepdims=True)
    g3 = ((probs * many - drawn) * (1.0 / math.sqrt(N_TRAIN))).astype(BF)
    gl[...] = g3
    g2 = (dot(g3, w3[...], 1, 1) * slope2).astype(BF)
    gm[...] = g2
    gf[...] = (dot(g2, w2[...], 1, 1) * slope1).astype(BF)


def fixed_block(shape):
    return pl.BlockSpec(shape, lambda i, c: (0,) * len(shape))


def row_block(width):
    return pl.BlockSpec((MLP_ROWS, width), lambda i, c: (i, 0))


def first_layer_early(pos, pieces, w1):
    return pl.pallas_call(
        early_kernel,
        grid_spec=pltpu.PrefetchScalarGridSpec(
            num_scalar_prefetch=1,
            grid=(ROWS // MLP_ROWS,),
            in_specs=[row_block(TILE)] * 12 + [fixed_block(w1.shape)],
            out_specs=row_block(HID),
        ),
        out_shape=struct((ROWS, HID), F32),
        compiler_params=params(20),
        name="first_layer_early",
        cost_estimate=pl.CostEstimate(
            flops=2 * ROWS * HID * 3 * 512, bytes_accessed=11 * MIB, transcendentals=0
        ),
    )(pos, *pieces, w1)


def mlp(pos, pieces, early, counts, w1, w2, w3):
    widths = (HID, HID, CP, HID, HID)
    return pl.pallas_call(
        mlp_kernel,
        grid_spec=pltpu.PrefetchScalarGridSpec(
            num_scalar_prefetch=1,
            grid=(ROWS // MLP_ROWS,),
            in_specs=[row_block(TILE)] * 4
            + [row_block(HID), row_block(CP)]
            + [fixed_block(w.shape) for w in (w1, w2, w3)],
            out_specs=[row_block(w) for w in widths],
        ),
        out_shape=[struct((ROWS, w)) for w in widths],
        compiler_params=params(36),
        name="mlp",
        cost_estimate=pl.CostEstimate(
            flops=2 * ROWS * HID * (2 * HID + 512 + 2 * CP),
            bytes_accessed=20 * MIB,
            transcendentals=2 * ROWS * HID,
        ),
    )(pos, *pieces, early, counts, w1, w2, w3)


WIDE = (HID + CP) // 2
SIDE = 16


def outer_kernel(pos, act1, act2, gl, gm, keep, send):
    own = pos[1] == 0
    width = HID // Y
    for y in range(Y):
        cut = slice(y * width, (y + 1) * width)
        mid = dot(act1[:, cut], gm[...], 0, 0)
        out = dot(act2[:, cut], gl[...], 0, 0)
        both = jnp.concatenate([mid, out], axis=1).reshape(X, CORE, REP, 8, HID + CP)
        both = jnp.concatenate([both[..., :WIDE], both[..., WIDE:]], axis=3)
        zero, one = both[:, 0], both[:, 1]
        kept = jnp.where(own, zero, one).astype(BF)
        sent = jnp.where(own, one, zero).astype(BF)
        for z in range(REP):
            k = lax.rem(z + REP - pos[0], REP)
            keep[k, y * X : (y + 1) * X] = kept[:, z]
            send[k, y * X : (y + 1) * X] = sent[:, z]


def outer_grads(pos, act1, act2, gl, gm):
    return pl.pallas_call(
        outer_kernel,
        in_specs=[whole(pltpu.SMEM)] + [whole()] * 4,
        out_specs=[whole()] * 2,
        out_shape=[struct((REP, SIDE, 16, WIDE))] * 2,
        compiler_params=params(30),
        name="outer_grads",
        cost_estimate=pl.CostEstimate(
            flops=2 * ROWS * HID * (HID + CP), bytes_accessed=8 * MIB, transcendentals=0
        ),
    )(pos, act1, act2, gl, gm)


def first_kernel(steps, pos, *refs):
    n = (HOPS + 1) * len(steps)
    pieces, (gf, keep, send) = refs[:n], refs[n:]
    own = pos[1] == 0
    for at in range(len(steps)):
        for y in range(0, Y, 2):
            two = [pieces[at * (HOPS + 1) + u][:ROWS] for u in (y, y + 1)]
            x = jnp.concatenate(two, axis=1)
            got = dot(x, gf[...], 0, 0).reshape(2 * X, CORE, 16, HID)
            zero, one = got[:, 0], got[:, 1]
            here = slice(y * X, (y + 2) * X)
            keep[at, here] = jnp.where(own, zero, one).astype(BF)
            send[at, here] = jnp.where(own, one, zero).astype(BF)


def first_grads(pos, pieces, gf, steps):
    used = [pieces[h][(REP - k) % REP] for k in steps for h in range(HOPS + 1)]
    return pl.pallas_call(
        functools.partial(first_kernel, steps),
        in_specs=[whole(pltpu.SMEM)] + [whole()] * (len(used) + 1),
        out_specs=[whole()] * 2,
        out_shape=[struct((len(steps), SIDE, 16, HID))] * 2,
        compiler_params=params(24),
        name="first_grads_" + "".join(str(k) for k in steps),
        cost_estimate=pl.CostEstimate(
            flops=len(steps) * ROWS * HID * HID, bytes_accessed=6 * MIB, transcendentals=0
        ),
    )(pos, *used, gf)


def plus(*values):
    return sum(v.astype(F32) for v in values)


def far_kernel(at, keep, got, ahead, behind):
    half = SIDE // 2
    ahead[...] = plus(keep[at, :half], got[at, :half]).astype(BF)
    behind[...] = plus(keep[at, half:], got[at, half:]).astype(BF)


def near_kernel(one, three, keep, got, ahead, behind, q1, q3):
    half = SIDE // 2
    q1[:half] = plus(keep[one, :half], got[one, :half], ahead[...]).astype(BF)
    q1[half:] = plus(keep[one, half:], got[one, half:]).astype(BF)
    q3[:half] = plus(keep[three, :half], got[three, :half]).astype(BF)
    q3[half:] = plus(keep[three, half:], got[three, half:], behind[...]).astype(BF)


def own_kernel(kf, gf, rf1, rf3, km, gm, rm1, rm3, out):
    out[:, :, :HID] = plus(kf[0], gf[0], rf1[...], rf3[...]).astype(BF)
    out[:, :, HID:] = plus(km[0], gm[0], rm1[...], rm3[...]).astype(BF)


def small(kernel, outs, name, *args):
    moved = sum(a.size for a in args) * 2
    return pl.pallas_call(
        kernel,
        in_specs=[whole()] * len(args),
        out_specs=[whole()] * len(outs),
        out_shape=[struct(s) for s in outs],
        compiler_params=params(14),
        name=name,
        cost_estimate=pl.CostEstimate(
            flops=moved, bytes_accessed=2 * moved, transcendentals=0
        ),
    )(*args)


def far_parts(at, keep, got, tag):
    half = (SIDE // 2,) + keep.shape[2:]
    kernel = functools.partial(far_kernel, at)
    return small(kernel, [half, half], "far_" + tag, keep, got)


def send_far(parts, axis):
    return shift(parts[0], axis, 1), shift(parts[1], axis, 3)


def send_near(one, three, keep, got, far, axis, tag):
    kernel = functools.partial(near_kernel, one, three)
    q1, q3 = small(kernel, [keep.shape[1:]] * 2, "near_" + tag, keep, got, *far)
    return shift(q1, axis, 1), shift(q3, axis, 3)


def total_kernel(parts, first, mid, out):
    total = jnp.sum(parts[...].astype(F32), axis=0)
    first[0] = total[:, :HID]
    rest = jnp.concatenate([total[:8, HID:], total[8:, HID:]], axis=1)
    mid[...] = rest[:, :HID]
    out[...] = rest[:, HID : HID + C]


def total_grads(parts):
    return pl.pallas_call(
        total_kernel,
        in_specs=[whole()],
        out_specs=[whole()] * 3,
        out_shape=[struct((1, 16, HID), F32), struct((8, HID), F32), struct((8, C), F32)],
        compiler_params=params(12),
        name="total_grads",
    )(parts)


def shift(value, axis, by):
    size = lax.axis_size(axis)
    return lax.ppermute(value, axis, [(i, (i + by) % size) for i in range(size)])


def swap(value, axes):
    return lax.all_to_all(value, axes, split_axis=0, concat_axis=0, tiled=True)


def exchange(quarters):
    return [quarters[0]] + [shift(quarters[d], "rep", d) for d in (1, 2, 3)]


def per_device(
    features,
    tile_values,
    tile_columns,
    boundary_rows,
    train_rows,
    shuffle,
    labels,
    first_weight,
    mid_weight,
    out_weight,
):
    y, x, core, rep = (lax.axis_index(a) for a in ("y", "x", "core", "rep"))
    pos = jnp.stack([rep, core, lax.rem(rep + REP - y, REP), y]).astype(jnp.int32)

    part = tile_columns - NB
    halo_at = NB + (part + core) % CORE * (NB // CORE) + part // CORE
    cols = jnp.where(tile_columns < NB, tile_columns, halo_at).reshape(-1)
    inner = lax.rem((y * X + x) * CORE + core, DOM // REP)
    cols = jnp.concatenate([cols, jnp.stack([rep, core, inner])]).astype(jnp.int32)
    brow = boundary_rows

    export, *quarters = export_first(pos, features, brow, labels.reshape(8, TILE))
    hop, pieces, counts = features, [], None
    for h in range(HOPS):
        got = exchange(quarters)
        if h == HOPS - 1:
            counts = count_labels(
                pos, pieces[1], shuffle.reshape(DOM, TILE), train_rows.reshape(DOM, TILE)
            )
        near, got[1], got[3], counts = lax.optimization_barrier(
            (swap(export, ("y", "x")), got[1], got[3], counts)
        )
        far = shift(near, "core", 1)
        pieces.append(got)
        made = propagate(h, cols, tile_values, hop, near, far, brow)
        made, got[2] = lax.optimization_barrier((made, got[2]))
        hop, export, quarters = made[0], made[1], made[-4:]
    early = first_layer_early(
        pos, [pieces[h][d] for d in range(REP) for h in range(HOPS)], first_weight
    )
    pieces.append(exchange(quarters))

    w3 = jnp.pad(out_weight, ((0, 0), (0, CP - C)))
    act1, act2, gl, gm, gf = mlp(
        pos, pieces[3], early, counts, first_weight, mid_weight, w3
    )
    keep2, send2 = first_grads(pos, pieces, gf, (2,))
    got2 = shift(send2, "core", 1)
    keep2, gm = lax.optimization_barrier((keep2, gm))
    keep_m, send_m = outer_grads(pos, act1, act2, gl, gm)
    got2, keep_m, send_m, gf = lax.optimization_barrier((got2, keep_m, send_m, gf))
    got_m = shift(send_m, "core", 1)
    parts_f = far_parts(0, keep2, got2, "first")
    parts_f, gf = lax.optimization_barrier((parts_f, gf))
    far_f = send_far(parts_f, "rep")
    keep13, send13 = first_grads(pos, pieces, gf, (1, 3))
    got_m, far_f, keep13, send13, gf = lax.optimization_barrier(
        (got_m, far_f, keep13, send13, gf)
    )
    got13 = shift(send13, "core", 1)
    far_m = send_far(far_parts(2, keep_m, got_m, "middle"), "rep")
    keep0, send0 = first_grads(pos, pieces, gf, (0,))
    got0 = shift(send0, "core", 1)
    got13, far_m = lax.optimization_barrier((got13, far_m))
    near_f = send_near(0, 1, keep13, got13, far_f, "rep", "first")
    near_m = send_near(1, 3, keep_m, got_m, far_m, "rep", "middle")
    args = (keep0, got0, *near_f, keep_m, got_m, *near_m)
    parts = small(own_kernel, [(SIDE, 16, HID + WIDE)], "own_share", *args)[0]
    first, mid, out = total_grads(swap(parts, ("y", "x")))
    return first, mid, out


def solution(mesh):
    fine = Mesh(mesh.devices.reshape(Y, X, CORE, REP), ("y", "x", "core", "rep"))
    dom = ("y", "x", "core")
    every = dom + ("rep",)
    placed = (
        P(dom, "rep"),
        P(dom, None, None, None),
        P(dom, None),
        P(dom, None),
        P(dom, None),
        P(dom, None),
        P(every),
        P(),
        P(),
        P(),
    )
    return jax.shard_map(
        per_device,
        mesh=fine,
        in_specs=placed,
        out_specs=(P("rep", dom, None), P(every, None), P(every, None)),
        check_vma=False,
    )
```

```python
import functools
import math

import jax
import jax.numpy as jnp
from jax import lax
from jax.experimental import pallas as pl
from jax.experimental.pallas import tpu as pltpu
from jax.sharding import Mesh, PartitionSpec as P

HOPS = 3
TILE = 128
NB = 32
K = 8
R = 4096
HID = 1024
C = 153
CP = 256
Y, X, CORE, REP = 4, 4, 2, 4
DOM = Y * X * CORE
ROWS = R // REP
N_TRAIN = DOM * R
BF = jnp.bfloat16
F32 = jnp.float32
LAB = 16
MIB = 2**20

root_two_pi = 0.7978845608028654
cubic_term = 0.044715


def gelu_pair(v):
    sq = v * v
    t = jnp.tanh(root_two_pi * (v + cubic_term * sq * v))
    half = 0.5 * (1.0 + t)
    slope = half + (0.5 * root_two_pi) * v * (1.0 - t * t) * (
        1.0 + (3.0 * cubic_term) * sq
    )
    return v * half, slope


def dot(a, b, ca, cb):
    return lax.dot_general(a, b, (((ca,), (cb,)), ((), ())), preferred_element_type=F32)


def params(mib):
    return pltpu.CompilerParams(vmem_limit_bytes=mib * MIB)


def whole(memory_space=pltpu.VMEM):
    return pl.BlockSpec(memory_space=memory_space)


def struct(shape, dtype=BF):
    return jax.ShapeDtypeStruct(shape, dtype)


def export_rows(hop, brow):
    here = lax.broadcasted_iota(jnp.int32, (TILE, TILE), 0)
    there = lax.broadcasted_iota(jnp.int32, (TILE, TILE), 1)
    column = jnp.sum(jnp.where(here == there, brow[...], 0), axis=1, keepdims=True)
    row = lax.broadcasted_iota(jnp.int32, (TILE, R), 1)
    return dot((row == column).astype(BF), hop[...], 1, 0).astype(BF)


def take_quarters(rep, hop, quarters):
    for d, q in enumerate(quarters):
        start = pl.multiple_of(lax.rem(rep + d, REP) * ROWS, ROWS)
        q[:ROWS] = hop[pl.ds(start, ROWS), :]


def export_kernel(pos, hop, brow, labels, export, *quarters):
    got = export_rows(hop, brow)
    extra = jnp.concatenate([labels[...].astype(F32), jnp.zeros((8, TILE), F32)])
    extra = extra.astype(BF)
    for t in range(Y * X):
        export[t, :TILE] = got
        export[t, TILE:] = extra
    take_quarters(pos[0], hop, quarters)


def export_first(pos, hop, brow, labels):
    return pl.pallas_call(
        export_kernel,
        in_specs=[whole(pltpu.SMEM)] + [whole()] * 3,
        out_specs=[whole()] * 5,
        out_shape=[struct((Y * X, TILE + LAB, TILE))] + [struct((ROWS, TILE))] * 4,
        compiler_params=params(16),
        name="export_first",
        cost_estimate=pl.CostEstimate(
            flops=2 * TILE * TILE * R, bytes_accessed=2 * MIB, transcendentals=0
        ),
    )(pos, hop, brow, labels)


CUTS = 8
STEP = NB // CUTS


def prop_kernel(h, cols, tiles, hop, near, far, brow, *rest):
    last = h == HOPS - 1
    if last:
        q0, q1, q2, q3, joined, held, sem, out = rest
    else:
        out, export, q0, q1, q2, q3, joined, held, sem = rest
    r, core, inner = cols[NB * K], cols[NB * K + 1], cols[NB * K + 2]

    def copy(c):
        here = pl.ds(c * STEP, STEP)
        return pltpu.make_async_copy(tiles.at[here], held.at[here], sem.at[c])

    for c in range(CUTS):
        copy(c).start()
    joined[:R] = hop[...]
    for t in range(Y * X):
        at = R + t * TILE
        joined[at : at + TILE] = near[t, :TILE]
        joined[at + R // 2 : at + R // 2 + TILE] = far[t, :TILE]

    @pl.loop(0, CUTS)
    def _(c):
        copy(c).wait()
        for b in range(STEP):
            b = c * STEP + b
            parts = []
            for k in range(K):
                at = pl.multiple_of(cols[b * K + k] * TILE, TILE)
                parts.append(joined[pl.ds(at, TILE), :])
            left = jnp.concatenate([held[b, k] for k in range(K)], axis=1)
            got = dot(left, jnp.concatenate(parts, axis=0), 1, 0)
            out[pl.ds(pl.multiple_of(b * TILE, TILE), TILE), :] = got.astype(BF)

    if not last:
        got = export_rows(out, brow)
        for t in range(Y * X):
            export[t] = got
    quarters = (q0, q1, q2, q3)
    take_quarters(r, out, quarters)
    if h == 0:
        pick = lax.broadcasted_iota(jnp.int32, (LAB, TILE), 0) == inner
        labs = []
        for t in range(Y * X):
            two = [
                jnp.sum(jnp.where(pick, v[t, TILE:].astype(F32), 0.0), axis=0, keepdims=True)
                for v in (near, far)
            ]
            labs.append(jnp.where(core == 0, two[0], two[1]))
            labs.append(jnp.where(core == 0, two[1], two[0]))
        labs = jnp.concatenate(labs, axis=0).astype(BF)
        for q in quarters:
            q[ROWS:] = labs


def propagate(h, cols, tiles, hop, near, far, brow):
    last = h == HOPS - 1
    outs = [] if last else [(R, TILE), (Y * X, TILE, TILE)]
    outs += [(ROWS + DOM if h == 0 else ROWS, TILE)] * 4
    scratch = [
        pltpu.VMEM((2 * R, TILE), BF),
        pltpu.VMEM((NB, K, TILE, TILE), BF),
        pltpu.SemaphoreType.DMA((CUTS,)),
    ]
    scratch += [pltpu.VMEM((R, TILE), BF)] if last else []
    return pl.pallas_call(
        functools.partial(prop_kernel, h),
        in_specs=[whole(pltpu.SMEM), whole(pltpu.HBM)] + [whole()] * 4,
        out_specs=[whole()] * len(outs),
        scratch_shapes=scratch,
        out_shape=[struct(s) for s in outs],
        compiler_params=params(54),
        name="propagate_" + str(h),
        cost_estimate=pl.CostEstimate(
            flops=2 * NB * K * TILE**3, bytes_accessed=12 * MIB, transcendentals=0
        ),
    )(cols, tiles, hop, near, far, brow)


def count_kernel(pos, lab0, lab1, lab2, lab3, shuffle, train, out):
    labels = jnp.zeros((DOM, TILE), F32)
    for d, v in enumerate((lab0, lab1, lab2, lab3)):
        labels = jnp.where(pos[2] == d, v[...].astype(F32), labels)
    first = lax.broadcasted_iota(jnp.int32, (DOM, TILE), 0)
    second = lax.broadcasted_iota(jnp.int32, (TILE, TILE), 0)
    slots = jnp.zeros((DOM, TILE), F32)
    for lo in range(0, DOM, 8):
        a, b = [], []
        for e in range(lo, lo + 8):
            slot = shuffle[e : e + 1, :]
            label = labels[e : e + 1, :]
            a.append(jnp.where(first == slot // TILE, label, 0.0).astype(BF))
            b.append((second == lax.rem(slot, TILE)).astype(BF))
        slots += dot(jnp.concatenate(a, axis=1), jnp.concatenate(b, axis=1), 1, 1)
    slots = slots.astype(jnp.int32)
    paper = lax.broadcasted_iota(jnp.int32, (ROWS, TILE), 0) + pos[0] * ROWS
    kind = lax.broadcasted_iota(jnp.int32, (CP, TILE), 0)
    total = jnp.zeros((ROWS, CP), F32)
    for lo in range(0, DOM, 8):
        a, b = [], []
        for e in range(lo, lo + 8):
            a.append((paper == train[e : e + 1, :]).astype(BF))
            b.append((kind == slots[e : e + 1, :]).astype(BF))
        total += dot(jnp.concatenate(a, axis=1), jnp.concatenate(b, axis=1), 1, 1)
    out[...] = total


def count_labels(pos, both, shuffle, train):
    def fixed(shape):
        return pl.BlockSpec(shape, lambda i, c: (0, 0))

    tail = pl.BlockSpec((DOM, TILE), lambda i, c: (ROWS // DOM, 0))
    return pl.pallas_call(
        count_kernel,
        grid_spec=pltpu.PrefetchScalarGridSpec(
            num_scalar_prefetch=1,
            grid=(1,),
            in_specs=[tail] * 4 + [fixed((DOM, TILE))] * 2,
            out_specs=fixed((ROWS, CP)),
        ),
        out_shape=struct((ROWS, CP), F32),
        compiler_params=params(24),
        name="count_labels",
        cost_estimate=pl.CostEstimate(
            flops=2 * ROWS * R * CP, bytes_accessed=2 * MIB, transcendentals=0
        ),
    )(pos, *both, shuffle, train)


MLP_ROWS = 256


def slab_of(rep, d):
    return lax.rem(rep + REP - d, REP)


def early_kernel(pos, *refs):
    pieces, (w1, out) = refs[:12], refs[12:]
    total = jnp.zeros((MLP_ROWS, HID), F32)
    for d in range(REP):
        x = jnp.concatenate([pieces[3 * d + h][...] for h in range(HOPS)], axis=1)
        total += dot(x, w1[slab_of(pos[0], d), : HOPS * TILE], 1, 0)
    out[...] = total


def mlp_kernel(pos, *refs):
    pieces, (early, counts, w1, w2, w3, act1, act2, gl, gm, gf) = refs[:4], refs[4:]
    pre1 = early[...]
    for d in range(REP):
        pre1 += dot(pieces[d][...], w1[slab_of(pos[0], d), HOPS * TILE :], 1, 0)
    a1, slope1 = gelu_pair(pre1)
    a1 = a1.astype(BF)
    act1[...] = a1
    a2, slope2 = gelu_pair(dot(a1, w2[...], 1, 0))
    a2 = a2.astype(BF)
    act2[...] = a2
    logits = dot(a2, w3[...], 1, 0)
    kind = lax.broadcasted_iota(jnp.int32, (MLP_ROWS, CP), 1)
    ex = jnp.where(kind < C, jnp.exp(logits), 0.0)
    probs = ex / jnp.sum(ex, axis=1, keepdims=True)
    drawn = counts[...]
    many = jnp.sum(drawn, axis=1, keepdims=True)
    g3 = ((probs * many - drawn) * (1.0 / math.sqrt(N_TRAIN))).astype(BF)
    gl[...] = g3
    g2 = (dot(g3, w3[...], 1, 1) * slope2).astype(BF)
    gm[...] = g2
    gf[...] = (dot(g2, w2[...], 1, 1) * slope1).astype(BF)


def fixed_block(shape):
    return pl.BlockSpec(shape, lambda i, c: (0,) * len(shape))


def row_block(width):
    return pl.BlockSpec((MLP_ROWS, width), lambda i, c: (i, 0))


def first_layer_early(pos, pieces, w1):
    return pl.pallas_call(
        early_kernel,
        grid_spec=pltpu.PrefetchScalarGridSpec(
            num_scalar_prefetch=1,
            grid=(ROWS // MLP_ROWS,),
            in_specs=[row_block(TILE)] * 12 + [fixed_block(w1.shape)],
            out_specs=row_block(HID),
        ),
        out_shape=struct((ROWS, HID), F32),
        compiler_params=params(20),
        name="first_layer_early",
        cost_estimate=pl.CostEstimate(
            flops=2 * ROWS * HID * 3 * 512, bytes_accessed=11 * MIB, transcendentals=0
        ),
    )(pos, *pieces, w1)


def mlp(pos, pieces, early, counts, w1, w2, w3):
    widths = (HID, HID, CP, HID, HID)
    return pl.pallas_call(
        mlp_kernel,
        grid_spec=pltpu.PrefetchScalarGridSpec(
            num_scalar_prefetch=1,
            grid=(ROWS // MLP_ROWS,),
            in_specs=[row_block(TILE)] * 4
            + [row_block(HID), row_block(CP)]
            + [fixed_block(w.shape) for w in (w1, w2, w3)],
            out_specs=[row_block(w) for w in widths],
        ),
        out_shape=[struct((ROWS, w)) for w in widths],
        compiler_params=params(36),
        name="mlp",
        cost_estimate=pl.CostEstimate(
            flops=2 * ROWS * HID * (2 * HID + 512 + 2 * CP),
            bytes_accessed=20 * MIB,
            transcendentals=2 * ROWS * HID,
        ),
    )(pos, *pieces, early, counts, w1, w2, w3)


WIDE = (HID + CP) // 2
SIDE = 16


def outer_kernel(pos, act1, act2, gl, gm, keep, send):
    own = pos[1] == 0
    width = HID // Y
    for k in range(Y):
        at = pl.multiple_of(lax.rem(pos[3] + k, Y) * width, width)
        mid = dot(act1[:, pl.ds(at, width)], gm[...], 0, 0)
        out = dot(act2[:, pl.ds(at, width)], gl[...], 0, 0)
        both = jnp.concatenate([mid, out], axis=1).reshape(X, CORE, REP, 8, HID + CP)
        both = jnp.concatenate([both[..., :WIDE], both[..., WIDE:]], axis=3)
        zero, one = both[:, 0], both[:, 1]
        shape = (SIDE, 16, WIDE)
        keep[k] = jnp.where(own, zero, one).astype(BF).reshape(shape)
        send[k] = jnp.where(own, one, zero).astype(BF).reshape(shape)


def outer_grads(pos, act1, act2, gl, gm):
    return pl.pallas_call(
        outer_kernel,
        in_specs=[whole(pltpu.SMEM)] + [whole()] * 4,
        out_specs=[whole()] * 2,
        out_shape=[struct((Y, SIDE, 16, WIDE))] * 2,
        compiler_params=params(30),
        name="outer_grads",
        cost_estimate=pl.CostEstimate(
            flops=2 * ROWS * HID * (HID + CP), bytes_accessed=8 * MIB, transcendentals=0
        ),
    )(pos, act1, act2, gl, gm)


def first_kernel(steps, pos, *refs):
    n = (HOPS + 1) * len(steps)
    pieces, (gf, keep, send) = refs[:n], refs[n:]
    own = pos[1] == 0
    for at in range(len(steps)):
        for y in range(0, Y, 2):
            two = [pieces[at * (HOPS + 1) + u][:ROWS] for u in (y, y + 1)]
            x = jnp.concatenate(two, axis=1)
            got = dot(x, gf[...], 0, 0).reshape(2 * X, CORE, 16, HID)
            zero, one = got[:, 0], got[:, 1]
            here = slice(y * X, (y + 2) * X)
            keep[at, here] = jnp.where(own, zero, one).astype(BF)
            send[at, here] = jnp.where(own, one, zero).astype(BF)


def first_grads(pos, pieces, gf, steps):
    used = [pieces[h][(REP - k) % REP] for k in steps for h in range(HOPS + 1)]
    return pl.pallas_call(
        functools.partial(first_kernel, steps),
        in_specs=[whole(pltpu.SMEM)] + [whole()] * (len(used) + 1),
        out_specs=[whole()] * 2,
        out_shape=[struct((len(steps), SIDE, 16, HID))] * 2,
        compiler_params=params(24),
        name="first_grads_" + "".join(str(k) for k in steps),
        cost_estimate=pl.CostEstimate(
            flops=len(steps) * ROWS * HID * HID, bytes_accessed=6 * MIB, transcendentals=0
        ),
    )(pos, *used, gf)


def plus(*values):
    return sum(v.astype(F32) for v in values)


def far_kernel(at, keep, got, ahead, behind):
    half = SIDE // 2
    ahead[...] = plus(keep[at, :half], got[at, :half]).astype(BF)
    behind[...] = plus(keep[at, half:], got[at, half:]).astype(BF)


def near_kernel(one, three, keep, got, ahead, behind, q1, q3):
    half = SIDE // 2
    q1[:half] = plus(keep[one, :half], got[one, :half], ahead[...]).astype(BF)
    q1[half:] = plus(keep[one, half:], got[one, half:]).astype(BF)
    q3[:half] = plus(keep[three, :half], got[three, :half]).astype(BF)
    q3[half:] = plus(keep[three, half:], got[three, half:], behind[...]).astype(BF)


def own_kernel(keep, got, r1, r3, out):
    out[...] = plus(keep[0], got[0], r1[...], r3[...]).astype(BF)


def small(kernel, outs, name, *args):
    moved = sum(a.size for a in args) * 2
    return pl.pallas_call(
        kernel,
        in_specs=[whole()] * len(args),
        out_specs=[whole()] * len(outs),
        out_shape=[struct(s) for s in outs],
        compiler_params=params(14),
        name=name,
        cost_estimate=pl.CostEstimate(
            flops=moved, bytes_accessed=2 * moved, transcendentals=0
        ),
    )(*args)


def send_far(at, keep, got, axis, tag):
    half = (SIDE // 2,) + keep.shape[2:]
    kernel = functools.partial(far_kernel, at)
    ahead, behind = small(kernel, [half, half], "far_" + tag, keep, got)
    return shift(ahead, axis, 1), shift(behind, axis, 3)


def send_near(one, three, keep, got, far, axis, tag):
    kernel = functools.partial(near_kernel, one, three)
    q1, q3 = small(kernel, [keep.shape[1:]] * 2, "near_" + tag, keep, got, *far)
    return shift(q1, axis, 1), shift(q3, axis, 3)


def own_share(keep, got, near, tag):
    return small(own_kernel, [keep.shape[1:]], "own_" + tag, keep, got, *near)[0]


def total_kernel(part_f, part_m, first, mid, out):
    first[0] = jnp.sum(part_f[...].astype(F32), axis=0)
    total = jnp.sum(part_m[...].astype(F32), axis=0)
    rest = jnp.concatenate([total[:8], total[8:]], axis=1)
    mid[...] = rest[:, :HID]
    out[...] = rest[:, HID : HID + C]


def total_grads(part_f, part_m):
    return pl.pallas_call(
        total_kernel,
        in_specs=[whole()] * 2,
        out_specs=[whole()] * 3,
        out_shape=[struct((1, 16, HID), F32), struct((8, HID), F32), struct((8, C), F32)],
        compiler_params=params(12),
        name="total_grads",
    )(part_f, part_m)


def shift(value, axis, by):
    size = lax.axis_size(axis)
    return lax.ppermute(value, axis, [(i, (i + by) % size) for i in range(size)])


def swap(value, axes):
    return lax.all_to_all(value, axes, split_axis=0, concat_axis=0, tiled=True)


def exchange(quarters):
    return [quarters[0]] + [shift(quarters[d], "rep", d) for d in (1, 2, 3)]


def per_device(
    features,
    tile_values,
    tile_columns,
    boundary_rows,
    train_rows,
    shuffle,
    labels,
    first_weight,
    mid_weight,
    out_weight,
):
    y, x, core, rep = (lax.axis_index(a) for a in ("y", "x", "core", "rep"))
    pos = jnp.stack([rep, core, lax.rem(rep + REP - y, REP), y]).astype(jnp.int32)

    part = tile_columns - NB
    halo_at = NB + (part + core) % CORE * (NB // CORE) + part // CORE
    cols = jnp.where(tile_columns < NB, tile_columns, halo_at).reshape(-1)
    inner = lax.rem((y * X + x) * CORE + core, DOM // REP)
    cols = jnp.concatenate([cols, jnp.stack([rep, core, inner])]).astype(jnp.int32)
    brow = boundary_rows

    export, *quarters = export_first(pos, features, brow, labels.reshape(8, TILE))
    hop, pieces, counts = features, [], None
    for h in range(HOPS):
        got = exchange(quarters)
        if h == HOPS - 1:
            counts = count_labels(
                pos, pieces[1], shuffle.reshape(DOM, TILE), train_rows.reshape(DOM, TILE)
            )
        near, got[1], got[3], counts = lax.optimization_barrier(
            (swap(export, ("y", "x")), got[1], got[3], counts)
        )
        far = shift(near, "core", 1)
        pieces.append(got)
        made = propagate(h, cols, tile_values, hop, near, far, brow)
        made, got[2] = lax.optimization_barrier((made, got[2]))
        hop, export, quarters = made[0], made[1], made[-4:]
    early = first_layer_early(
        pos, [pieces[h][d] for d in range(REP) for h in range(HOPS)], first_weight
    )
    pieces.append(exchange(quarters))

    w3 = jnp.pad(out_weight, ((0, 0), (0, CP - C)))
    act1, act2, gl, gm, gf = mlp(
        pos, pieces[3], early, counts, first_weight, mid_weight, w3
    )
    keep_m, send_m = outer_grads(pos, act1, act2, gl, gm)
    got_m = shift(send_m, "core", 1)
    keep2, send2 = first_grads(pos, pieces, gf, (2,))
    got2 = shift(send2, "core", 1)
    keep2, gf = lax.optimization_barrier((keep2, gf))
    keep13, send13 = first_grads(pos, pieces, gf, (1, 3))
    got_m, got2, keep13, send13, gf = lax.optimization_barrier(
        (got_m, got2, keep13, send13, gf)
    )
    got13 = shift(send13, "core", 1)
    far_m = send_far(2, keep_m, got_m, "y", "middle")
    far_f = send_far(0, keep2, got2, "rep", "first")
    keep0, send0 = first_grads(pos, pieces, gf, (0,))
    got0 = shift(send0, "core", 1)
    near_m = send_near(1, 3, keep_m, got_m, far_m, "y", "middle")
    part_m = swap(own_share(keep_m, got_m, near_m, "middle"), ("x", "rep"))
    near_f = send_near(0, 1, keep13, got13, far_f, "rep", "first")
    part_f = swap(own_share(keep0, got0, near_f, "first"), ("y", "x"))
    first, mid, out = total_grads(part_f, part_m)
    return first, mid, out


def solution(mesh):
    fine = Mesh(mesh.devices.reshape(Y, X, CORE, REP), ("y", "x", "core", "rep"))
    dom = ("y", "x", "core")
    every = dom + ("rep",)
    placed = (
        P(dom, "rep"),
        P(dom, None, None, None),
        P(dom, None),
        P(dom, None),
        P(dom, None),
        P(dom, None),
        P(every),
        P(),
        P(),
        P(),
    )
    return jax.shard_map(
        per_device,
        mesh=fine,
        in_specs=placed,
        out_specs=(P("rep", dom, None), P(every, None), P(every, None)),
        check_vma=False,
    )
```

```python
import functools
import math

import jax
import jax.numpy as jnp
from jax import lax
from jax.experimental import pallas as pl
from jax.experimental.pallas import tpu as pltpu
from jax.sharding import Mesh, PartitionSpec as P

HOPS = 3
TILE = 128
NB = 32
K = 8
R = 4096
HID = 1024
C = 153
CP = 256
Y, X, CORE, REP = 4, 4, 2, 4
DOM = Y * X * CORE
ROWS = R // REP
N_TRAIN = DOM * R
BF = jnp.bfloat16
F32 = jnp.float32
LAB = 16
MIB = 2**20

root_two_pi = 0.7978845608028654
cubic_term = 0.044715


def gelu_pair(v):
    sq = v * v
    t = jnp.tanh(root_two_pi * (v + cubic_term * sq * v))
    half = 0.5 * (1.0 + t)
    slope = half + (0.5 * root_two_pi) * v * (1.0 - t * t) * (
        1.0 + (3.0 * cubic_term) * sq
    )
    return v * half, slope


def dot(a, b, ca, cb):
    return lax.dot_general(a, b, (((ca,), (cb,)), ((), ())), preferred_element_type=F32)


def params(mib):
    return pltpu.CompilerParams(vmem_limit_bytes=mib * MIB)


def whole(memory_space=pltpu.VMEM):
    return pl.BlockSpec(memory_space=memory_space)


def struct(shape, dtype=BF):
    return jax.ShapeDtypeStruct(shape, dtype)


def export_rows(hop, brow):
    here = lax.broadcasted_iota(jnp.int32, (TILE, TILE), 0)
    there = lax.broadcasted_iota(jnp.int32, (TILE, TILE), 1)
    column = jnp.sum(jnp.where(here == there, brow[...], 0), axis=1, keepdims=True)
    row = lax.broadcasted_iota(jnp.int32, (TILE, R), 1)
    return dot((row == column).astype(BF), hop[...], 1, 0).astype(BF)


def take_quarters(rep, hop, quarters):
    for d, q in enumerate(quarters):
        start = pl.multiple_of(lax.rem(rep + d, REP) * ROWS, ROWS)
        q[:ROWS] = hop[pl.ds(start, ROWS), :]


def export_kernel(pos, hop, brow, labels, export, *quarters):
    got = export_rows(hop, brow)
    extra = jnp.concatenate([labels[...].astype(F32), jnp.zeros((8, TILE), F32)])
    extra = extra.astype(BF)
    for t in range(Y * X):
        export[t, :TILE] = got
        export[t, TILE:] = extra
    take_quarters(pos[0], hop, quarters)


def export_first(pos, hop, brow, labels):
    return pl.pallas_call(
        export_kernel,
        in_specs=[whole(pltpu.SMEM)] + [whole()] * 3,
        out_specs=[whole()] * 5,
        out_shape=[struct((Y * X, TILE + LAB, TILE))] + [struct((ROWS, TILE))] * 4,
        compiler_params=params(16),
        name="export_first",
        cost_estimate=pl.CostEstimate(
            flops=2 * TILE * TILE * R, bytes_accessed=2 * MIB, transcendentals=0
        ),
    )(pos, hop, brow, labels)


CUTS = 8
STEP = NB // CUTS


def prop_kernel(h, cols, tiles, hop, near, far, brow, *rest):
    last = h == HOPS - 1
    if last:
        q0, q1, q2, q3, joined, held, sem, out = rest
    else:
        out, export, q0, q1, q2, q3, joined, held, sem = rest
    r, core, inner = cols[NB * K], cols[NB * K + 1], cols[NB * K + 2]

    def copy(c):
        here = pl.ds(c * STEP, STEP)
        return pltpu.make_async_copy(tiles.at[here], held.at[here], sem.at[c])

    for c in range(CUTS):
        copy(c).start()
    joined[:R] = hop[...]
    for t in range(Y * X):
        at = R + t * TILE
        joined[at : at + TILE] = near[t, :TILE]
        joined[at + R // 2 : at + R // 2 + TILE] = far[t, :TILE]

    @pl.loop(0, CUTS)
    def _(c):
        copy(c).wait()
        for b in range(STEP):
            b = c * STEP + b
            parts = []
            for k in range(K):
                at = pl.multiple_of(cols[b * K + k] * TILE, TILE)
                parts.append(joined[pl.ds(at, TILE), :])
            left = jnp.concatenate([held[b, k] for k in range(K)], axis=1)
            got = dot(left, jnp.concatenate(parts, axis=0), 1, 0)
            out[pl.ds(pl.multiple_of(b * TILE, TILE), TILE), :] = got.astype(BF)

    if not last:
        got = export_rows(out, brow)
        for t in range(Y * X):
            export[t] = got
    quarters = (q0, q1, q2, q3)
    take_quarters(r, out, quarters)
    if h == 0:
        pick = lax.broadcasted_iota(jnp.int32, (LAB, TILE), 0) == inner
        labs = []
        for t in range(Y * X):
            two = [
                jnp.sum(jnp.where(pick, v[t, TILE:].astype(F32), 0.0), axis=0, keepdims=True)
                for v in (near, far)
            ]
            labs.append(jnp.where(core == 0, two[0], two[1]))
            labs.append(jnp.where(core == 0, two[1], two[0]))
        labs = jnp.concatenate(labs, axis=0).astype(BF)
        for q in quarters:
            q[ROWS:] = labs


def propagate(h, cols, tiles, hop, near, far, brow):
    last = h == HOPS - 1
    outs = [] if last else [(R, TILE), (Y * X, TILE, TILE)]
    outs += [(ROWS + DOM if h == 0 else ROWS, TILE)] * 4
    scratch = [
        pltpu.VMEM((2 * R, TILE), BF),
        pltpu.VMEM((NB, K, TILE, TILE), BF),
        pltpu.SemaphoreType.DMA((CUTS,)),
    ]
    scratch += [pltpu.VMEM((R, TILE), BF)] if last else []
    return pl.pallas_call(
        functools.partial(prop_kernel, h),
        in_specs=[whole(pltpu.SMEM), whole(pltpu.HBM)] + [whole()] * 4,
        out_specs=[whole()] * len(outs),
        scratch_shapes=scratch,
        out_shape=[struct(s) for s in outs],
        compiler_params=params(54),
        name="propagate_" + str(h),
        cost_estimate=pl.CostEstimate(
            flops=2 * NB * K * TILE**3, bytes_accessed=12 * MIB, transcendentals=0
        ),
    )(cols, tiles, hop, near, far, brow)


def count_kernel(pos, lab0, lab1, lab2, lab3, shuffle, train, out):
    labels = jnp.zeros((DOM, TILE), F32)
    for d, v in enumerate((lab0, lab1, lab2, lab3)):
        labels = jnp.where(pos[2] == d, v[...].astype(F32), labels)
    first = lax.broadcasted_iota(jnp.int32, (DOM, TILE), 0)
    second = lax.broadcasted_iota(jnp.int32, (TILE, TILE), 0)
    slots = jnp.zeros((DOM, TILE), F32)
    for lo in range(0, DOM, 8):
        a, b = [], []
        for e in range(lo, lo + 8):
            slot = shuffle[e : e + 1, :]
            label = labels[e : e + 1, :]
            a.append(jnp.where(first == slot // TILE, label, 0.0).astype(BF))
            b.append((second == lax.rem(slot, TILE)).astype(BF))
        slots += dot(jnp.concatenate(a, axis=1), jnp.concatenate(b, axis=1), 1, 1)
    slots = slots.astype(jnp.int32)
    paper = lax.broadcasted_iota(jnp.int32, (ROWS, TILE), 0) + pos[0] * ROWS
    kind = lax.broadcasted_iota(jnp.int32, (CP, TILE), 0)
    total = jnp.zeros((ROWS, CP), F32)
    for lo in range(0, DOM, 8):
        a, b = [], []
        for e in range(lo, lo + 8):
            a.append((paper == train[e : e + 1, :]).astype(BF))
            b.append((kind == slots[e : e + 1, :]).astype(BF))
        total += dot(jnp.concatenate(a, axis=1), jnp.concatenate(b, axis=1), 1, 1)
    out[...] = total


def count_labels(pos, both, shuffle, train):
    def fixed(shape):
        return pl.BlockSpec(shape, lambda i, c: (0, 0))

    tail = pl.BlockSpec((DOM, TILE), lambda i, c: (ROWS // DOM, 0))
    return pl.pallas_call(
        count_kernel,
        grid_spec=pltpu.PrefetchScalarGridSpec(
            num_scalar_prefetch=1,
            grid=(1,),
            in_specs=[tail] * 4 + [fixed((DOM, TILE))] * 2,
            out_specs=fixed((ROWS, CP)),
        ),
        out_shape=struct((ROWS, CP), F32),
        compiler_params=params(24),
        name="count_labels",
        cost_estimate=pl.CostEstimate(
            flops=2 * ROWS * R * CP, bytes_accessed=2 * MIB, transcendentals=0
        ),
    )(pos, *both, shuffle, train)


MLP_ROWS = 512


def slab_of(rep, d):
    return lax.rem(rep + REP - d, REP)


def early_kernel(pos, *refs):
    pieces, (w1, out) = refs[:12], refs[12:]
    total = jnp.zeros((MLP_ROWS, HID), F32)
    for d in range(REP):
        x = jnp.concatenate([pieces[3 * d + h][...] for h in range(HOPS)], axis=1)
        total += dot(x, w1[slab_of(pos[0], d), : HOPS * TILE], 1, 0)
    out[...] = total


def mlp_kernel(pos, *refs):
    pieces, (early, counts, w1, w2, w3, act1, act2, gl, gm, gf) = refs[:4], refs[4:]
    pre1 = early[...]
    for d in range(REP):
        pre1 += dot(pieces[d][...], w1[slab_of(pos[0], d), HOPS * TILE :], 1, 0)
    a1, slope1 = gelu_pair(pre1)
    a1 = a1.astype(BF)
    act1[...] = a1
    a2, slope2 = gelu_pair(dot(a1, w2[...], 1, 0))
    a2 = a2.astype(BF)
    act2[...] = a2
    logits = dot(a2, w3[...], 1, 0)
    kind = lax.broadcasted_iota(jnp.int32, (MLP_ROWS, CP), 1)
    ex = jnp.where(kind < C, jnp.exp(logits), 0.0)
    probs = ex / jnp.sum(ex, axis=1, keepdims=True)
    drawn = counts[...]
    many = jnp.sum(drawn, axis=1, keepdims=True)
    g3 = ((probs * many - drawn) * (1.0 / math.sqrt(N_TRAIN))).astype(BF)
    gl[...] = g3
    g2 = (dot(g3, w3[...], 1, 1) * slope2).astype(BF)
    gm[...] = g2
    gf[...] = (dot(g2, w2[...], 1, 1) * slope1).astype(BF)


def fixed_block(shape):
    return pl.BlockSpec(shape, lambda i, c: (0,) * len(shape))


def row_block(width):
    return pl.BlockSpec((MLP_ROWS, width), lambda i, c: (i, 0))


def first_layer_early(pos, pieces, w1):
    return pl.pallas_call(
        early_kernel,
        grid_spec=pltpu.PrefetchScalarGridSpec(
            num_scalar_prefetch=1,
            grid=(ROWS // MLP_ROWS,),
            in_specs=[row_block(TILE)] * 12 + [fixed_block(w1.shape)],
            out_specs=row_block(HID),
        ),
        out_shape=struct((ROWS, HID), F32),
        compiler_params=params(20),
        name="first_layer_early",
        cost_estimate=pl.CostEstimate(
            flops=2 * ROWS * HID * 3 * 512, bytes_accessed=11 * MIB, transcendentals=0
        ),
    )(pos, *pieces, w1)


def mlp(pos, pieces, early, counts, w1, w2, w3):
    widths = (HID, HID, CP, HID, HID)
    return pl.pallas_call(
        mlp_kernel,
        grid_spec=pltpu.PrefetchScalarGridSpec(
            num_scalar_prefetch=1,
            grid=(ROWS // MLP_ROWS,),
            in_specs=[row_block(TILE)] * 4
            + [row_block(HID), row_block(CP)]
            + [fixed_block(w.shape) for w in (w1, w2, w3)],
            out_specs=[row_block(w) for w in widths],
        ),
        out_shape=[struct((ROWS, w)) for w in widths],
        compiler_params=params(48),
        name="mlp",
        cost_estimate=pl.CostEstimate(
            flops=2 * ROWS * HID * (2 * HID + 512 + 2 * CP),
            bytes_accessed=20 * MIB,
            transcendentals=2 * ROWS * HID,
        ),
    )(pos, *pieces, early, counts, w1, w2, w3)


WIDE = (HID + CP) // 2
SIDE = 16


def outer_kernel(pos, act1, act2, gl, gm, keep, send):
    own = pos[1] == 0
    width = HID // Y
    for k in range(Y):
        at = pl.multiple_of(lax.rem(pos[3] + k, Y) * width, width)
        mid = dot(act1[:, pl.ds(at, width)], gm[...], 0, 0)
        out = dot(act2[:, pl.ds(at, width)], gl[...], 0, 0)
        both = jnp.concatenate([mid, out], axis=1).reshape(X, CORE, REP, 8, HID + CP)
        both = jnp.concatenate([both[..., :WIDE], both[..., WIDE:]], axis=3)
        zero, one = both[:, 0], both[:, 1]
        shape = (SIDE, 16, WIDE)
        keep[k] = jnp.where(own, zero, one).astype(BF).reshape(shape)
        send[k] = jnp.where(own, one, zero).astype(BF).reshape(shape)


def outer_grads(pos, act1, act2, gl, gm):
    return pl.pallas_call(
        outer_kernel,
        in_specs=[whole(pltpu.SMEM)] + [whole()] * 4,
        out_specs=[whole()] * 2,
        out_shape=[struct((Y, SIDE, 16, WIDE))] * 2,
        compiler_params=params(30),
        name="outer_grads",
        cost_estimate=pl.CostEstimate(
            flops=2 * ROWS * HID * (HID + CP), bytes_accessed=8 * MIB, transcendentals=0
        ),
    )(pos, act1, act2, gl, gm)


def first_kernel(steps, pos, *refs):
    n = (HOPS + 1) * len(steps)
    pieces, (gf, keep, send) = refs[:n], refs[n:]
    own = pos[1] == 0
    for at in range(len(steps)):
        for y in range(0, Y, 2):
            two = [pieces[at * (HOPS + 1) + u][:ROWS] for u in (y, y + 1)]
            x = jnp.concatenate(two, axis=1)
            got = dot(x, gf[...], 0, 0).reshape(2 * X, CORE, 16, HID)
            zero, one = got[:, 0], got[:, 1]
            here = slice(y * X, (y + 2) * X)
            keep[at, here] = jnp.where(own, zero, one).astype(BF)
            send[at, here] = jnp.where(own, one, zero).astype(BF)


def first_grads(pos, pieces, gf, steps):
    used = [pieces[h][(REP - k) % REP] for k in steps for h in range(HOPS + 1)]
    return pl.pallas_call(
        functools.partial(first_kernel, steps),
        in_specs=[whole(pltpu.SMEM)] + [whole()] * (len(used) + 1),
        out_specs=[whole()] * 2,
        out_shape=[struct((len(steps), SIDE, 16, HID))] * 2,
        compiler_params=params(24),
        name="first_grads_" + "".join(str(k) for k in steps),
        cost_estimate=pl.CostEstimate(
            flops=len(steps) * ROWS * HID * HID, bytes_accessed=6 * MIB, transcendentals=0
        ),
    )(pos, *used, gf)


def plus(*values):
    return sum(v.astype(F32) for v in values)


def far_kernel(at, keep, got, ahead, behind):
    half = SIDE // 2
    ahead[...] = plus(keep[at, :half], got[at, :half]).astype(BF)
    behind[...] = plus(keep[at, half:], got[at, half:]).astype(BF)


def near_kernel(one, three, keep, got, ahead, behind, q1, q3):
    half = SIDE // 2
    q1[:half] = plus(keep[one, :half], got[one, :half], ahead[...]).astype(BF)
    q1[half:] = plus(keep[one, half:], got[one, half:]).astype(BF)
    q3[:half] = plus(keep[three, :half], got[three, :half]).astype(BF)
    q3[half:] = plus(keep[three, half:], got[three, half:], behind[...]).astype(BF)


def own_kernel(keep, got, r1, r3, out):
    out[...] = plus(keep[0], got[0], r1[...], r3[...]).astype(BF)


def small(kernel, outs, name, *args):
    moved = sum(a.size for a in args) * 2
    return pl.pallas_call(
        kernel,
        in_specs=[whole()] * len(args),
        out_specs=[whole()] * len(outs),
        out_shape=[struct(s) for s in outs],
        compiler_params=params(14),
        name=name,
        cost_estimate=pl.CostEstimate(
            flops=moved, bytes_accessed=2 * moved, transcendentals=0
        ),
    )(*args)


def send_far(at, keep, got, axis, tag):
    half = (SIDE // 2,) + keep.shape[2:]
    kernel = functools.partial(far_kernel, at)
    ahead, behind = small(kernel, [half, half], "far_" + tag, keep, got)
    return shift(ahead, axis, 1), shift(behind, axis, 3)


def send_near(one, three, keep, got, far, axis, tag):
    kernel = functools.partial(near_kernel, one, three)
    q1, q3 = small(kernel, [keep.shape[1:]] * 2, "near_" + tag, keep, got, *far)
    return shift(q1, axis, 1), shift(q3, axis, 3)


def own_share(keep, got, near, tag):
    return small(own_kernel, [keep.shape[1:]], "own_" + tag, keep, got, *near)[0]


def total_kernel(part_f, part_m, first, mid, out):
    first[0] = jnp.sum(part_f[...].astype(F32), axis=0)
    total = jnp.sum(part_m[...].astype(F32), axis=0)
    rest = jnp.concatenate([total[:8], total[8:]], axis=1)
    mid[...] = rest[:, :HID]
    out[...] = rest[:, HID : HID + C]


def total_grads(part_f, part_m):
    return pl.pallas_call(
        total_kernel,
        in_specs=[whole()] * 2,
        out_specs=[whole()] * 3,
        out_shape=[struct((1, 16, HID), F32), struct((8, HID), F32), struct((8, C), F32)],
        compiler_params=params(12),
        name="total_grads",
    )(part_f, part_m)


def shift(value, axis, by):
    size = lax.axis_size(axis)
    return lax.ppermute(value, axis, [(i, (i + by) % size) for i in range(size)])


def swap(value, axes):
    return lax.all_to_all(value, axes, split_axis=0, concat_axis=0, tiled=True)


def exchange(quarters):
    return [quarters[0]] + [shift(quarters[d], "rep", d) for d in (1, 2, 3)]


def per_device(
    features,
    tile_values,
    tile_columns,
    boundary_rows,
    train_rows,
    shuffle,
    labels,
    first_weight,
    mid_weight,
    out_weight,
):
    y, x, core, rep = (lax.axis_index(a) for a in ("y", "x", "core", "rep"))
    pos = jnp.stack([rep, core, lax.rem(rep + REP - y, REP), y]).astype(jnp.int32)

    part = tile_columns - NB
    halo_at = NB + (part + core) % CORE * (NB // CORE) + part // CORE
    cols = jnp.where(tile_columns < NB, tile_columns, halo_at).reshape(-1)
    inner = lax.rem((y * X + x) * CORE + core, DOM // REP)
    cols = jnp.concatenate([cols, jnp.stack([rep, core, inner])]).astype(jnp.int32)
    brow = boundary_rows

    export, *quarters = export_first(pos, features, brow, labels.reshape(8, TILE))
    hop, pieces, counts = features, [], None
    for h in range(HOPS):
        got = exchange(quarters)
        if h == HOPS - 1:
            counts = count_labels(
                pos, pieces[1], shuffle.reshape(DOM, TILE), train_rows.reshape(DOM, TILE)
            )
        near, got[1], got[3], counts = lax.optimization_barrier(
            (swap(export, ("y", "x")), got[1], got[3], counts)
        )
        far = shift(near, "core", 1)
        pieces.append(got)
        made = propagate(h, cols, tile_values, hop, near, far, brow)
        made, got[2] = lax.optimization_barrier((made, got[2]))
        hop, export, quarters = made[0], made[1], made[-4:]
    early = first_layer_early(
        pos, [pieces[h][d] for d in range(REP) for h in range(HOPS)], first_weight
    )
    pieces.append(exchange(quarters))

    w3 = jnp.pad(out_weight, ((0, 0), (0, CP - C)))
    act1, act2, gl, gm, gf = mlp(
        pos, pieces[3], early, counts, first_weight, mid_weight, w3
    )
    keep_m, send_m = outer_grads(pos, act1, act2, gl, gm)
    got_m = shift(send_m, "core", 1)
    keep2, send2 = first_grads(pos, pieces, gf, (2,))
    got2 = shift(send2, "core", 1)
    keep2, gf = lax.optimization_barrier((keep2, gf))
    keep13, send13 = first_grads(pos, pieces, gf, (1, 3))
    got_m, got2, keep13, send13, gf = lax.optimization_barrier(
        (got_m, got2, keep13, send13, gf)
    )
    got13 = shift(send13, "core", 1)
    far_m = send_far(2, keep_m, got_m, "y", "middle")
    far_f = send_far(0, keep2, got2, "rep", "first")
    keep0, send0 = first_grads(pos, pieces, gf, (0,))
    got0 = shift(send0, "core", 1)
    near_m = send_near(1, 3, keep_m, got_m, far_m, "y", "middle")
    part_m = swap(own_share(keep_m, got_m, near_m, "middle"), ("x", "rep"))
    near_f = send_near(0, 1, keep13, got13, far_f, "rep", "first")
    part_f = swap(own_share(keep0, got0, near_f, "first"), ("y", "x"))
    first, mid, out = total_grads(part_f, part_m)
    return first, mid, out


def solution(mesh):
    fine = Mesh(mesh.devices.reshape(Y, X, CORE, REP), ("y", "x", "core", "rep"))
    dom = ("y", "x", "core")
    every = dom + ("rep",)
    placed = (
        P(dom, "rep"),
        P(dom, None, None, None),
        P(dom, None),
        P(dom, None),
        P(dom, None),
        P(dom, None),
        P(every),
        P(),
        P(),
        P(),
    )
    return jax.shard_map(
        per_device,
        mesh=fine,
        in_specs=placed,
        out_specs=(P("rep", dom, None), P(every, None), P(every, None)),
        check_vma=False,
    )
```
